32 devices in a mesh: dp: 8 (over y, x, core), expert: 4 (over z).
Axes of the slice: x: 2, y: 2, z: 4, core: 2. Of those that a mesh axis runs over, the one named last changes fastest.
Arguments:
- tokens: bfloat16 [4096, 1536], P(('dp', 'expert')), may hold values from -6 to 6
- segment_ids: int32 [32, 128], P(('dp', 'expert')), may hold values from 0 to 3, never falling along the last dimension, each value on 1 to 64 neighbouring positions
- routes: int32 [4096, 8], P(('dp', 'expert')), may hold values from 0 to 19, as said below
- cotangent: bfloat16 [4096, 1536], P(('dp', 'expert')), may hold values from -6 to 6
- query_weight: bfloat16 [1536, 1536], P('dp'), may hold values from -0.15625 to 0.15625
- key_weight: bfloat16 [1536, 512], P('dp'), may hold values from -0.15625 to 0.15625
- value_matrix: bfloat16 [1536, 512], P('dp'), may hold values from -0.15625 to 0.15625
- out_weight: bfloat16 [1536, 1536], P('dp'), may hold values from -1.25 to 1.25
- first_gain: bfloat16 [1536], P('dp'), may hold values from 0.5 to 1.5
- second_gain: bfloat16 [1536], P('dp'), may hold values from 0.5 to 1.5
- router_weight: bfloat16 [1536, 20], P('dp'), may hold values from -0.078125 to 0.078125
- gate_weight: bfloat16 [20, 1536, 512], P('expert'), may hold values from -0.15625 to 0.15625
- up_weight: bfloat16 [20, 1536, 512], P('expert'), may hold values from -0.15625 to 0.15625
- down_weight: bfloat16 [20, 512, 1536], P('expert'), may hold values from -0.5 to 0.5
Outputs:
- layer_out: bfloat16 [4096, 1536], P(('dp', 'expert'))
- input_grad: float32 [4096, 1536], P(('dp', 'expert'))
- query_grad: float32 [1536, 1536], P('dp')
- key_grad: float32 [1536, 512], P('dp')
- value_grad: float32 [1536, 512], P('dp')
- out_grad: float32 [1536, 1536], P('dp')
- first_grad: float32 [1536], P('dp')
- second_grad: float32 [1536], P('dp')
- router_grad: float32 [1536, 20], P('dp')
- gate_grad: float32 [20, 1536, 512], P('expert', 'dp')
- up_grad: float32 [20, 1536, 512], P('expert', 'dp')
- down_grad: float32 [20, 512, 1536], P('expert', 'dp')
The draws below stay inside these ranges and needn't reach their ends.
Inputs may be any that keep to these rules, and one draw needn't show every extreme that they name: `segment_ids`: within each row the segment ids start at 0, never fall and take 4 values; a sequence has at most 64 tokens and some sequence has exactly that many. `routes`: each token names 8 different experts. Among the 128 tokens of one device no expert is named more than 96 times; in every such block between four and eight experts are named exactly 96 times.
All inputs are finite; a program needn't handle non-finite values.
Results may differ from the reference program's by a relative error of at most 0.012.
Values may be sent and summed in bfloat16 or wider, within the bound.
No kernel may reach another device: no remote copies, remote signals or barrier semaphores. Data moves between devices by JAX's collectives and lax.ppermute only.
A program may use at most 256 MiB of HBM per device.

```python
import math
import jax
import jax.numpy as jnp
import numpy as np
from jax import lax

MODEL_WIDTH = 1536
QUERY_HEADS = 24
KEY_VALUE_HEADS = 8
HEAD_SIZE = 64
HID = 512
TOPK = 8
NSEG = 4
TOK_DEV = 128
EXPERTS = 20
CAP = 96
SEGMAX = 64
SHARDS = 32
TOKENS = 4096
N_DP = 8
N_EXPERT = 4


def draw_routes(key, part):
    blocks = TOKENS // TOK_DEV
    ids = jnp.arange(EXPERTS, dtype=jnp.int32)
    anchor = jax.random.randint(jax.random.fold_in(key, 11), (), 0, EXPERTS, dtype=jnp.int32)
    priority = jax.random.randint(jax.random.fold_in(key, 12), (blocks, EXPERTS), 0, 65536, dtype=jnp.int32) * EXPERTS + ids[None, :]
    priority = jnp.where(ids[None, :] == anchor, -1, priority)
    rank = jnp.sum((priority[:, None, :] < priority[:, :, None]).astype(jnp.int32), axis=-1)
    hot_count = jax.random.randint(jax.random.fold_in(key, 13), (blocks, 1), 4, 9, dtype=jnp.int32)
    is_hot = rank < hot_count
    cold_count = EXPERTS - hot_count
    token_keys = jax.random.randint(jax.random.fold_in(key, 14), (blocks, TOK_DEV), 0, 65536, dtype=jnp.int32) * TOK_DEV + jnp.arange(TOK_DEV, dtype=jnp.int32)[None, :]
    shuffled = jnp.argsort(token_keys, axis=1).astype(jnp.int32)
    named_hot = is_hot[:, None, :] & ((shuffled[:, :, None] + rank[:, None, :]) % 4 != 0)
    needed = TOPK - jnp.sum(named_hot.astype(jnp.int32), axis=-1)
    stride = needed + jax.random.randint(jax.random.fold_in(key, 15), (blocks, TOK_DEV), 0, 3, dtype=jnp.int32)
    begin = jnp.cumsum(stride, axis=1) - stride
    cold_index = rank - hot_count
    offset = (cold_index[:, None, :] - begin[:, :, None]) % cold_count[:, :, None]
    named_cold = jnp.logical_not(is_hot)[:, None, :] & (offset < needed[:, :, None])
    named = named_hot | named_cold
    score = jnp.where(named, 16777216 + ids[None, None, :], -1 - ids[None, None, :])
    _, picked = lax.top_k(score, TOPK)
    order_keys = jax.random.randint(jax.random.fold_in(key, 16), (blocks, TOK_DEV, TOPK), 0, 65536, dtype=jnp.int32) * TOPK + jnp.arange(TOPK, dtype=jnp.int32)[None, None, :]
    order = jnp.argsort(order_keys, axis=-1)
    picked = jnp.take_along_axis(picked, order, axis=-1)
    return picked.reshape(TOKENS, TOPK).astype(jnp.int32)


def block_scale(own_key, dims, cuts, smallest, high):
    level, own = 1.0, jax.random.fold_in(own_key, 6)
    for axis_at, blocks in cuts:
        draws = jnp.exp(jax.random.uniform(jax.random.fold_in(own, axis_at), (blocks,), jnp.float32, smallest / len(cuts), high / len(cuts)))
        level = level * jnp.repeat(draws, dims[axis_at] // blocks).reshape([-1 if axis == axis_at else 1 for axis in range(len(dims))])
    return level


def length_profile(count, total, limit, slope):
    loads = [(1 << 20) // math.isqrt(standing ** slope) + 1 for standing in range(2, count + 1)]
    surplus, given = total - limit - (count - 1), [1] * (count - 1)
    while surplus > 0:
        movable = [i for i in range(count - 1) if given[i] < limit]
        pool, remaining = sum([loads[i] for i in movable]), surplus
        for i in movable:
            extra = min(limit - given[i], max(1, remaining * loads[i] // pool), surplus)
            given[i] = given[i] + extra
            surplus = surplus - extra
    return np.array([limit] + given)


def uneven(rng, count, total, limit, slope):
    if count == 2:
        one = jax.random.randint(rng, (), max(1, total - limit), min(limit, total - 1) + 1)
        return jnp.stack([one, total - one])
    sizes = jnp.asarray(length_profile(count, total, limit, slope), jnp.int32)
    pairs = (count - 1) // 2
    source_of, sink = sizes[1:1 + 2 * pairs:2], sizes[2:2 + 2 * pairs:2]
    room = jnp.minimum(source_of - 1, limit - sink)
    passed = jax.random.randint(jax.random.fold_in(rng, 1), (pairs,), 0, 1 << 20) % (room + 1)
    sizes = sizes.at[1:1 + 2 * pairs:2].set(source_of - passed).at[2:2 + 2 * pairs:2].set(sink + passed)
    return sizes[jax.random.permutation(jax.random.fold_in(rng, 2), count)]


def normal_values(rng, extent, scale, reach, shards=(), kind=jnp.bfloat16):
    entries = scale * jax.random.normal(rng, extent, jnp.float32)
    if shards:
        entries = entries * block_scale(rng, extent, shards, -0.22, 0.18)
    return jnp.clip(entries, -reach, reach).astype(kind)


def setup_inputs(seed: int = 0) -> dict:
    keys = jax.random.split(jax.random.key(seed), 15)
    tokens = normal_values(keys[0], (TOKENS, MODEL_WIDTH), 1.0, 6.0, ((0, 32),))
    segment_ids = jax.vmap(lambda own: jnp.searchsorted(jnp.cumsum(uneven(own, NSEG, TOK_DEV, SEGMAX, 2)), jnp.arange(TOK_DEV), side="right"))(jax.random.split(keys[1], SHARDS)).reshape((SHARDS, TOK_DEV)).astype(jnp.int32)
    routes = draw_routes(jax.random.fold_in(keys[14], 71), 0)
    cotangent = normal_values(keys[3], (TOKENS, MODEL_WIDTH), 1.0, 6.0, ((0, 32),))
    query_weight = normal_values(keys[4], (MODEL_WIDTH, QUERY_HEADS * HEAD_SIZE), MODEL_WIDTH ** -0.5, 0.15625, ((0, 8),))
    key_weight = normal_values(keys[5], (MODEL_WIDTH, KEY_VALUE_HEADS * HEAD_SIZE), MODEL_WIDTH ** -0.5, 0.15625, ((0, 8),))
    value_matrix = normal_values(keys[6], (MODEL_WIDTH, KEY_VALUE_HEADS * HEAD_SIZE), MODEL_WIDTH ** -0.5, 0.15625, ((0, 8),))
    out_weight = normal_values(keys[7], (QUERY_HEADS * HEAD_SIZE, MODEL_WIDTH), (QUERY_HEADS * HEAD_SIZE // 64) ** -0.5, 1.25, ((0, 8),))
    first_gain = jnp.clip(1.0 + 0.1 * jax.random.normal(keys[8], (MODEL_WIDTH,), jnp.float32), 0.5, 1.5).astype(jnp.bfloat16)
    second_gain = jnp.clip(1.0 + 0.1 * jax.random.normal(keys[9], (MODEL_WIDTH,), jnp.float32), 0.5, 1.5).astype(jnp.bfloat16)
    router_weight = normal_values(keys[10], (MODEL_WIDTH, EXPERTS), (4 * MODEL_WIDTH) ** -0.5, 0.078125, ((0, 8),))
    gate_weight = normal_values(keys[11], (EXPERTS, MODEL_WIDTH, HID), MODEL_WIDTH ** -0.5, 0.15625, ((0, 4),))
    up_weight = normal_values(keys[12], (EXPERTS, MODEL_WIDTH, HID), MODEL_WIDTH ** -0.5, 0.15625, ((0, 4),))
    down_weight = normal_values(keys[13], (EXPERTS, HID, MODEL_WIDTH), (HID // 4) ** -0.5, 0.5, ((0, 4),))
    return dict(tokens=tokens, segment_ids=segment_ids, routes=routes, cotangent=cotangent, query_weight=query_weight, key_weight=key_weight, value_matrix=value_matrix, out_weight=out_weight, first_gain=first_gain, second_gain=second_gain, router_weight=router_weight, gate_weight=gate_weight, up_weight=up_weight, down_weight=down_weight)


EPSILON = 1e-06
ROTARY_BASE = 10000.0
SCORE_FACTOR = 0.015625
HIGHEST = lax.Precision.HIGHEST

def rope_tables(positions, width):
    half = width // 2
    freq = ROTARY_BASE ** (-jnp.arange(half, dtype=jnp.float32) * 2.0 / width)
    angle = positions.astype(jnp.float32)[:, None] * freq[None, :]
    return (jnp.cos(angle)[:, None, :], jnp.sin(angle)[:, None, :])

def rotate(field, cosine, sine):
    half = field.shape[-1] // 2
    first, second = (field[..., :half], field[..., half:])
    return jnp.concatenate([first * cosine - second * sine, second * cosine + first * sine], axis=-1)

def rotate_back(grad, cosine, sine):
    half = grad.shape[-1] // 2
    first, second = (grad[..., :half], grad[..., half:])
    return jnp.concatenate([first * cosine + second * sine, second * cosine - first * sine], axis=-1)

def positions_of(segments):
    count = segments.shape[0]
    earlier = lax.optimization_barrier(jnp.sum((segments[None, :] < segments[:, None]).astype(jnp.int32), axis=1))
    return jnp.arange(count, dtype=jnp.int32) - earlier

def attention_mask(segments):
    count = segments.shape[0]
    index = jnp.arange(count, dtype=jnp.int32)
    return (segments[:, None] == segments[None, :]) & (index[None, :] <= index[:, None])

def rms_forward(field, gain):
    inverse = lax.rsqrt(lax.optimization_barrier(jnp.mean(field * field, axis=-1, keepdims=True)) + EPSILON)
    return (inverse, field * inverse * gain.astype(jnp.float32))

def rms_backward(field, inverse, gain, grad):
    scaled = grad * gain.astype(jnp.float32)
    inner = lax.optimization_barrier(jnp.mean(scaled * field, axis=-1, keepdims=True))
    return (inverse * scaled - field * inverse ** 3 * inner, lax.optimization_barrier(jnp.sum(grad * field * inverse, axis=0)))

def score_block(query_rows, key_rows, mask):
    score_matrix = jnp.einsum('qean,wen->eaqw', query_rows.astype(jnp.float32), key_rows.astype(jnp.float32)) * SCORE_FACTOR
    return jnp.where(mask[None, None], score_matrix, -1e+30)

def layer(inputs_bf, segments, picks, grad_bf, weights):
    query_weight, key_weight, value_matrix, out_weight, first_gain, second_gain, router_weight, gate_weight, up_weight, down_weight = weights
    token_rows, width = inputs_bf.shape
    query_head_rows = query_weight.shape[1] // HEAD_SIZE
    key_heads = key_weight.shape[1] // HEAD_SIZE
    head_group = query_head_rows // key_heads
    experts = router_weight.shape[1]
    choices_per = picks.shape[1]
    mask = attention_mask(segments)
    cosine, sine = rope_tables(positions_of(segments), HEAD_SIZE)
    inputs = inputs_bf.astype(jnp.float32)
    first_inverse, normed1 = rms_forward(inputs, first_gain)
    normed1 = normed1.astype(jnp.bfloat16)
    query_rows = rotate(jnp.dot(normed1, query_weight, preferred_element_type=jnp.float32).reshape(token_rows, query_head_rows, HEAD_SIZE), cosine, sine)
    query_rows = query_rows.astype(jnp.bfloat16).reshape(token_rows, key_heads, head_group, HEAD_SIZE)
    key_rows = rotate(jnp.dot(normed1, key_weight, preferred_element_type=jnp.float32).reshape(token_rows, key_heads, HEAD_SIZE), cosine, sine).astype(jnp.bfloat16)
    value_rows = jnp.dot(normed1, value_matrix, preferred_element_type=jnp.float32).astype(jnp.bfloat16).reshape(token_rows, key_heads, HEAD_SIZE)
    score_matrix = score_block(query_rows, key_rows, mask)
    peak = lax.optimization_barrier(jnp.max(score_matrix, axis=-1, keepdims=True))
    logsum = peak + jnp.log(lax.optimization_barrier(jnp.sum(jnp.exp(score_matrix - peak), axis=-1, keepdims=True)))
    probabilities = jnp.exp(score_matrix - logsum).astype(jnp.bfloat16)
    mixed_values = jnp.einsum('wmik,kwy->iwmy', probabilities.astype(jnp.float32), value_rows.astype(jnp.float32))
    mixed_values = mixed_values.astype(jnp.bfloat16).reshape(token_rows, query_head_rows * HEAD_SIZE)
    resid = inputs + jnp.dot(mixed_values, out_weight, preferred_element_type=jnp.float32)
    second_inverse, normed2 = rms_forward(resid, second_gain)
    normed2 = normed2.astype(jnp.bfloat16)
    logits = jnp.dot(normed2, router_weight, preferred_element_type=jnp.float32)
    chosen = jnp.take_along_axis(logits, picks, axis=1)
    top = lax.optimization_barrier(jnp.max(chosen, axis=-1, keepdims=True))
    raised = jnp.exp(chosen - top)
    gates = raised / lax.optimization_barrier(jnp.sum(raised, axis=-1, keepdims=True))
    flat = picks.reshape(-1)
    hits = (flat[:, None] == jnp.arange(experts, dtype=jnp.int32)[None, :]).astype(jnp.int32)
    slots = lax.optimization_barrier(jnp.sum((jnp.cumsum(hits, axis=0) - hits) * hits, axis=1)).astype(jnp.int32)
    empty = jnp.zeros((experts, CAP, width), jnp.bfloat16)
    outgoing = empty.at[flat, slots].set(jnp.repeat(normed2, choices_per, axis=0))
    gate_pre = jnp.einsum('ecd,edh->ech', outgoing.astype(jnp.float32), gate_weight.astype(jnp.float32))
    up_pre = jnp.einsum('ecd,edh->ech', outgoing.astype(jnp.float32), up_weight.astype(jnp.float32))
    hidden = (jax.nn.silu(gate_pre) * up_pre).astype(jnp.bfloat16)
    produced = jnp.einsum('ech,ehd->ecd', hidden.astype(jnp.float32), down_weight.astype(jnp.float32)).astype(jnp.bfloat16)
    picked_bf = produced[flat, slots].reshape(token_rows, choices_per, width)
    picked = picked_bf.astype(jnp.float32)
    combined = jnp.einsum('tk,tkd->td', gates, picked, precision=HIGHEST)
    layer_out = (resid + combined).astype(jnp.bfloat16)
    grad_out = grad_bf.astype(jnp.float32)
    gate_back = jnp.einsum('td,tkd->tk', grad_bf, picked_bf, preferred_element_type=jnp.float32)
    chosen_back = gates * (gate_back - lax.optimization_barrier(jnp.sum(gates * gate_back, axis=-1, keepdims=True)))
    choose = (picks[:, :, None] == jnp.arange(experts, dtype=jnp.int32)[None, None, :]).astype(jnp.float32)
    logit_back = lax.optimization_barrier(jnp.sum(choose * chosen_back[:, :, None], axis=1))
    router_grad = jnp.dot(normed2.astype(jnp.float32).T, logit_back, precision=HIGHEST)
    normed2_back = jnp.dot(logit_back, router_weight.astype(jnp.float32).T, precision=HIGHEST)
    row_grads = (gates[:, :, None] * grad_out[:, None, :]).astype(jnp.bfloat16).reshape(token_rows * choices_per, width)
    leaving = empty.at[flat, slots].set(row_grads)
    hidden_back = jnp.einsum('ecd,ehd->ech', leaving.astype(jnp.float32), down_weight.astype(jnp.float32))
    sigma = jax.nn.sigmoid(gate_pre)
    gate_rows = (hidden_back * up_pre * sigma * (1.0 + gate_pre * (1.0 - sigma))).astype(jnp.bfloat16)
    up_rows = (hidden_back * gate_pre * sigma).astype(jnp.bfloat16)
    down_grad = jnp.einsum('ech,ecd->ehd', hidden.astype(jnp.float32), leaving.astype(jnp.float32))
    gate_grad = jnp.einsum('ecd,ech->edh', outgoing.astype(jnp.float32), gate_rows.astype(jnp.float32))
    up_grad = jnp.einsum('ecd,ech->edh', outgoing.astype(jnp.float32), up_rows.astype(jnp.float32))
    rows_back = jnp.einsum('ech,edh->ecd', gate_rows.astype(jnp.float32), gate_weight.astype(jnp.float32))
    rows_back = rows_back + jnp.einsum('ech,edh->ecd', up_rows.astype(jnp.float32), up_weight.astype(jnp.float32))
    rows_back = rows_back.astype(jnp.bfloat16)
    normed2_back = normed2_back + lax.optimization_barrier(jnp.sum(rows_back[flat, slots].reshape(token_rows, choices_per, width).astype(jnp.float32), axis=1))
    resid_part, second_grad = rms_backward(resid, second_inverse, second_gain, normed2_back)
    resid_back = grad_out + resid_part
    attended_back = resid_back.astype(jnp.bfloat16)
    out_grad = jnp.dot(mixed_values.T, attended_back, preferred_element_type=jnp.float32)
    mixed_values_gradient = jnp.dot(attended_back, out_weight.T, preferred_element_type=jnp.float32).astype(jnp.bfloat16)
    mixed_values_gradient = mixed_values_gradient.reshape(token_rows, key_heads, head_group, HEAD_SIZE)
    second_pass = jnp.exp(score_block(query_rows, key_rows, mask) - logsum)
    value_rows_gradient = jnp.einsum('kjal,akjx->lkx', second_pass.astype(jnp.bfloat16).astype(jnp.float32), mixed_values_gradient.astype(jnp.float32))
    probability_gradient = jnp.einsum('qean,wen->eaqw', mixed_values_gradient.astype(jnp.float32), value_rows.astype(jnp.float32))
    delta = lax.optimization_barrier(jnp.sum(second_pass * probability_gradient, axis=-1, keepdims=True))
    score_gradient = (second_pass * (probability_gradient - delta) * SCORE_FACTOR).astype(jnp.bfloat16)
    query_rows_gradient = jnp.einsum('wmik,kwy->iwmy', score_gradient.astype(jnp.float32), key_rows.astype(jnp.float32)).reshape(token_rows, query_head_rows, HEAD_SIZE)
    key_rows_gradient = jnp.einsum('kjal,akjx->lkx', score_gradient.astype(jnp.float32), query_rows.astype(jnp.float32))
    query_rows_gradient = rotate_back(query_rows_gradient, cosine, sine).astype(jnp.bfloat16).reshape(token_rows, query_head_rows * HEAD_SIZE)
    key_rows_gradient = rotate_back(key_rows_gradient, cosine, sine).astype(jnp.bfloat16).reshape(token_rows, key_heads * HEAD_SIZE)
    value_rows_gradient = value_rows_gradient.astype(jnp.bfloat16).reshape(token_rows, key_heads * HEAD_SIZE)
    query_grad = jnp.dot(normed1.T, query_rows_gradient, preferred_element_type=jnp.float32)
    key_grad = jnp.dot(normed1.T, key_rows_gradient, preferred_element_type=jnp.float32)
    value_grad = jnp.dot(normed1.T, value_rows_gradient, preferred_element_type=jnp.float32)
    normed1_back = jnp.dot(query_rows_gradient, query_weight.T, preferred_element_type=jnp.float32)
    normed1_back = normed1_back + jnp.dot(key_rows_gradient, key_weight.T, preferred_element_type=jnp.float32)
    normed1_back = normed1_back + jnp.dot(value_rows_gradient, value_matrix.T, preferred_element_type=jnp.float32)
    input_part, first_grad = rms_backward(inputs, first_inverse, first_gain, normed1_back)
    input_grad = resid_back + input_part
    grads = (query_grad, key_grad, value_grad, out_grad, first_grad, second_grad, router_grad, gate_grad, up_grad, down_grad)
    return (layer_out, input_grad, grads)

def reference(tokens, segment_ids, routes, cotangent, query_weight, key_weight, value_matrix, out_weight, first_gain, second_gain, router_weight, gate_weight, up_weight, down_weight):
    devices = N_DP * N_EXPERT
    weights = (query_weight, key_weight, value_matrix, out_weight, first_gain, second_gain, router_weight, gate_weight, up_weight, down_weight)
    blocks = (tokens.reshape(devices, TOK_DEV, MODEL_WIDTH), segment_ids, routes.reshape(devices, TOK_DEV, TOPK), cotangent.reshape(devices, TOK_DEV, MODEL_WIDTH))
    zeros = tuple((jnp.zeros(weight.shape, jnp.float32) for weight in weights))

    def advance(carry, block):
        layer_out, input_grad, grads = layer(block[0], block[1], block[2], block[3], weights)
        return (tuple((total + part for total, part in zip(carry, grads))), (layer_out, input_grad))
    totals, (outputs, inputs_back) = lax.scan(advance, zeros, blocks)
    return (outputs.reshape(TOKENS, MODEL_WIDTH), inputs_back.reshape(TOKENS, MODEL_WIDTH), totals[0], totals[1], totals[2], totals[3], totals[4], totals[5], totals[6], totals[7], totals[8], totals[9])
```

```python
import functools
import jax, jax.numpy as jnp
from jax import lax
from jax.experimental import pallas as pl
from jax.experimental.pallas import tpu as pltpu

F32=jnp.float32; BF=jnp.bfloat16
def dot_nn(a,b): return lax.dot_general(a,b,(((1,),(0,)),((),())),preferred_element_type=F32)
def dot_nt(a,b): return lax.dot_general(a,b,(((1,),(1,)),((),())),preferred_element_type=F32)

def column(table, lane):
    at = lax.broadcasted_iota(jnp.int32, table.shape, 1) == lane
    return jnp.sum(jnp.where(at, table, 0.0), axis=1, keepdims=True)

def expert_kernel(blocks, where_ref, *refs):
    n2_refs, refs = refs[:blocks], refs[blocks:]
    cot_refs, refs = refs[:blocks], refs[blocks:]
    route_refs, refs = refs[:blocks], refs[blocks:]
    (router_ref, gate_ref, up_ref, down_ref,
     comb_ref, rows_ref, aux_ref, gates_ref, n2t_ref, hid_ref, grow_ref, urow_ref,
     n2, cot, comb, rows) = refs
    e = pl.program_id(0)
    own = where_ref[0]; dev = where_ref[1]
    experts_here = pl.num_programs(0)
    T = n2_refs[0].shape[0]; W = n2_refs[0].shape[1]; H = gate_ref.shape[2]
    C = 512
    n_dp = n2t_ref.shape[0] * n2t_ref.shape[1]; R = W // n_dp; D = H // n_dp

    @pl.when(e == 0)
    def _():
        for b in range(blocks):
            n2[b * T:(b + 1) * T, :] = n2_refs[b][...]
            cot[b * T:(b + 1) * T, :] = cot_refs[b][...]
            logits = dot_nn(n2_refs[b][...], router_ref[...])
            lane = lax.broadcasted_iota(jnp.int32, logits.shape, 1)
            named = lane < 0
            for k in range(route_refs[b].shape[1]):
                named = named | (lane == route_refs[b][:, k:k + 1])
            logits = jnp.where(named, logits, -1e30)
            top = jnp.max(logits, axis=1, keepdims=True)
            raised = jnp.where(named, jnp.exp(logits - top), 0.0)
            gates_ref[b * T:(b + 1) * T, :] = raised / jnp.sum(raised, axis=1, keepdims=True)
        aux_ref[...] = jnp.zeros_like(aux_ref)
        comb[...] = jnp.zeros_like(comb)
        rows[...] = jnp.zeros_like(rows)
        for r in range(n_dp):
            at = (r ^ dev) * R if False else None
        turned = n2[...].T
        for d in range(n_dp):
            r = d ^ dev
            n2t_ref[lax.rem(r, 2), lax.div(r, 2), :, :] = turned[d * R:(d + 1) * R, :]

    mine = own * experts_here + e
    g = column(gates_ref[...], mine)
    gate_pre = dot_nn(n2[...], gate_ref[0])
    up_pre = dot_nn(n2[...], up_ref[0])
    sig = 1.0 / (1.0 + jnp.exp(-gate_pre))
    silu = gate_pre * sig
    hidden = (silu * up_pre).astype(BF)
    turned = hidden.T
    for d in range(n_dp):
        r = d ^ dev
        hid_ref[0, lax.rem(r, 2), lax.div(r, 2), :, :] = turned[d * D:(d + 1) * D, :]
    back = jnp.zeros((blocks * T, 1), F32)
    hid_back = jnp.zeros((blocks * T, H), F32)
    for j in range(W // C):
        cols = slice(j * C, (j + 1) * C)
        made = dot_nn(hidden, down_ref[0, :, cols]).astype(BF).astype(F32)
        cj = cot[:, cols].astype(F32)
        back = back + jnp.sum(cj * made, axis=1, keepdims=True)
        comb[:, cols] += g * made
        hid_back = hid_back + dot_nt((g * cj).astype(BF), down_ref[0, :, cols])
    lane = lax.broadcasted_iota(jnp.int32, aux_ref.shape, 1)
    aux_ref[...] = jnp.where(lane == mine, back, aux_ref[...])
    grow = (hid_back * up_pre * sig * (1.0 + gate_pre * (1.0 - sig))).astype(BF)
    urow = (hid_back * silu).astype(BF)
    grow_ref[0] = grow
    urow_ref[0] = urow
    for j in range(W // C):
        cols = slice(j * C, (j + 1) * C)
        rows[:, cols] += dot_nt(grow, gate_ref[0, cols, :]) + dot_nt(urow, up_ref[0, cols, :])

    @pl.when(e == experts_here - 1)
    def _():
        comb_ref[...] = comb[...].astype(BF)
        rows_ref[...] = rows[...].astype(BF)

def expert_rows(where, n2s, cots, routes, router, gate_w, up_w, down_w, n_dp):
    blocks = len(n2s); T, W = n2s[0].shape; E, _, H = gate_w.shape
    R, D = W // n_dp, H // n_dp; A = blocks * T
    once = lambda s: pl.BlockSpec(s, lambda e, w: (0,) * len(s), pipeline_mode=pl.Buffered(1))
    out1 = lambda s: pl.BlockSpec(s, lambda e, w: (0,) * len(s))
    per = lambda s: pl.BlockSpec((1,) + s, lambda e, w: (e,) + (0,) * len(s))
    S = jax.ShapeDtypeStruct
    return pl.pallas_call(
        functools.partial(expert_kernel, blocks),
        out_shape=(S((A, W), BF), S((A, W), BF), S((A, 128), F32), S((A, 128), F32),
                   S((2, n_dp // 2, R, A), BF), S((E, 2, n_dp // 2, D, A), BF),
                   S((E, A, H), BF), S((E, A, H), BF)),
        grid_spec=pltpu.PrefetchScalarGridSpec(
            num_scalar_prefetch=1, grid=(E,),
            in_specs=[once((T, W))] * (2 * blocks) + [once((T, routes[0].shape[1]))] * blocks
            + [once((W, 128)), per((W, H)), per((W, H)), per((H, W))],
            out_specs=[out1((A, W)), out1((A, W)), out1((A, 128)), out1((A, 128)),
                       out1((2, n_dp // 2, R, A)), per((2, n_dp // 2, D, A)), per((A, H)), per((A, H))],
            scratch_shapes=[pltpu.VMEM((A, W), BF), pltpu.VMEM((A, W), BF),
                            pltpu.VMEM((A, W), F32), pltpu.VMEM((A, W), F32)]),
        compiler_params=pltpu.CompilerParams(vmem_limit_bytes=60 << 20),
        cost_estimate=pl.CostEstimate(flops=12 * A * W * H * E, bytes_accessed=6 * E * W * H + 12 * A * W, transcendentals=A * H * E),
    )(where, *n2s, *cots, *routes, router, gate_w, up_w, down_w)

def grad_kernel(blocks, first, where_ref, *refs):
    cot_refs, refs = refs[:blocks], refs[blocks:]
    gates_ref, n2t_ref, hid_ref, grow_ref, urow_ref, keep_ref, send_ref = refs
    T = cot_refs[0].shape[0]
    e = pl.program_id(0) + first
    experts_here = where_ref[2]
    half, R = n2t_ref.shape[1], n2t_ref.shape[2]; D = hid_ref.shape[3]; A = n2t_ref.shape[3]
    W = cot_refs[0].shape[1]; C = grow_ref.shape[2]
    g = column(gates_ref[...], where_ref[0] * experts_here + e)
    grow, urow = grow_ref[0], urow_ref[0]
    for s, out in ((1, send_ref), (0, keep_ref)):
        left = n2t_ref[s].reshape(half * R, A)
        out[0, :, 0:R, :] = dot_nn(left, grow).astype(BF).reshape(half, R, C)
        out[0, :, R:2 * R, :] = dot_nn(left, urow).astype(BF).reshape(half, R, C)
    for j in range(W // C):
        cols = slice(j * C, (j + 1) * C)
        rb = jnp.concatenate([(g[b * T:(b + 1) * T] * cot_refs[b][:, cols].astype(F32)).astype(BF) for b in range(blocks)], axis=0)
        for s, out in ((1, send_ref), (0, keep_ref)):
            left = hid_ref[0, s].reshape(half * D, A)
            out[0, :, 2 * R + j * D:2 * R + (j + 1) * D, :] = dot_nn(left, rb).astype(BF).reshape(half, D, C)

def expert_grads(first, count, where, cots, gates, n2t, hid, grow, urow):
    blocks = len(cots); T, W = cots[0].shape; E, A, H = grow.shape
    half, R = n2t.shape[1:3]; D = hid.shape[3]
    once = lambda s: pl.BlockSpec(s, lambda e, w: (0,) * len(s), pipeline_mode=pl.Buffered(1))
    per = lambda s: pl.BlockSpec((1,) + s, lambda e, w: (e + first,) + (0,) * len(s))
    S = jax.ShapeDtypeStruct
    P_ = 2 * R + (W // H) * D
    o = pl.BlockSpec((1, half, P_, H), lambda e, w: (e, 0, 0, 0))
    return pl.pallas_call(
        functools.partial(grad_kernel, blocks, first),
        out_shape=(S((count, half, P_, H), BF),) * 2,
        grid_spec=pltpu.PrefetchScalarGridSpec(
            num_scalar_prefetch=1, grid=(count,),
            in_specs=[once((T, W))] * blocks + [once((A, 128)), once((2, half, R, A)), per((2, half, D, A)), per((A, H)), per((A, H))],
            out_specs=[o, o]),
        compiler_params=pltpu.CompilerParams(vmem_limit_bytes=60 << 20),
        cost_estimate=pl.CostEstimate(flops=6 * A * W * H * count, bytes_accessed=6 * count * W * H + 6 * A * W, transcendentals=0),
    )(where, *cots, gates, n2t, hid, grow, urow)


from jax.sharding import PartitionSpec as P

HEAD_SIZE = 64
EPSILON = 1e-06
ROTARY_BASE = 10000.0
SCORE_FACTOR = 0.015625
HIGHEST = lax.Precision.HIGHEST
GROUPS = ((0, 2), (2, 2), (4, 1))


def attn_grad_kernel(blocks, dev_ref, *refs):
    n1_refs, refs = refs[:blocks], refs[blocks:]
    mix_refs, refs = refs[:blocks], refs[blocks:]
    qkv_refs, refs = refs[:blocks], refs[blocks:]
    att_refs, refs = refs[:blocks], refs[blocks:]
    keep_ref, send_ref, left = refs
    dev = dev_ref[0]
    T, W = n1_refs[0].shape
    half, R, C = keep_ref.shape
    n_dp = 2 * half
    at = 0
    for lefts, rights in ((n1_refs, qkv_refs), (mix_refs, att_refs)):
        width = rights[0].shape[1]
        for b in range(blocks):
            turned = lefts[b][...].T
            for d in range(n_dp):
                r = d ^ dev
                left[lax.rem(r, 2), lax.div(r, 2), :, b * T:(b + 1) * T] = turned[d * R:(d + 1) * R, :]
        right = jnp.concatenate([ref[...] for ref in rights], axis=0)
        for s, out in ((1, send_ref), (0, keep_ref)):
            out[:, :, at:at + width] = dot_nn(left[s].reshape(half * R, blocks * T), right).astype(BF).reshape(half, R, width)
        at += width


def attn_grads(dev, n1s, mixs, qkvs, atts, n_dp):
    blocks = len(n1s); T, W = n1s[0].shape
    C = qkvs[0].shape[1] + atts[0].shape[1]
    R = W // n_dp
    S = jax.ShapeDtypeStruct
    v = pl.BlockSpec(memory_space=pltpu.VMEM)
    return pl.pallas_call(
        functools.partial(attn_grad_kernel, blocks),
        out_shape=(S((n_dp // 2, R, C), BF),) * 2,
        in_specs=[pl.BlockSpec(memory_space=pltpu.SMEM)] + [v] * (4 * blocks),
        out_specs=(v, v),
        scratch_shapes=[pltpu.VMEM((2, n_dp // 2, R, blocks * T), BF)],
        compiler_params=pltpu.CompilerParams(vmem_limit_bytes=60 << 20),
        cost_estimate=pl.CostEstimate(flops=2 * blocks * T * W * C, bytes_accessed=4 * W * C, transcendentals=0),
    )(dev, *n1s, *mixs, *qkvs, *atts)


def rope_tables(positions, width):
    half = width // 2
    freq = ROTARY_BASE ** (-jnp.arange(half, dtype=F32) * 2.0 / width)
    angle = positions.astype(F32)[:, None] * freq[None, :]
    return (jnp.cos(angle)[:, None, :], jnp.sin(angle)[:, None, :])


def rotate(field, cosine, sine):
    half = field.shape[-1] // 2
    first, second = (field[..., :half], field[..., half:])
    return jnp.concatenate([first * cosine - second * sine, second * cosine + first * sine], axis=-1)


def rotate_back(grad, cosine, sine):
    half = grad.shape[-1] // 2
    first, second = (grad[..., :half], grad[..., half:])
    return jnp.concatenate([first * cosine + second * sine, second * cosine - first * sine], axis=-1)


def positions_of(segments):
    count = segments.shape[0]
    earlier = jnp.sum((segments[None, :] < segments[:, None]).astype(jnp.int32), axis=1)
    return jnp.arange(count, dtype=jnp.int32) - earlier


def attention_mask(segments):
    index = jnp.arange(segments.shape[0], dtype=jnp.int32)
    return (segments[:, None] == segments[None, :]) & (index[None, :] <= index[:, None])


def rms_forward(field, gain):
    inverse = lax.rsqrt(jnp.mean(field * field, axis=-1, keepdims=True) + EPSILON)
    return (inverse, field * inverse * gain)


def rms_backward(field, inverse, gain, grad):
    scaled = grad * gain
    inner = jnp.mean(scaled * field, axis=-1, keepdims=True)
    return (inverse * scaled - field * inverse**3 * inner, jnp.sum(grad * field * inverse, axis=0))


def score_block(query_rows, key_rows, mask):
    score_matrix = jnp.einsum("qean,wen->eaqw", query_rows, key_rows, preferred_element_type=F32) * SCORE_FACTOR
    return jnp.where(mask[None, None], score_matrix, -1e30)


def flip(x, axis, mask, size):
    return lax.ppermute(x, axis, [(i, i ^ mask) for i in range(size)])


def add(a, b):
    return (a.astype(F32) + b.astype(F32)).astype(BF)


def scatter_dp(keep, send, n_dp):
    bits = n_dp.bit_length() - 1
    whole = add(keep, flip(send, "dp", 1, n_dp))
    group, _, rows, cols = whole.shape
    parts = []
    for lo, hi, order in ((0, rows // 2, range(1, bits)), (rows // 2, rows, range(bits - 1, 0, -1))):
        part = whole.reshape((group,) + (2,) * (bits - 1) + (rows, cols))[..., lo:hi, :]
        left = list(range(bits - 1, 0, -1))
        for bit in order:
            axis = 1 + left.index(bit)
            mine = lax.index_in_dim(part, 0, axis, keepdims=False)
            theirs = flip(lax.index_in_dim(part, 1, axis, keepdims=False), "dp", 1 << bit, n_dp)
            left.remove(bit)
            part = add(mine, theirs) if left else mine.astype(F32) + theirs.astype(F32)
        parts.append(part)
    return jnp.concatenate(parts, axis=1)


def reorder(stack, index, size):
    bit = 1
    shape = stack.shape
    while bit < size:
        split = stack.reshape((size // (2 * bit), 2, bit) + shape[1:])
        stack = jnp.where((index & bit) != 0, split[:, ::-1], split).reshape(shape)
        bit *= 2
    return stack


def butterfly(x, n_dp, ne):
    for axis, size in (("dp", n_dp), ("expert", ne)):
        bit = 1
        while bit < size:
            x = x + flip(x, axis, bit, size)
            bit *= 2
    return x


def local(n_dp, ne, tokens, segment_ids, routes, cotangent, query_weight, key_weight, value_matrix, out_weight,
          first_gain, second_gain, router_weight, gate_weight, up_weight, down_weight):
    d = lax.axis_index("dp")
    z = lax.axis_index("expert")
    zx = lambda x, k: x if k == 0 else flip(x, "expert", k, ne)
    ks = range(ne)
    T, W = tokens.shape
    experts = router_weight.shape[1]
    E, _, H = gate_weight.shape
    R = W // n_dp
    D = H // n_dp
    KV = key_weight.shape[1]
    where = jnp.stack([z, d, jnp.int32(E), jnp.int32(0)]).astype(jnp.int32)

    small = jnp.concatenate([first_gain[None], second_gain[None], router_weight.T], axis=0)
    small = lax.all_gather(small, "dp", axis=0, tiled=False).transpose(1, 0, 2).reshape(2 + experts, W)
    gain_one = small[0].astype(F32)
    gain_two = small[1].astype(F32)
    router_t = small[2:]
    router_pad = jnp.pad(router_t.T, ((0, 0), (0, 128 - experts)))
    qkv_full = lax.all_gather(jnp.concatenate([query_weight, key_weight, value_matrix], axis=1), "dp", axis=0, tiled=True)
    out_full = lax.all_gather(out_weight, "dp", axis=0, tiled=True)
    cots = [zx(cotangent, k) for k in ks]
    picks = [zx(routes, k) for k in ks]

    key_heads = KV // HEAD_SIZE
    query_heads = query_weight.shape[1] // HEAD_SIZE
    head_group = query_heads // key_heads
    segments = segment_ids[0]
    mask = attention_mask(segments)
    cosine, sine = rope_tables(positions_of(segments), HEAD_SIZE)
    inputs = tokens.astype(F32)
    first_inverse, normed1 = rms_forward(inputs, gain_one)
    normed1 = normed1.astype(BF)
    qkv = jnp.dot(normed1, qkv_full, preferred_element_type=F32)
    query_rows = rotate(qkv[:, :W].reshape(T, query_heads, HEAD_SIZE), cosine, sine)
    query_rows = query_rows.astype(BF).reshape(T, key_heads, head_group, HEAD_SIZE)
    key_rows = rotate(qkv[:, W:W + KV].reshape(T, key_heads, HEAD_SIZE), cosine, sine).astype(BF)
    value_rows = qkv[:, W + KV:].astype(BF).reshape(T, key_heads, HEAD_SIZE)
    score_matrix = score_block(query_rows, key_rows, mask)
    peak = jnp.max(score_matrix, axis=-1, keepdims=True)
    logsum = peak + jnp.log(jnp.sum(jnp.exp(score_matrix - peak), axis=-1, keepdims=True))
    probabilities = jnp.exp(score_matrix - logsum).astype(BF)
    mixed = jnp.einsum("wmik,kwy->iwmy", probabilities, value_rows, preferred_element_type=F32)
    mixed = mixed.astype(BF).reshape(T, W)
    resid = inputs + jnp.dot(mixed, out_full, preferred_element_type=F32)
    second_inverse, normed2 = rms_forward(resid, gain_two)
    normed2 = normed2.astype(BF)

    n2s = [zx(normed2, k) for k in ks]
    comb, rows, aux, gates, n2t, hid, grow, urow = expert_rows(
        where, n2s, cots, picks, router_pad, gate_weight, up_weight, down_weight, n_dp)
    cut = lambda x, k: x[k * T:(k + 1) * T]
    back = sum(zx(cut(aux, k), k) for k in ks)
    rows_in = [zx(cut(rows, k), k) for k in ks]
    pieces = []
    for first, count in GROUPS:
        keep, send = expert_grads(first, count, where, cots, gates, n2t, hid, grow, urow)
        pieces.append(scatter_dp(keep, send, n_dp))
    comb_in = [zx(cut(comb, k), k) for k in ks]

    gates_own = gates[:T]
    logit_back = gates_own * (back - jnp.sum(gates_own * back, axis=1, keepdims=True))
    logit_back = logit_back[:, :experts]
    grad_out = cotangent.astype(F32)
    router_part = lax.dot_general(logit_back, normed2.astype(F32), (((0,), (0,)), ((), ())), precision=HIGHEST)
    normed2_back = jnp.dot(logit_back, router_t.astype(F32), precision=HIGHEST)
    normed2_back = normed2_back + sum(r.astype(F32) for r in rows_in)
    resid_part, second_part = rms_backward(resid, second_inverse, gain_two, normed2_back)
    resid_back = grad_out + resid_part
    attended_back = resid_back.astype(BF)
    layer_out = (resid + sum(c.astype(F32) for c in comb_in)).astype(BF)
    mixed_back = lax.dot_general(attended_back, out_full, (((1,), (1,)), ((), ())), preferred_element_type=F32).astype(BF)
    mixed_back = mixed_back.reshape(T, key_heads, head_group, HEAD_SIZE)
    second_pass = jnp.exp(score_matrix - logsum)
    value_back = jnp.einsum("kjal,akjx->lkx", second_pass.astype(BF), mixed_back, preferred_element_type=F32)
    prob_back = jnp.einsum("qean,wen->eaqw", mixed_back, value_rows, preferred_element_type=F32)
    delta = jnp.sum(second_pass * prob_back, axis=-1, keepdims=True)
    score_back = (second_pass * (prob_back - delta) * SCORE_FACTOR).astype(BF)
    query_back = jnp.einsum("wmik,kwy->iwmy", score_back, key_rows, preferred_element_type=F32).reshape(T, query_heads, HEAD_SIZE)
    key_back = jnp.einsum("kjal,akjx->lkx", score_back, query_rows, preferred_element_type=F32)
    query_back = rotate_back(query_back, cosine, sine).astype(BF).reshape(T, W)
    key_back = rotate_back(key_back, cosine, sine).astype(BF).reshape(T, KV)
    value_back = value_back.astype(BF).reshape(T, KV)

    def columns(x, k):
        width = x.shape[1] // ne
        return lax.dynamic_slice_in_dim(x, (z ^ k) * width, width, axis=1)

    n1s = [zx(normed1, k) for k in ks]
    mixs = [zx(mixed, k) for k in ks]
    atts = [zx(columns(attended_back, k), k) for k in ks]
    qkvs = [zx(jnp.concatenate([columns(query_back, k), columns(key_back, k), columns(value_back, k)], axis=1), k) for k in ks]
    keep, send = attn_grads(d.reshape(1).astype(jnp.int32), n1s, mixs, qkvs, atts, n_dp)
    part = scatter_dp(keep[None], send[None], n_dp)[0].astype(BF)
    full = reorder(jnp.stack([zx(part, k) for k in ks]), z, ne).astype(F32)
    edges = [0, W // ne, (W + KV) // ne, (W + 2 * KV) // ne, (2 * W + 2 * KV) // ne]
    query_grad, key_grad, value_grad, out_grad = [
        full[:, :, a:b].transpose(1, 0, 2).reshape(R, -1) for a, b in zip(edges[:-1], edges[1:])]

    back_qkv = jnp.concatenate([query_back, key_back, value_back], axis=1)
    normed1_back = lax.dot_general(back_qkv, qkv_full, (((1,), (1,)), ((), ())), preferred_element_type=F32)
    input_part, first_part = rms_backward(inputs, first_inverse, gain_one, normed1_back)
    input_grad = resid_back + input_part
    early = butterfly(jnp.concatenate([second_part[None], router_part], axis=0), n_dp, ne)
    late = butterfly(first_part[None], n_dp, ne)
    own = lambda x: lax.dynamic_slice_in_dim(x, d * R, R, axis=1)
    early, late = own(early), own(late)
    packed = jnp.concatenate(pieces, axis=0)
    gate_grad, up_grad = packed[:, :R], packed[:, R:2 * R]
    down_grad = packed[:, 2 * R:].reshape(E, W // H, D, H).transpose(0, 2, 1, 3).reshape(E, D, W)
    return (layer_out, input_grad, query_grad, key_grad, value_grad, out_grad, late[0], early[0], early[1:].T,
            gate_grad, up_grad, down_grad)


def solution(mesh):
    both = P(("dp", "expert"), None)
    dp = P("dp", None)
    own = P("expert", None, None)
    part = P("expert", "dp", None)
    return jax.shard_map(
        functools.partial(local, mesh.shape["dp"], mesh.shape["expert"]),
        mesh=mesh,
        in_specs=(both, both, both, both, dp, dp, dp, dp, P("dp"), P("dp"), dp, own, own, own),
        out_specs=(both, both, dp, dp, dp, dp, P("dp"), P("dp"), dp, part, part, part),
        check_vma=False,
    )
```

```python
import functools
import jax
import jax.numpy as jnp
from jax import lax
from jax.experimental import pallas as pl
from jax.experimental.pallas import tpu as pltpu
from jax.sharding import PartitionSpec as P

HEAD_SIZE = 64
EPSILON = 1e-06
ROTARY_BASE = 10000.0
SCORE_FACTOR = 0.015625
F32=jnp.float32; BF=jnp.bfloat16
def dot_nn(a,b): return lax.dot_general(a,b,(((1,),(0,)),((),())),preferred_element_type=F32)
def dot_nt(a,b): return lax.dot_general(a,b,(((1,),(1,)),((),())),preferred_element_type=F32)

def column(table, lane):
    at = lax.broadcasted_iota(jnp.int32, table.shape, 1) == lane
    return jnp.sum(jnp.where(at, table, 0.0), axis=1, keepdims=True)

def expert_kernel(blocks, choices, where_ref, *refs):
    n2_refs, refs = refs[:blocks], refs[blocks:]
    cot_refs, refs = refs[:blocks], refs[blocks:]
    (router_ref, gate_ref, up_ref, down_ref,
     comb_ref, rows_ref, gates_ref, n2t_ref, hid_ref, grow_ref, urow_ref,
     n2, cot, comb, rows, aux_ref) = refs
    e = pl.program_id(0)
    own = where_ref[0]
    experts_here = pl.num_programs(0)
    T = n2_refs[0].shape[0]; W = n2_refs[0].shape[1]; H = gate_ref.shape[2]
    C = 512

    @pl.when(e == 0)
    def _():
        for b in range(blocks):
            n2[b * T:(b + 1) * T, :] = n2_refs[b][...]
            cot[b * T:(b + 1) * T, :] = cot_refs[b][:, :W]
            picks = cot_refs[b][:, W:].astype(F32)
            logits = dot_nn(n2_refs[b][...], router_ref[...])
            lane = lax.broadcasted_iota(jnp.int32, logits.shape, 1)
            named = lane < 0
            for k in range(choices):
                named = named | (lane.astype(F32) == picks[:, k:k + 1])
            logits = jnp.where(named, logits, -1e30)
            top = jnp.max(logits, axis=1, keepdims=True)
            raised = jnp.where(named, jnp.exp(logits - top), 0.0)
            gates_ref[b * T:(b + 1) * T, :] = raised / jnp.sum(raised, axis=1, keepdims=True)
        aux_ref[...] = jnp.zeros_like(aux_ref)
        comb[...] = jnp.zeros_like(comb)
        rows[...] = jnp.zeros_like(rows)
        n2t_ref[...] = n2[...].T

    mine = own * experts_here + e
    g = column(gates_ref[...], mine)
    gate_pre = dot_nn(n2[...], gate_ref[0])
    up_pre = dot_nn(n2[...], up_ref[0])
    raw_back = dot_nt(cot[...], down_ref[0])
    sig = 1.0 / (1.0 + jnp.exp(-gate_pre))
    silu = gate_pre * sig
    hidden = (silu * up_pre).astype(BF).astype(F32)
    back = jnp.sum(hidden * raw_back, axis=1, keepdims=True)
    weighed = (g * hidden).astype(BF)
    hid_ref[0] = weighed.T
    lane = lax.broadcasted_iota(jnp.int32, aux_ref.shape, 1)
    aux_ref[...] = jnp.where(lane == mine, back, aux_ref[...])
    hid_back = g * raw_back
    grow = (hid_back * up_pre * (sig + silu * (1.0 - sig))).astype(BF)
    urow = (hid_back * silu).astype(BF)
    grow_ref[0] = grow
    urow_ref[0] = urow
    for j in range(W // C):
        cols = slice(j * C, (j + 1) * C)
        rows[:, cols] += dot_nt(grow, gate_ref[0, cols, :]) + dot_nt(urow, up_ref[0, cols, :])
        comb[:, cols] += dot_nn(weighed, down_ref[0, :, cols])

    @pl.when(e == experts_here - 1)
    def _():
        hi = aux_ref[...].astype(BF).astype(F32)
        packed = (hi + pltpu.roll(aux_ref[...] - hi, 64, 1)).astype(BF)
        for b in range(blocks):
            part = slice(b * T, (b + 1) * T)
            comb_ref[own ^ b] = comb[part, :].astype(BF)
            rows_ref[own ^ b, :, :W] = rows[part, :].astype(BF)
            rows_ref[own ^ b, :, W:] = packed[part, :]


def expert_rows(where, n2s, cots, choices, router, gate_w, up_w, down_w):
    blocks = len(n2s)
    T, W = n2s[0].shape
    E, _, H = gate_w.shape
    A = blocks * T
    once = lambda s: pl.BlockSpec(s, lambda e, w: (0,) * len(s), pipeline_mode=pl.Buffered(1))
    whole = lambda s: pl.BlockSpec(s, lambda e, w: (0,) * len(s))
    per = lambda s: pl.BlockSpec((1,) + s, lambda e, w: (e,) + (0,) * len(s))
    S = jax.ShapeDtypeStruct
    return pl.pallas_call(
        functools.partial(expert_kernel, blocks, choices),
        out_shape=(S((blocks, T, W), BF), S((blocks, T, W + 128), BF), S((A, 128), F32), S((W, A), BF),
                   S((E, H, A), BF), S((E, A, H), BF), S((E, A, H), BF)),
        grid_spec=pltpu.PrefetchScalarGridSpec(
            num_scalar_prefetch=1, grid=(E,),
            in_specs=[once((T, W))] * blocks + [once((T, W + 128))] * blocks
            + [once((W, 128)), per((W, H)), per((W, H)), per((H, W))],
            out_specs=[whole((blocks, T, W)), whole((blocks, T, W + 128)), whole((A, 128)), whole((W, A)),
                       per((H, A)), per((A, H)), per((A, H))],
            scratch_shapes=[pltpu.VMEM((A, W), BF), pltpu.VMEM((A, W), BF),
                            pltpu.VMEM((A, W), F32), pltpu.VMEM((A, W), F32), pltpu.VMEM((A, 128), F32)]),
        compiler_params=pltpu.CompilerParams(vmem_limit_bytes=60 << 20),
        cost_estimate=pl.CostEstimate(flops=12 * A * W * H * E, bytes_accessed=6 * E * W * H + 12 * A * W, transcendentals=A * H * E),
    )(where, *n2s, *cots, router, gate_w, up_w, down_w)


def grad_kernel(blocks, *refs):
    cot_refs, refs = refs[:blocks], refs[blocks:]
    n2t_ref, hid_ref, grow_ref, urow_ref, out_ref = refs
    n_dp, _, _, C = out_ref.shape
    W = n2t_ref.shape[0]
    H = hid_ref.shape[1]
    R, D = W // n_dp, H // n_dp
    left = n2t_ref[...]
    out_ref[:, 0, 0:R, :] = dot_nn(left, grow_ref[0]).astype(BF).reshape(n_dp, R, C)
    out_ref[:, 0, R:2 * R, :] = dot_nn(left, urow_ref[0]).astype(BF).reshape(n_dp, R, C)
    for j in range(W // C):
        cot = jnp.concatenate([ref[:, j * C:(j + 1) * C] for ref in cot_refs], axis=0)
        out_ref[:, 0, 2 * R + j * D:2 * R + (j + 1) * D, :] = dot_nn(hid_ref[0], cot).astype(BF).reshape(n_dp, D, C)


def expert_grads(first, count, cots, n2t, hid, grow, urow, n_dp):
    blocks = len(cots)
    T = cots[0].shape[0]
    W, A = n2t.shape
    _, _, H = grow.shape
    P_ = 2 * (W // n_dp) + (W // H) * (H // n_dp)
    once = lambda s: pl.BlockSpec(s, lambda e: (0,) * len(s), pipeline_mode=pl.Buffered(1))
    per = lambda s: pl.BlockSpec((1,) + s, lambda e: (e + first,) + (0,) * len(s))
    return pl.pallas_call(
        functools.partial(grad_kernel, blocks),
        out_shape=jax.ShapeDtypeStruct((n_dp, count, P_, H), BF),
        grid=(count,),
        in_specs=[once((T, W))] * blocks + [once((W, A)), per((H, A)), per((A, H)), per((A, H))],
        out_specs=pl.BlockSpec((n_dp, 1, P_, H), lambda e: (0, e, 0, 0)),
        compiler_params=pltpu.CompilerParams(vmem_limit_bytes=60 << 20),
        cost_estimate=pl.CostEstimate(flops=6 * A * W * H * count, bytes_accessed=6 * count * W * H + 6 * A * W, transcendentals=0),
    )(*cots, n2t, hid, grow, urow)


def rope_tile(x, cosine, sine):
    lane = lax.broadcasted_iota(jnp.int32, x.shape, 1)
    other = jnp.where(lax.rem(lane, 64) < 32, pltpu.roll(x, 96, 1), pltpu.roll(x, 32, 1))
    return x * cosine + other * sine


def half_mask(shape, half):
    lane = lax.broadcasted_iota(jnp.int32, shape, 1)
    return (lane < 64) if half == 0 else (lane >= 64)


def stacked(tiles, group, per, T):
    out = []
    for i in range(per):
        h = group * per + i
        x = tiles[h // 2]
        if h % 2 != group % 2:
            x = pltpu.roll(x, 64, 1)
        out.append(jnp.where(half_mask(x.shape, group % 2), x, 0.0).astype(BF))
    return jnp.concatenate(out, axis=0)


def unstacked(value, group, per, T, tiles):
    for i in range(per):
        h = group * per + i
        x = value[i * T:(i + 1) * T]
        if h % 2 != group % 2:
            x = pltpu.roll(x, 64, 1)
        x = jnp.where(half_mask(x.shape, h % 2), x, 0.0)
        tiles[h // 2] = x if tiles[h // 2] is None else tiles[h // 2] + x


def allowed(seg_row_ref, seg_col_ref, T, per):
    row = lax.broadcasted_iota(jnp.int32, (T, T), 0)
    col = lax.broadcasted_iota(jnp.int32, (T, T), 1)
    ok = (seg_col_ref[...] == seg_row_ref[...]) & (col <= row)
    bias = jnp.where(ok, 0.0, -1e30)
    return jnp.concatenate([bias] * per, axis=0)


def fetch(places, pieces, dev, dst, sems, at):
    R = pieces[0].shape[0]
    copies = []
    for i, ((r, col), piece) in enumerate(zip(places, pieces)):
        row = pl.multiple_of((dev ^ r) * R, R)
        copies.append(pltpu.make_async_copy(piece, dst.at[pl.ds(row, R), col:col + piece.shape[1]], sems.at[at + i]))
        copies[-1].start()
    return copies


def forward_kernel(places, dev_ref, tok_ref, n1_ref, g2_ref, cos_ref, sin_ref, segr_ref, segc_ref, qkv_hbm, *refs):
    outs, refs = refs[:len(places)], refs[len(places):]
    qkv_ref, mix_ref, resid_ref, n2_ref, wq, wo, sems = refs
    T, W = tok_ref.shape
    C = 512
    chunks = qkv_hbm.shape[1] // C
    copies = []
    for j in range(chunks):
        copies.append(pltpu.make_async_copy(qkv_hbm.at[:, j * C:(j + 1) * C], wq.at[j], sems.at[j]))
        copies[-1].start()
    fetched = fetch(places, outs, dev_ref[1], wo, sems, chunks)
    n1 = n1_ref[...]
    cosine, sine = cos_ref[...], sin_ref[...]
    tiles = []
    q_tiles = W // 128
    k_tiles = (qkv_hbm.shape[1] - W) // 256
    for j in range(chunks):
        copies[j].wait()
        made = dot_nn(n1, wq[j])
        for t in range(C // 128):
            tile = made[:, t * 128:(t + 1) * 128]
            if len(tiles) < q_tiles + k_tiles:
                tile = rope_tile(tile, cosine, sine)
            tile = tile.astype(BF)
            qkv_ref[:, len(tiles) * 128:(len(tiles) + 1) * 128] = tile
            tiles.append(tile)
    per = q_tiles // k_tiles
    bias = allowed(segr_ref, segc_ref, T, per)
    q = [t.astype(F32) for t in tiles[:q_tiles]]
    mixed = [None] * q_tiles
    for g in range(2 * k_tiles):
        k_tile, v_tile = tiles[q_tiles + g // 2], tiles[q_tiles + k_tiles + g // 2]
        s = dot_nt(stacked(q, g, per, T), k_tile) * SCORE_FACTOR + bias
        raised = jnp.exp(s - jnp.max(s, axis=1, keepdims=True))
        p = raised / jnp.sum(raised, axis=1, keepdims=True)
        unstacked(dot_nn(p.astype(BF), v_tile), g, per, T, mixed)
    for t in range(q_tiles):
        mix_ref[:, t * 128:(t + 1) * 128] = mixed[t].astype(BF)
    for copy in fetched:
        copy.wait()
    total = jnp.zeros((T, 1), F32)
    for j in range(W // C):
        cols = slice(j * C, (j + 1) * C)
        r = tok_ref[:, cols].astype(F32) + dot_nn(mix_ref[...], wo[:, cols])
        resid_ref[:, cols] = r
        total = total + jnp.sum(r * r, axis=1, keepdims=True)
    inverse = lax.rsqrt(total / W + EPSILON)
    n2_ref[...] = (resid_ref[...] * inverse * g2_ref[...]).astype(BF)


def forward(where, tokens, n1, gain2, cosine, sine, segr, segc, qkv_w, outs, places):
    T, W = tokens.shape
    N = qkv_w.shape[1]
    S = jax.ShapeDtypeStruct
    v = pl.BlockSpec(memory_space=pltpu.VMEM)
    hbm = pl.BlockSpec(memory_space=pl.ANY)
    return pl.pallas_call(
        functools.partial(forward_kernel, places),
        out_shape=(S((T, N), BF), S((T, W), BF), S((T, W), F32), S((T, W), BF)),
        in_specs=[pl.BlockSpec(memory_space=pltpu.SMEM)] + [v] * 7 + [hbm] * (1 + len(places)),
        out_specs=(v,) * 4,
        scratch_shapes=[pltpu.VMEM((N // 512, W, 512), BF), pltpu.VMEM((W, W), BF), pltpu.SemaphoreType.DMA((N // 512 + len(places),))],
        compiler_params=pltpu.CompilerParams(vmem_limit_bytes=60 << 20),
        cost_estimate=pl.CostEstimate(flops=12 * T * W * (N + W), bytes_accessed=2 * W * (N + W), transcendentals=24 * T * T),
    )(where, tokens, n1, gain2, cosine, sine, segr, segc, qkv_w, *outs)


def split(x):
    hi = x.astype(BF)
    return hi, (x - hi.astype(F32)).astype(BF)


def dot_tn(a, b): return lax.dot_general(a, b, (((0,), (0,)), ((), ())), preferred_element_type=F32)


def ones_at(T, lane):
    return jnp.where(lax.broadcasted_iota(jnp.int32, (T, 128), 1) == lane, 1.0, 0.0).astype(BF)


def middle_kernel(experts, *refs):
    (rows_ref, gates_ref, router_ref, n2_ref, resid_ref, g2_ref, cot_ref, att_ref, cut_ref, back_ref, extra_ref) = refs
    T, W = n2_ref.shape
    total = rows_ref[0].astype(F32)
    for b in range(1, rows_ref.shape[0]):
        total = total + rows_ref[b].astype(F32)
    aux = total[:, W:]
    gate_back = aux + pltpu.roll(aux, 64, 1)
    gates = gates_ref[...]
    hi, lo = split(gates * (gate_back - jnp.sum(gates * gate_back, axis=1, keepdims=True)))
    n2_back = total[:, :W] + dot_nt(hi, router_ref[...]) + dot_nt(lo, router_ref[...])
    resid = resid_ref[...]
    inverse = lax.rsqrt(jnp.mean(resid * resid, axis=1, keepdims=True) + EPSILON)
    scaled = n2_back * g2_ref[...]
    inner = jnp.mean(scaled * resid, axis=1, keepdims=True)
    back = cot_ref[...].astype(F32) + inverse * scaled - resid * (inverse * inverse * inverse * inner)
    back_ref[...] = back
    att_ref[...] = back.astype(BF)
    width = cut_ref.shape[2]
    for b in range(cut_ref.shape[0]):
        cut_ref[b] = back[:, b * width:(b + 1) * width].astype(BF)
    p_hi, p_lo = split(n2_back * resid * inverse)
    one = ones_at(T, experts)
    extra_ref[...] = dot_tn(n2_ref[...], hi) + dot_tn(n2_ref[...], lo) + dot_tn(p_hi, one) + dot_tn(p_lo, one)


def middle(rows_in, gates, router, n2, resid, gain2, cot, experts):
    T, W = n2.shape
    blocks = rows_in.shape[0]
    S = jax.ShapeDtypeStruct
    v = lambda s: pl.BlockSpec(s, lambda i: (0, 0))
    return pl.pallas_call(
        functools.partial(middle_kernel, experts),
        grid=(1,),
        out_shape=(S((T, W), BF), S((blocks, T, W // blocks), BF), S((T, W), F32), S((W, 128), F32)),
        in_specs=[pl.BlockSpec((blocks, T, W + 128), lambda i: (0, 0, 0)), v((T, 128)), v((W, 128)), v((T, W)), v((T, W)), v((1, W)), v((T, W))],
        out_specs=(v((T, W)), pl.BlockSpec((blocks, T, W // blocks), lambda i: (0, 0, 0)), v((T, W)), v((W, 128))),
        compiler_params=pltpu.CompilerParams(vmem_limit_bytes=40 << 20),
        cost_estimate=pl.CostEstimate(flops=12 * T * W * 128, bytes_accessed=30 * T * W, transcendentals=T),
    )(rows_in, gates, router, n2, resid, gain2, cot)


def backward_kernel(places, dev_ref, att_ref, qkv_ref, cos_ref, sin_ref, segr_ref, segc_ref, *refs):
    outs, refs = refs[:len(places)], refs[len(places):]
    back_ref, cut_ref, wo, sems = refs
    T, W = att_ref.shape
    fetched = fetch(places, outs, dev_ref[1], wo, sems, 0)
    q_tiles = W // 128
    k_tiles = (qkv_ref.shape[1] - W) // 256
    per = q_tiles // k_tiles
    tile = lambda t: qkv_ref[:, t * 128:(t + 1) * 128]
    q = [tile(t).astype(F32) for t in range(q_tiles)]
    bias = allowed(segr_ref, segc_ref, T, per)
    cosine, sine = cos_ref[...], -sin_ref[...]
    for copy in fetched:
        copy.wait()
    mixed_back = []
    for j in range(W // 512):
        made = dot_nt(att_ref[...], wo[j * 512:(j + 1) * 512, :]).astype(BF).astype(F32)
        mixed_back += [made[:, t * 128:(t + 1) * 128] for t in range(4)]
    q_back = [None] * q_tiles
    k_back = [None] * k_tiles
    v_back = [None] * k_tiles
    for g in range(2 * k_tiles):
        k_tile, v_tile = tile(q_tiles + g // 2), tile(q_tiles + k_tiles + g // 2)
        qs = stacked(q, g, per, T)
        ms = stacked(mixed_back, g, per, T)
        s = dot_nt(qs, k_tile) * SCORE_FACTOR + bias
        raised = jnp.exp(s - jnp.max(s, axis=1, keepdims=True))
        p = raised / jnp.sum(raised, axis=1, keepdims=True)
        dp = dot_nt(ms, v_tile)
        ds = (p * (dp - jnp.sum(p * dp, axis=1, keepdims=True)) * SCORE_FACTOR).astype(BF)
        unstacked(dot_nn(ds, k_tile), g, per, T, q_back)
        kb, vb = dot_tn(ds, qs), dot_tn(p.astype(BF), ms)
        k_back[g // 2] = kb if g % 2 == 0 else k_back[g // 2] + kb
        v_back[g // 2] = vb if g % 2 == 0 else v_back[g // 2] + vb
    made = [rope_tile(t, cosine, sine) for t in q_back + k_back] + v_back
    for t, value in enumerate(made):
        back_ref[:, t * 128:(t + 1) * 128] = value.astype(BF)
        of, place = (q_tiles, t) if t < q_tiles else (k_tiles, (t - q_tiles) % k_tiles)
        each = of // cut_ref.shape[0]
        at = place % each * 128 + (0 if t < q_tiles else (q_tiles + (k_tiles if t >= q_tiles + k_tiles else 0)) // cut_ref.shape[0] * 128)
        cut_ref[place // each, :, at:at + 128] = value.astype(BF)


def backward(where, att, qkv, cosine, sine, segr, segc, outs, places, ne):
    T, W = att.shape
    N = qkv.shape[1]
    S = jax.ShapeDtypeStruct
    v = pl.BlockSpec(memory_space=pltpu.VMEM)
    hbm = pl.BlockSpec(memory_space=pl.ANY)
    return pl.pallas_call(
        functools.partial(backward_kernel, places),
        out_shape=(S((T, N), BF), S((ne, T, N // ne), BF)),
        in_specs=[pl.BlockSpec(memory_space=pltpu.SMEM)] + [v] * 6 + [hbm] * len(places),
        out_specs=(v, v),
        scratch_shapes=[pltpu.VMEM((W, W), BF), pltpu.SemaphoreType.DMA((len(places),))],
        compiler_params=pltpu.CompilerParams(vmem_limit_bytes=60 << 20),
        cost_estimate=pl.CostEstimate(flops=30 * T * W * W, bytes_accessed=2 * W * W, transcendentals=24 * T * T),
    )(where, att, qkv, cosine, sine, segr, segc, *outs)


def last_kernel(experts, back_ref, tok_ref, g1_ref, resid_back_ref, extra_ref, w_ref, grad_ref, more_ref, nb):
    j = pl.program_id(0)
    T, W = tok_ref.shape
    C = w_ref.shape[0]
    nb[j] = dot_nt(back_ref[...], w_ref[...])

    @pl.when(j == pl.num_programs(0) - 1)
    def _():
        x = tok_ref[...].astype(F32)
        inverse = lax.rsqrt(jnp.mean(x * x, axis=1, keepdims=True) + EPSILON)
        n1_back = jnp.concatenate([nb[i] for i in range(W // C)], axis=1)
        scaled = n1_back * g1_ref[...]
        inner = jnp.mean(scaled * x, axis=1, keepdims=True)
        grad_ref[...] = resid_back_ref[...] + inverse * scaled - x * (inverse * inverse * inverse * inner)
        p_hi, p_lo = split(n1_back * x * inverse)
        one = ones_at(T, experts + 1)
        more_ref[...] = extra_ref[...] + dot_tn(p_hi, one) + dot_tn(p_lo, one)


def last(back, tokens, gain1, resid_back, extra, qkv_w, experts):
    T, W = tokens.shape
    N = back.shape[1]
    C = 512
    S = jax.ShapeDtypeStruct
    v = lambda s: pl.BlockSpec(s, lambda j: (0, 0))
    return pl.pallas_call(
        functools.partial(last_kernel, experts),
        grid=(W // C,),
        out_shape=(S((T, W), F32), S((W, 128), F32)),
        in_specs=[v((T, N)), v((T, W)), v((1, W)), v((T, W)), v((W, 128)), pl.BlockSpec((C, N), lambda j: (j, 0))],
        out_specs=(v((T, W)), v((W, 128))),
        scratch_shapes=[pltpu.VMEM((W // C, T, C), F32)],
        compiler_params=pltpu.CompilerParams(vmem_limit_bytes=40 << 20),
        cost_estimate=pl.CostEstimate(flops=6 * T * W * N, bytes_accessed=2 * W * N, transcendentals=T),
    )(back, tokens, gain1, resid_back, extra, qkv_w)


def attn_grad_kernel(blocks, where_ref, *refs):
    n1_refs, refs = refs[:blocks], refs[blocks:]
    mix_refs, refs = refs[:blocks], refs[blocks:]
    qkv_ref, att_ref, extra_ref, keep_ref, send_ref, left = refs
    own, dev = where_ref[0], where_ref[1]
    T = n1_refs[0].shape[0]
    W = extra_ref.shape[0]
    half, _, R, C = keep_ref.shape
    n_dp = 2 * half
    at = 0
    for side, right_ref in ((n1_refs, qkv_ref), (mix_refs, att_ref)):
        width = right_ref.shape[2]
        for b in range(blocks):
            turned = side[b][...].T
            for d in range(n_dp):
                r = d ^ dev
                left[lax.rem(r, 2), lax.div(r, 2), :, b * T:(b + 1) * T] = turned[d * R:(d + 1) * R, :]
        right = jnp.concatenate([right_ref[own ^ b] for b in range(blocks)], axis=0)
        for s, out in ((1, send_ref), (0, keep_ref)):
            out[:, 0, :, at:at + width] = dot_nn(left[s].reshape(half * R, blocks * T), right).astype(BF).reshape(half, R, width)
        at += width
    for d in range(n_dp):
        more = extra_ref[d * R:(d + 1) * R, :].astype(BF)
        r = d ^ dev

        @pl.when(lax.rem(r, 2) == 0)
        def _(more=more, r=r):
            keep_ref[lax.div(r, 2), 0, :, at:] = more

        @pl.when(lax.rem(r, 2) == 1)
        def _(more=more, r=r):
            send_ref[lax.div(r, 2), 0, :, at:] = more


def attn_grads(where, n1s, mixs, qkv_cut, att_cut, extra, n_dp):
    blocks = len(n1s)
    T = n1s[0].shape[0]
    W = extra.shape[0]
    C = qkv_cut.shape[2] + att_cut.shape[2] + 128
    R = W // n_dp
    S = jax.ShapeDtypeStruct
    v = pl.BlockSpec(memory_space=pltpu.VMEM)
    return pl.pallas_call(
        functools.partial(attn_grad_kernel, blocks),
        out_shape=(S((n_dp // 2, 1, R, C), BF),) * 2,
        in_specs=[pl.BlockSpec(memory_space=pltpu.SMEM)] + [v] * (2 * blocks + 3),
        out_specs=(v, v),
        scratch_shapes=[pltpu.VMEM((2, n_dp // 2, R, blocks * T), BF)],
        compiler_params=pltpu.CompilerParams(vmem_limit_bytes=60 << 20),
        cost_estimate=pl.CostEstimate(flops=2 * blocks * T * W * C, bytes_accessed=4 * W * C, transcendentals=0),
    )(where, *n1s, *mixs, qkv_cut, att_cut, extra)


def flip(x, axis, mask, size):
    return lax.ppermute(x, axis, [(i, i ^ mask) for i in range(size)])


def add(a, b):
    return (a.astype(F32) + b.astype(F32)).astype(BF)


def split_kernel(keep_ref, theirs_ref, a_keep, a_send, b_keep, b_send):
    count = keep_ref.shape[0]
    a = a_keep.shape[3]
    for q in range(count):
        total = (keep_ref[q, 0].astype(F32) + theirs_ref[q, 0].astype(F32)).astype(BF)
        out = a_send if q % 2 else a_keep
        out[q // 2, 0] = total[:, :a]
        out = b_send if q >= count // 2 else b_keep
        out[q % (count // 2), 0] = total[:, a:]


def halves(keep, theirs, n_dp):
    bits = n_dp.bit_length() - 1
    count, group, rows, cols = keep.shape
    a = cols // 256 * 128
    S = jax.ShapeDtypeStruct
    spec = lambda n, c: pl.BlockSpec((n, 1, rows, c), lambda g: (0, g, 0, 0))
    widths = (a, a, cols - a, cols - a)
    outs = pl.pallas_call(
        split_kernel,
        grid=(group,),
        out_shape=tuple(S((count // 2, group, rows, c), BF) for c in widths),
        in_specs=[spec(count, cols)] * 2,
        out_specs=tuple(spec(count // 2, c) for c in widths),
        compiler_params=pltpu.CompilerParams(vmem_limit_bytes=40 << 20),
        cost_estimate=pl.CostEstimate(flops=rows * cols, bytes_accessed=rows * cols, transcendentals=0),
    )(keep, theirs)
    left = tuple(range(bits - 1, 0, -1))
    shaped = lambda x: x.reshape((2,) * (bits - 2) + x.shape[1:])
    return [(shaped(outs[0]), shaped(outs[1]), left[:-1], tuple(range(1, bits))),
            (shaped(outs[2]), shaped(outs[3]), left[1:], left)]


def halve(parts, n_dp):
    done = []
    for mine, sent, left, order in parts:
        theirs = flip(sent, "dp", 1 << order[0], n_dp)
        if left:
            total = add(mine, theirs)
            axis = left.index(order[1])
            mine, theirs = (lax.index_in_dim(total, i, axis, keepdims=False) for i in (0, 1))
        done.append((mine, theirs, tuple(b for b in left if b != order[1]) if left else (), order[1:]))
    return done


def finish(parts, n_dp):
    while parts[0][3]:
        parts = halve(parts, n_dp)
    return parts


def tie_parts(parts, *others):
    arrays, others = lax.optimization_barrier(([p[:2] for p in parts], others))
    return [tuple(a) + p[2:] for a, p in zip(arrays, parts)], *others


def unpack_kernel(in_ref, gate_ref, up_ref, down_ref):
    R, D = gate_ref.shape[1], down_ref.shape[1]
    H = gate_ref.shape[2]
    total = in_ref[0, 0].astype(F32)
    gate_ref[0] = total[:R]
    up_ref[0] = total[R:2 * R]
    for j in range(down_ref.shape[2] // H):
        down_ref[0, :, j * H:(j + 1) * H] = total[2 * R + j * D:2 * R + (j + 1) * D]


def unpack(packed, R, D, W):
    _, E, rows, H = packed.shape
    S = jax.ShapeDtypeStruct
    out = lambda a, b: pl.BlockSpec((1, a, b), lambda e: (e, 0, 0))
    return pl.pallas_call(
        unpack_kernel,
        grid=(E,),
        out_shape=(S((E, R, H), F32), S((E, R, H), F32), S((E, D, W), F32)),
        in_specs=[pl.BlockSpec((1, 1, rows, H), lambda e: (0, e, 0, 0))],
        out_specs=(out(R, H), out(R, H), out(D, W)),
        compiler_params=pltpu.CompilerParams(vmem_limit_bytes=40 << 20),
        cost_estimate=pl.CostEstimate(flops=3 * E * R * H, bytes_accessed=18 * E * R * H, transcendentals=0),
    )(packed)


def spread_kernel(kv, where_ref, *refs):
    blocks = len(refs) - 5
    parts, (q_ref, k_ref, v_ref, o_ref, extra_ref) = refs[:blocks], refs[blocks:]
    wide, narrow = q_ref.shape[1] // blocks, kv // blocks
    extra = None
    for b, ref in enumerate(parts):
        at = where_ref[0] ^ b
        col = 0
        for out, width in ((q_ref, wide), (k_ref, narrow), (v_ref, narrow), (o_ref, wide)):
            out[:, pl.ds(pl.multiple_of(at * width, width), width)] = ref[:, col:col + width].astype(F32)
            col += width
        more = ref[:, col:].astype(F32)
        extra = more if extra is None else extra + more
    extra_ref[...] = extra


def spread(where, parts, W, kv):
    R, C = parts[0].shape
    S = jax.ShapeDtypeStruct
    v = pl.BlockSpec(memory_space=pltpu.VMEM)
    return pl.pallas_call(
        functools.partial(spread_kernel, kv),
        out_shape=(S((R, W), F32), S((R, kv), F32), S((R, kv), F32), S((R, W), F32), S((R, 128), F32)),
        in_specs=[pl.BlockSpec(memory_space=pltpu.SMEM)] + [v] * len(parts),
        out_specs=(v,) * 5,
        compiler_params=pltpu.CompilerParams(vmem_limit_bytes=40 << 20),
        cost_estimate=pl.CostEstimate(flops=R * C, bytes_accessed=24 * R * C, transcendentals=0),
    )(where, *parts)


def begin_z(x, ne):
    found = {0: x}
    bit = 1
    while bit < ne:
        found[bit] = flip(x, "expert", bit, ne)
        bit *= 2
    return found


def end_z(found, ne):
    for k in range(ne):
        if k not in found:
            found[k] = flip(found[k & (k - 1)], "expert", k & -k, ne)
    return [found[k] for k in range(ne)]


def gather_z(x, ne):
    return end_z(begin_z(x, ne), ne)


def gather_dp(w, n_dp):
    half = w.shape[1] // 2
    found = {(0, 0): w[:, :half], (0, half): w[:, half:]}
    whole = {0: w}
    for r in range(2, n_dp, 2):
        low, high = r & -r, 1 << (r.bit_length() - 1)
        if low == high:
            whole[r] = flip(w, "dp", r, n_dp)
            found[r, 0], found[r, half] = whole[r][:, :half], whole[r][:, half:]
        else:
            found[r, 0] = flip(found[r ^ high, 0], "dp", high, n_dp)
            found[r, half] = flip(found[r ^ low, half], "dp", low, n_dp)
    pieces = {}
    for (r, col), x in found.items():
        if r in whole:
            pieces[r, 0] = whole[r]
        else:
            pieces[r, col] = x
    for (r, col), x in list(pieces.items()):
        pieces[r ^ 1, col] = flip(x, "dp", 1, n_dp)
    places = sorted(pieces)
    return tuple(places), [pieces[p] for p in places]


def local(n_dp, ne, tokens, segment_ids, routes, cotangent, query_weight, key_weight, value_matrix, out_weight,
          first_gain, second_gain, router_weight, gate_weight, up_weight, down_weight):
    d = lax.axis_index("dp")
    z = lax.axis_index("expert")
    tie = lax.optimization_barrier
    T, W = tokens.shape
    experts = router_weight.shape[1]
    E, _, H = gate_weight.shape
    R = W // n_dp
    D = H // n_dp
    KV = key_weight.shape[1]
    where = jnp.stack([z, d, jnp.int32(E), jnp.int32(0)]).astype(jnp.int32)

    small = jnp.concatenate([first_gain[None], second_gain[None], router_weight.T], axis=0)
    small = lax.all_gather(small, "dp", axis=0, tiled=False).transpose(1, 0, 2).reshape(2 + experts, W)
    gain_one = small[0:1].astype(F32)
    gain_two = small[1:2].astype(F32)
    router_pad = jnp.pad(small[2:].T, ((0, 0), (0, 128 - experts)))
    qkv_full = lax.all_gather(jnp.concatenate([query_weight, key_weight, value_matrix], axis=1), "dp", axis=0, tiled=True)
    places, outs = gather_dp(out_weight, n_dp)
    choices = routes.shape[1]
    cot_routes = jnp.concatenate([cotangent, jnp.pad(routes.astype(BF), ((0, 0), (0, 128 - choices)))], axis=1)
    cots = gather_z(cot_routes, ne)

    segments = segment_ids[0]
    segr, segc = segments[None, :], segments[:, None]
    positions = jnp.arange(T, dtype=jnp.int32) - jnp.sum((segr < segc).astype(jnp.int32), axis=1)
    half = HEAD_SIZE // 2
    freq = ROTARY_BASE ** (-jnp.arange(half, dtype=F32) * 2.0 / HEAD_SIZE)
    angle = positions.astype(F32)[:, None] * freq[None, :]
    cosine = jnp.tile(jnp.cos(angle), (1, 4))
    sine = jnp.sin(angle)
    sine = jnp.concatenate([-sine, sine, -sine, sine], axis=1)
    inputs = tokens.astype(F32)
    normed1 = inputs * lax.rsqrt(jnp.mean(inputs * inputs, axis=-1, keepdims=True) + EPSILON) * gain_one
    normed1 = normed1.astype(BF)

    cots, outs, qkv_full = tie((cots, outs, qkv_full))
    qkv, mixed, resid, normed2 = forward(where, tokens, normed1, gain_two, cosine, sine, segr, segc, qkv_full, outs, places)
    core = lambda x: flip(x, "dp", 1, n_dp)
    exchange = lambda x: lax.all_to_all(x, "expert", split_axis=0, concat_axis=0, tiled=True)
    n2s = gather_z(normed2, ne)
    n2s, normed1, mixed = tie((n2s, normed1, mixed))
    n1s, mixs = begin_z(normed1, ne), begin_z(mixed, ne)
    made = expert_rows(where, n2s, cots, choices, router_pad, gate_weight, up_weight, down_weight)
    made, n1s, mixs = tie((made, n1s, mixs))
    comb, rows, gates, n2t, hid, grow, urow = made
    rows = exchange(rows)
    partial = expert_grads(0, E, cots, n2t, hid, grow, urow, n_dp)
    rows, partial, n1s, mixs = tie((rows, partial, n1s, mixs))
    packed = lax.psum_scatter(partial, "dp", scatter_dimension=0, tiled=True)
    n1s, mixs = end_z(n1s, ne), end_z(mixs, ne)
    attended, att_cut, resid_back, extra = middle(
        rows, gates, router_pad, normed2, resid, gain_two, cotangent, experts)
    att_cut = exchange(att_cut)
    back, back_cut = backward(where, attended, qkv, cosine, sine, segr, segc, outs, places, ne)
    att_cut, back, back_cut, n1s, mixs = tie((att_cut, back, back_cut, n1s, mixs))
    back_cut = exchange(back_cut)
    input_grad, extra = last(back, tokens, gain_one, resid_back, extra, qkv_full, experts)
    back_cut, extra, comb = tie((back_cut, extra, comb))
    comb = exchange(comb)
    keep, send = attn_grads(where, n1s, mixs, back_cut, att_cut, extra, n_dp)
    four = finish(halves(keep, core(send), n_dp), n_dp)
    part = jnp.concatenate([mine.astype(F32) + theirs.astype(F32) for mine, theirs, *_ in four], axis=-1)[0].astype(BF)
    part, comb = tie((part, comb))
    parts = gather_z(part, ne)
    query_grad, key_grad, value_grad, out_grad, extra = spread(where, parts, W, KV)
    layer_out = (resid + jnp.sum(comb.astype(F32), axis=0)).astype(BF)
    gate_grad, up_grad, down_grad = unpack(packed, R, D, W)
    return (layer_out, input_grad, query_grad, key_grad, value_grad, out_grad, extra[:, experts + 1], extra[:, experts],
            extra[:, :experts], gate_grad, up_grad, down_grad)


def solution(mesh):
    both = P(("dp", "expert"), None)
    dp = P("dp", None)
    own = P("expert", None, None)
    part = P("expert", "dp", None)
    return jax.shard_map(
        functools.partial(local, mesh.shape["dp"], mesh.shape["expert"]),
        mesh=mesh,
        in_specs=(both, both, both, both, dp, dp, dp, dp, P("dp"), P("dp"), dp, own, own, own),
        out_specs=(both, both, dp, dp, dp, dp, P("dp"), P("dp"), dp, part, part, part),
        check_vma=False,
    )
```

```python
import functools
import jax
import jax.numpy as jnp
from jax import lax
from jax.experimental import pallas as pl
from jax.experimental.pallas import tpu as pltpu
from jax.sharding import PartitionSpec as P

HEAD_SIZE = 64
EPSILON = 1e-06
ROTARY_BASE = 10000.0
SCORE_FACTOR = 0.015625
MANY = 4
F32=jnp.float32; BF=jnp.bfloat16
def dot_nn(a,b): return lax.dot_general(a,b,(((1,),(0,)),((),())),preferred_element_type=F32)
def dot_nt(a,b): return lax.dot_general(a,b,(((1,),(1,)),((),())),preferred_element_type=F32)

def column(table, lane):
    at = lax.broadcasted_iota(jnp.int32, table.shape, 1) == lane
    return jnp.sum(jnp.where(at, table, 0.0), axis=1, keepdims=True)

def expert_kernel(blocks, choices, where_ref, *refs):
    n2_refs, refs = refs[:blocks], refs[blocks:]
    cot_refs, refs = refs[:blocks], refs[blocks:]
    (router_ref, gate_ref, up_ref, down_ref,
     rows_ref, gates_ref, n2t_ref, hid_ref, weighed_ref, grow_ref, urow_ref,
     n2, cot, rows, aux_ref) = refs
    e = pl.program_id(0)
    own = where_ref[0]
    experts_here = pl.num_programs(0)
    T = n2_refs[0].shape[0]; W = n2_refs[0].shape[1]; H = gate_ref.shape[2]
    C = 512

    @pl.when(e == 0)
    def _():
        for b in range(blocks):
            n2[b * T:(b + 1) * T, :] = n2_refs[b][...]
            cot[b * T:(b + 1) * T, :] = cot_refs[b][:, :W]
            picks = cot_refs[b][:, W:].astype(F32)
            logits = dot_nn(n2_refs[b][...], router_ref[...])
            lane = lax.broadcasted_iota(jnp.int32, logits.shape, 1)
            named = lane < 0
            for k in range(choices):
                named = named | (lane.astype(F32) == picks[:, k:k + 1])
            logits = jnp.where(named, logits, -1e30)
            top = jnp.max(logits, axis=1, keepdims=True)
            raised = jnp.where(named, jnp.exp(logits - top), 0.0)
            gates_ref[b * T:(b + 1) * T, :] = raised / jnp.sum(raised, axis=1, keepdims=True)
        aux_ref[...] = jnp.zeros_like(aux_ref)
        rows[...] = jnp.zeros_like(rows)

    mine = own * experts_here + e
    g = column(gates_ref[...], mine)
    gate_pre = dot_nn(n2[...], gate_ref[0])
    up_pre = dot_nn(n2[...], up_ref[0])
    raw_back = dot_nt(cot[...], down_ref[0])
    sig = 1.0 / (1.0 + jnp.exp(-gate_pre))
    silu = gate_pre * sig
    hidden = (silu * up_pre).astype(BF).astype(F32)
    back = jnp.sum(hidden * raw_back, axis=1, keepdims=True)
    weighed = (g * hidden).astype(BF)
    weighed_ref[0] = weighed
    hid_ref[0] = weighed.T
    part = pl.multiple_of(jnp.minimum(e, W // C - 1) * C, C)
    n2t_ref[pl.ds(part, C), :] = n2[:, pl.ds(part, C)].T
    lane = lax.broadcasted_iota(jnp.int32, aux_ref.shape, 1)
    aux_ref[...] = jnp.where(lane == mine, back, aux_ref[...])
    hid_back = g * raw_back
    grow = (hid_back * up_pre * (sig + silu * (1.0 - sig))).astype(BF)
    urow = (hid_back * silu).astype(BF)
    grow_ref[0] = grow
    urow_ref[0] = urow
    for j in range(W // C):
        cols = slice(j * C, (j + 1) * C)
        rows[:, cols] += dot_nt(grow, gate_ref[0, cols, :]) + dot_nt(urow, up_ref[0, cols, :])

    @pl.when(e == experts_here - 1)
    def _():
        hi = aux_ref[...].astype(BF).astype(F32)
        packed = (hi + pltpu.roll(aux_ref[...] - hi, 64, 1)).astype(BF)
        for b in range(blocks):
            part = slice(b * T, (b + 1) * T)
            rows_ref[own ^ b, :, :W] = rows[part, :].astype(BF)
            rows_ref[own ^ b, :, W:] = packed[part, :]


def expert_rows(where, n2s, cots, choices, router, gate_w, up_w, down_w):
    blocks = len(n2s)
    T, W = n2s[0].shape
    E, _, H = gate_w.shape
    A = blocks * T
    once = lambda s: pl.BlockSpec(s, lambda e, w: (0,) * len(s), pipeline_mode=pl.Buffered(1))
    whole = lambda s: pl.BlockSpec(s, lambda e, w: (0,) * len(s))
    per = lambda s: pl.BlockSpec((1,) + s, lambda e, w: (e,) + (0,) * len(s))
    S = jax.ShapeDtypeStruct
    return pl.pallas_call(
        functools.partial(expert_kernel, blocks, choices),
        out_shape=(S((blocks, T, W + 128), BF), S((A, 128), F32), S((W, A), BF),
                   S((E, H, A), BF), S((E, A, H), BF), S((E, A, H), BF), S((E, A, H), BF)),
        grid_spec=pltpu.PrefetchScalarGridSpec(
            num_scalar_prefetch=1, grid=(E,),
            in_specs=[once((T, W))] * blocks + [once((T, W + 128))] * blocks
            + [once((W, 128)), per((W, H)), per((W, H)), per((H, W))],
            out_specs=[whole((blocks, T, W + 128)), whole((A, 128)), whole((W, A)),
                       per((H, A)), per((A, H)), per((A, H)), per((A, H))],
            scratch_shapes=[pltpu.VMEM((A, W), BF), pltpu.VMEM((A, W), BF), pltpu.VMEM((A, W), F32), pltpu.VMEM((A, 128), F32)]),
        compiler_params=pltpu.CompilerParams(vmem_limit_bytes=60 << 20),
        cost_estimate=pl.CostEstimate(flops=10 * A * W * H * E, bytes_accessed=6 * E * W * H + 12 * A * W, transcendentals=A * H * E),
    )(where, *n2s, *cots, router, gate_w, up_w, down_w)


def grad_kernel(blocks, apart, where_ref, *refs):
    cot_refs, refs = refs[:blocks], refs[blocks:]
    n2t_ref, hid_ref, grow_ref, urow_ref, *outs = refs
    C = grow_ref.shape[2]
    W = n2t_ref.shape[0]
    H = hid_ref.shape[1]
    n_dp = outs[0].shape[0] * len(outs)
    R, D = W // n_dp, H // n_dp
    core = where_ref[1] % 2

    def store(value, rows):
        if not apart:
            outs[0][:, 0, rows, :] = value
            return
        for own in range(2):
            @pl.when(core == own)
            def _(own=own):
                for d in range(n_dp):
                    outs[(d % 2) ^ own][d // 2, 0, rows, :] = value[d]

    left = n2t_ref[...]
    store(dot_nn(left, grow_ref[0]).astype(BF).reshape(n_dp, R, C), slice(0, R))
    store(dot_nn(left, urow_ref[0]).astype(BF).reshape(n_dp, R, C), slice(R, 2 * R))
    for j in range(W // C):
        cot = jnp.concatenate([ref[:, j * C:(j + 1) * C] for ref in cot_refs], axis=0)
        store(dot_nn(hid_ref[0], cot).astype(BF).reshape(n_dp, D, C), slice(2 * R + j * D, 2 * R + (j + 1) * D))


def expert_grads(first, count, apart, where, cots, n2t, hid, grow, urow, n_dp):
    blocks = len(cots)
    T = cots[0].shape[0]
    W, A = n2t.shape
    _, _, H = grow.shape
    P_ = 2 * (W // n_dp) + (W // H) * (H // n_dp)
    shape = (n_dp // 2 if apart else n_dp, count, P_, H)
    once = lambda s: pl.BlockSpec(s, lambda e, w: (0,) * len(s), pipeline_mode=pl.Buffered(1))
    per = lambda s: pl.BlockSpec((1,) + s, lambda e, w: (e + first,) + (0,) * len(s))
    outs = 2 if apart else 1
    made = pl.pallas_call(
        functools.partial(grad_kernel, blocks, apart),
        out_shape=(jax.ShapeDtypeStruct(shape, BF),) * outs,
        grid_spec=pltpu.PrefetchScalarGridSpec(
            num_scalar_prefetch=1, grid=(count,),
            in_specs=[once((T, W))] * blocks + [once((W, A)), per((H, A)), per((A, H)), per((A, H))],
            out_specs=(pl.BlockSpec((shape[0], 1, P_, H), lambda e, w: (0, e, 0, 0)),) * outs),
        compiler_params=pltpu.CompilerParams(vmem_limit_bytes=60 << 20),
        cost_estimate=pl.CostEstimate(flops=0, bytes_accessed=0, transcendentals=0),
    )(where, *cots, n2t, hid, grow, urow)
    return made if apart else made[0]


def combine_kernel(blocks, where_ref, weighed_ref, down_ref, gains_ref, *refs):
    payloads, (comb_ref, n1t_ref, total) = refs[:blocks], refs[blocks:]
    e = pl.program_id(0)
    own, dev = where_ref[0], where_ref[1]
    T = payloads[0].shape[0]
    W = comb_ref.shape[2]
    _, half, R, _ = n1t_ref.shape
    made = dot_nn(weighed_ref[0], down_ref[0])

    @pl.when(e == 0)
    def _():
        total[...] = made
        for b in range(blocks):
            x = payloads[b][:, W + 128:].astype(F32)
            inverse = lax.rsqrt(jnp.mean(x * x, axis=1, keepdims=True) + EPSILON)
            turned = (x * inverse * gains_ref[0:1, :]).astype(BF).T
            for d in range(2 * half):
                r = d ^ dev
                n1t_ref[lax.rem(r, 2), lax.div(r, 2), :, b * T:(b + 1) * T] = turned[d * R:(d + 1) * R, :]

    @pl.when(e > 0)
    def _():
        total[...] += made

    @pl.when(e == pl.num_programs(0) - 1)
    def _():
        for b in range(blocks):
            comb_ref[own ^ b] = total[b * T:(b + 1) * T, :].astype(BF)


def combine(where, weighed, down_w, gains, payloads, n_dp):
    E, A, H = weighed.shape
    W = down_w.shape[2]
    blocks = len(payloads)
    T = A // blocks
    R = W // n_dp
    whole = lambda s: pl.BlockSpec(s, lambda e, w: (0,) * len(s))
    once = lambda s: pl.BlockSpec(s, lambda e, w: (0,) * len(s), pipeline_mode=pl.Buffered(1))
    per = lambda s: pl.BlockSpec((1,) + s, lambda e, w: (e,) + (0,) * len(s))
    S = jax.ShapeDtypeStruct
    return pl.pallas_call(
        functools.partial(combine_kernel, blocks),
        out_shape=(S((blocks, T, W), BF), S((2, n_dp // 2, R, A), BF)),
        grid_spec=pltpu.PrefetchScalarGridSpec(
            num_scalar_prefetch=1, grid=(E,),
            in_specs=[per((A, H)), per((H, W)), once((8, W))] + [once((T, 2 * W + 128))] * blocks,
            out_specs=[whole((blocks, T, W)), whole((2, n_dp // 2, R, A))],
            scratch_shapes=[pltpu.VMEM((A, W), F32)]),
        compiler_params=pltpu.CompilerParams(vmem_limit_bytes=60 << 20),
        cost_estimate=pl.CostEstimate(flops=0, bytes_accessed=0, transcendentals=0),
    )(where, weighed, down_w, gains, *payloads)


def rope_tile(x, cosine, sine):
    lane = lax.broadcasted_iota(jnp.int32, x.shape, 1)
    other = jnp.where(lax.rem(lane, 64) < 32, pltpu.roll(x, 96, 1), pltpu.roll(x, 32, 1))
    return x * cosine + other * sine


def half_mask(shape, half):
    lane = lax.broadcasted_iota(jnp.int32, shape, 1)
    return (lane < 64) if half == 0 else (lane >= 64)


def stacked(tiles, group, per, T):
    out = []
    for i in range(per):
        h = group * per + i
        x = tiles[h // 2]
        if h % 2 != group % 2:
            x = pltpu.roll(x, 64, 1)
        out.append(jnp.where(half_mask(x.shape, group % 2), x, 0.0).astype(BF))
    return jnp.concatenate(out, axis=0)


def unstacked(value, group, per, T, tiles):
    for i in range(per):
        h = group * per + i
        x = value[i * T:(i + 1) * T]
        if h % 2 != group % 2:
            x = pltpu.roll(x, 64, 1)
        x = jnp.where(half_mask(x.shape, h % 2), x, 0.0)
        tiles[h // 2] = x if tiles[h // 2] is None else tiles[h // 2] + x


def allowed(seg_row_ref, seg_col_ref, T, per):
    row = lax.broadcasted_iota(jnp.int32, (T, T), 0)
    col = lax.broadcasted_iota(jnp.int32, (T, T), 1)
    ok = (seg_col_ref[...] == seg_row_ref[...]) & (col <= row)
    bias = jnp.where(ok, 0.0, -1e30)
    return jnp.concatenate([bias] * per, axis=0)


def fetch(places, pieces, dev, dst, sems, at, lo, hi):
    R = pieces[0].shape[0]
    copies = []
    for i, ((r, col), piece) in enumerate(zip(places, pieces)):
        a, b = max(lo, col), min(hi, col + piece.shape[1])
        if a < b:
            row = pl.multiple_of((dev ^ r) * R, R)
            copies.append(pltpu.make_async_copy(
                piece.at[:, a - col:b - col], dst.at[pl.ds(row, R), a - lo:b - lo], sems.at[at + i]))
            copies[-1].start()
    return copies


def forward_kernel(places, kv, experts, dev_ref, tok_ref, cos_ref, sin_ref, segr_ref, segc_ref, q_hbm, *refs):
    pieces, refs = refs[:len(places)], refs[len(places):]
    qkv_ref, mix_ref, resid_ref, n2_ref, gains_ref, router_ref, kv_ref, wq, wo, sems = refs
    T, W = tok_ref.shape
    C = 512
    chunks = W // C
    fetched = fetch(places, pieces, dev_ref[1], wo, sems, chunks, 0, wo.shape[1])
    copies = []
    for j in range(chunks):
        copies.append(pltpu.make_async_copy(q_hbm.at[:, j * C:(j + 1) * C], wq.at[j], sems.at[j]))
        copies[-1].start()
    x = tok_ref[...].astype(F32)
    inverse = lax.rsqrt(jnp.mean(x * x, axis=1, keepdims=True) + EPSILON)
    for copy in fetched:
        copy.wait()
    keep = pltpu.make_async_copy(wo.at[:, :2 * kv], kv_ref, sems.at[chunks + len(places)])
    keep.start()
    small = wo[:, 2 * kv + W:]
    router_ref[...] = small
    turned = small.astype(F32).T
    gain1, gain2 = turned[experts:experts + 1, :], turned[experts + 1:experts + 2, :]
    gains_ref[0:1, :] = gain1
    gains_ref[1:2, :] = gain2
    gains_ref[2:8, :] = jnp.zeros((6, W), F32)
    n1 = (x * inverse * gain1).astype(BF)
    cosine, sine = cos_ref[...], sin_ref[...]
    q_tiles = W // 128
    k_tiles = kv // 128
    side = dot_nn(n1, wo[:, :2 * kv])
    others = [side[:, t * 128:(t + 1) * 128] for t in range(2 * k_tiles)]
    others = [rope_tile(t, cosine, sine).astype(BF) for t in others[:k_tiles]] + [t.astype(BF) for t in others[k_tiles:]]
    tiles = []
    for j in range(chunks):
        copies[j].wait()
        made = dot_nn(n1, wq[j])
        tiles += [rope_tile(made[:, t * 128:(t + 1) * 128], cosine, sine).astype(BF) for t in range(C // 128)]
    tiles += others
    for t, tile in enumerate(tiles):
        qkv_ref[:, t * 128:(t + 1) * 128] = tile
    per = q_tiles // k_tiles
    bias = allowed(segr_ref, segc_ref, T, per)
    q = [t.astype(F32) for t in tiles[:q_tiles]]
    mixed = [None] * q_tiles
    for g in range(2 * k_tiles):
        k_tile, v_tile = tiles[q_tiles + g // 2], tiles[q_tiles + k_tiles + g // 2]
        s = dot_nt(stacked(q, g, per, T), k_tile) * SCORE_FACTOR + bias
        raised = jnp.exp(s - jnp.max(s, axis=1, keepdims=True))
        p = raised / jnp.sum(raised, axis=1, keepdims=True)
        unstacked(dot_nn(p.astype(BF), v_tile), g, per, T, mixed)
    for t in range(q_tiles):
        mix_ref[:, t * 128:(t + 1) * 128] = mixed[t].astype(BF)
    total = jnp.zeros((T, 1), F32)
    for j in range(chunks):
        cols = slice(j * C, (j + 1) * C)
        r = tok_ref[:, cols].astype(F32) + dot_nn(mix_ref[...], wo[:, 2 * kv + j * C:2 * kv + (j + 1) * C])
        resid_ref[:, cols] = r
        total = total + jnp.sum(r * r, axis=1, keepdims=True)
    inverse = lax.rsqrt(total / W + EPSILON)
    n2_ref[...] = (resid_ref[...] * inverse * gain2).astype(BF)
    keep.wait()


def forward(where, tokens, cosine, sine, segr, segc, q_w, pieces, places, kv, experts):
    T, W = tokens.shape
    N = W + 2 * kv
    S = jax.ShapeDtypeStruct
    v = pl.BlockSpec(memory_space=pltpu.VMEM)
    hbm = pl.BlockSpec(memory_space=pl.ANY)
    return pl.pallas_call(
        functools.partial(forward_kernel, places, kv, experts),
        out_shape=(S((T, N), BF), S((T, W), BF), S((T, W), F32), S((T, W), BF), S((8, W), F32), S((W, 128), BF), S((W, 2 * kv), BF)),
        in_specs=[pl.BlockSpec(memory_space=pltpu.SMEM)] + [v] * 5 + [hbm] * (1 + len(places)),
        out_specs=(v,) * 6 + (hbm,),
        scratch_shapes=[pltpu.VMEM((W // 512, W, 512), BF), pltpu.VMEM((W, N + 128), BF),
                        pltpu.SemaphoreType.DMA((W // 512 + len(places) + 1,))],
        compiler_params=pltpu.CompilerParams(vmem_limit_bytes=60 << 20),
        cost_estimate=pl.CostEstimate(flops=0, bytes_accessed=0, transcendentals=0),
    )(where, tokens, cosine, sine, segr, segc, q_w, *pieces)


def split(x):
    hi = x.astype(BF)
    return hi, (x - hi.astype(F32)).astype(BF)


def dot_tn(a, b): return lax.dot_general(a, b, (((0,), (0,)), ((), ())), preferred_element_type=F32)


def ones_at(T, lane):
    return jnp.where(lax.broadcasted_iota(jnp.int32, (T, 128), 1) == lane, 1.0, 0.0).astype(BF)


def middle_kernel(experts, *refs):
    (rows_ref, gates_ref, router_ref, n2_ref, resid_ref, g2_ref, cot_ref, att_ref, cut_ref, back_ref, extra_ref) = refs
    T, W = n2_ref.shape
    total = rows_ref[0].astype(F32)
    for b in range(1, rows_ref.shape[0]):
        total = total + rows_ref[b].astype(F32)
    aux = total[:, W:]
    gate_back = aux + pltpu.roll(aux, 64, 1)
    gates = gates_ref[...]
    hi, lo = split(gates * (gate_back - jnp.sum(gates * gate_back, axis=1, keepdims=True)))
    n2_back = total[:, :W] + dot_nt(hi, router_ref[...]) + dot_nt(lo, router_ref[...])
    resid = resid_ref[...]
    inverse = lax.rsqrt(jnp.mean(resid * resid, axis=1, keepdims=True) + EPSILON)
    scaled = n2_back * g2_ref[1:2, :]
    inner = jnp.mean(scaled * resid, axis=1, keepdims=True)
    back = cot_ref[...].astype(F32) + inverse * scaled - resid * (inverse * inverse * inverse * inner)
    back_ref[...] = back
    att_ref[...] = back.astype(BF)
    width = cut_ref.shape[2]
    for b in range(cut_ref.shape[0]):
        cut_ref[b] = back[:, b * width:(b + 1) * width].astype(BF)
    p_hi, p_lo = split(n2_back * resid * inverse)
    one = ones_at(T, experts)
    extra_ref[...] = dot_tn(n2_ref[...], hi) + dot_tn(n2_ref[...], lo) + dot_tn(p_hi, one) + dot_tn(p_lo, one)


def middle(rows_in, gates, router, n2, resid, gain2, cot, experts):
    T, W = n2.shape
    blocks = rows_in.shape[0]
    S = jax.ShapeDtypeStruct
    v = lambda s: pl.BlockSpec(s, lambda i: (0, 0))
    return pl.pallas_call(
        functools.partial(middle_kernel, experts),
        grid=(1,),
        out_shape=(S((T, W), BF), S((blocks, T, W // blocks), BF), S((T, W), F32), S((W, 128), F32)),
        in_specs=[pl.BlockSpec((blocks, T, W + 128), lambda i: (0, 0, 0)), v((T, 128)), v((W, 128)), v((T, W)), v((T, W)), v((8, W)), v((T, W))],
        out_specs=(v((T, W)), pl.BlockSpec((blocks, T, W // blocks), lambda i: (0, 0, 0)), v((T, W)), v((W, 128))),
        compiler_params=pltpu.CompilerParams(vmem_limit_bytes=40 << 20),
        cost_estimate=pl.CostEstimate(flops=400_000_000_000, bytes_accessed=30 * T * W, transcendentals=T),
    )(rows_in, gates, router, n2, resid, gain2, cot)


def backward_kernel(places, dev_ref, att_ref, qkv_ref, cos_ref, sin_ref, segr_ref, segc_ref, *refs):
    outs, refs = refs[:len(places)], refs[len(places):]
    back_ref, cut_ref, wo, sems = refs
    T, W = att_ref.shape
    fetched = fetch(places, outs, dev_ref[1], wo, sems, 0, qkv_ref.shape[1] - W, qkv_ref.shape[1])
    q_tiles = W // 128
    k_tiles = (qkv_ref.shape[1] - W) // 256
    per = q_tiles // k_tiles
    tile = lambda t: qkv_ref[:, t * 128:(t + 1) * 128]
    q = [tile(t).astype(F32) for t in range(q_tiles)]
    bias = allowed(segr_ref, segc_ref, T, per)
    cosine, sine = cos_ref[...], -sin_ref[...]
    for copy in fetched:
        copy.wait()
    mixed_back = []
    for j in range(W // 512):
        made = dot_nt(att_ref[...], wo[j * 512:(j + 1) * 512, :]).astype(BF).astype(F32)
        mixed_back += [made[:, t * 128:(t + 1) * 128] for t in range(4)]
    q_back = [None] * q_tiles
    k_back = [None] * k_tiles
    v_back = [None] * k_tiles
    for g in range(2 * k_tiles):
        k_tile, v_tile = tile(q_tiles + g // 2), tile(q_tiles + k_tiles + g // 2)
        qs = stacked(q, g, per, T)
        ms = stacked(mixed_back, g, per, T)
        s = dot_nt(qs, k_tile) * SCORE_FACTOR + bias
        raised = jnp.exp(s - jnp.max(s, axis=1, keepdims=True))
        p = raised / jnp.sum(raised, axis=1, keepdims=True)
        dp = dot_nt(ms, v_tile)
        ds = (p * (dp - jnp.sum(p * dp, axis=1, keepdims=True)) * SCORE_FACTOR).astype(BF)
        unstacked(dot_nn(ds, k_tile), g, per, T, q_back)
        kb, vb = dot_tn(ds, qs), dot_tn(p.astype(BF), ms)
        k_back[g // 2] = kb if g % 2 == 0 else k_back[g // 2] + kb
        v_back[g // 2] = vb if g % 2 == 0 else v_back[g // 2] + vb
    made = [rope_tile(t, cosine, sine) for t in q_back + k_back] + v_back
    for t, value in enumerate(made):
        back_ref[:, t * 128:(t + 1) * 128] = value.astype(BF)
        of, place = (q_tiles, t) if t < q_tiles else (k_tiles, (t - q_tiles) % k_tiles)
        each = of // cut_ref.shape[0]
        at = place % each * 128 + (0 if t < q_tiles else (q_tiles + (k_tiles if t >= q_tiles + k_tiles else 0)) // cut_ref.shape[0] * 128)
        cut_ref[place // each, :, at:at + 128] = value.astype(BF)


def backward(where, att, qkv, cosine, sine, segr, segc, outs, places, ne):
    T, W = att.shape
    N = qkv.shape[1]
    S = jax.ShapeDtypeStruct
    v = pl.BlockSpec(memory_space=pltpu.VMEM)
    hbm = pl.BlockSpec(memory_space=pl.ANY)
    return pl.pallas_call(
        functools.partial(backward_kernel, places),
        out_shape=(S((T, N), BF), S((ne, T, N // ne), BF)),
        in_specs=[pl.BlockSpec(memory_space=pltpu.SMEM)] + [v] * 6 + [hbm] * len(places),
        out_specs=(v, v),
        scratch_shapes=[pltpu.VMEM((W, W), BF), pltpu.SemaphoreType.DMA((len(places),))],
        compiler_params=pltpu.CompilerParams(vmem_limit_bytes=60 << 20),
        cost_estimate=pl.CostEstimate(flops=0, bytes_accessed=0, transcendentals=0),
    )(where, att, qkv, cosine, sine, segr, segc, *outs)


def last_kernel(experts, back_ref, tok_ref, g1_ref, resid_back_ref, extra_ref, q_ref, kv_ref, grad_ref, more_ref, nb):
    j = pl.program_id(0)
    T, W = tok_ref.shape
    C = q_ref.shape[0]
    nb[j] = dot_nt(back_ref[:, :W], q_ref[...]) + dot_nt(back_ref[:, W:], kv_ref[...])

    @pl.when(j == pl.num_programs(0) - 1)
    def _():
        x = tok_ref[...].astype(F32)
        inverse = lax.rsqrt(jnp.mean(x * x, axis=1, keepdims=True) + EPSILON)
        n1_back = jnp.concatenate([nb[i] for i in range(W // C)], axis=1)
        scaled = n1_back * g1_ref[0:1, :]
        inner = jnp.mean(scaled * x, axis=1, keepdims=True)
        grad_ref[...] = resid_back_ref[...] + inverse * scaled - x * (inverse * inverse * inverse * inner)
        p_hi, p_lo = split(n1_back * x * inverse)
        one = ones_at(T, experts + 1)
        more_ref[...] = extra_ref[...] + dot_tn(p_hi, one) + dot_tn(p_lo, one)


def last(back, tokens, gains, resid_back, extra, q_w, kv_w, experts):
    T, W = tokens.shape
    N = back.shape[1]
    C = 512
    S = jax.ShapeDtypeStruct
    v = lambda s: pl.BlockSpec(s, lambda j: (0, 0))
    return pl.pallas_call(
        functools.partial(last_kernel, experts),
        grid=(W // C,),
        out_shape=(S((T, W), F32), S((W, 128), F32)),
        in_specs=[v((T, N)), v((T, W)), v((8, W)), v((T, W)), v((W, 128)), pl.BlockSpec((C, W), lambda j: (j, 0)),
                  pl.BlockSpec((C, N - W), lambda j: (j, 0))],
        out_specs=(v((T, W)), v((W, 128))),
        scratch_shapes=[pltpu.VMEM((W // C, T, C), F32)],
        compiler_params=pltpu.CompilerParams(vmem_limit_bytes=40 << 20),
        cost_estimate=pl.CostEstimate(flops=0, bytes_accessed=0, transcendentals=0),
    )(back, tokens, gains, resid_back, extra, q_w, kv_w)


def out_grad_kernel(blocks, where_ref, *refs):
    mix_refs, (att_ref, keep_ref, send_ref, left) = refs[:blocks], refs[blocks:]
    own, dev = where_ref[0], where_ref[1]
    T = mix_refs[0].shape[0]
    half, _, R, C = keep_ref.shape
    for b in range(blocks):
        turned = mix_refs[b][...].T
        for d in range(2 * half):
            r = d ^ dev
            left[lax.rem(r, 2), lax.div(r, 2), :, b * T:(b + 1) * T] = turned[d * R:(d + 1) * R, :]
    right = jnp.concatenate([att_ref[own ^ b] for b in range(blocks)], axis=0)
    for s, out in ((1, send_ref), (0, keep_ref)):
        out[:, 0] = dot_nn(left[s].reshape(half * R, blocks * T), right).astype(BF).reshape(half, R, C)


def out_grads(where, mixs, att_cut, n_dp):
    blocks = len(mixs)
    T, W = mixs[0].shape
    C = att_cut.shape[2]
    R = W // n_dp
    S = jax.ShapeDtypeStruct
    v = pl.BlockSpec(memory_space=pltpu.VMEM)
    return pl.pallas_call(
        functools.partial(out_grad_kernel, blocks),
        out_shape=(S((n_dp // 2, 1, R, C), BF),) * 2,
        in_specs=[pl.BlockSpec(memory_space=pltpu.SMEM)] + [v] * (blocks + 1),
        out_specs=(v, v),
        scratch_shapes=[pltpu.VMEM((2, n_dp // 2, R, blocks * T), BF)],
        compiler_params=pltpu.CompilerParams(vmem_limit_bytes=60 << 20),
        cost_estimate=pl.CostEstimate(flops=0, bytes_accessed=0, transcendentals=0),
    )(where, *mixs, att_cut)


def qkv_grad_kernel(where_ref, left_ref, qkv_ref, extra_ref, keep_ref, send_ref):
    own, dev = where_ref[0], where_ref[1]
    blocks, _, width = qkv_ref.shape
    half, _, R, C = keep_ref.shape
    right = jnp.concatenate([qkv_ref[own ^ b] for b in range(blocks)], axis=0)
    for s, out in ((1, send_ref), (0, keep_ref)):
        left = left_ref[s].reshape(half * R, left_ref.shape[3])
        out[:, 0, :, :width] = dot_nn(left, right).astype(BF).reshape(half, R, width)
    for d in range(2 * half):
        more = extra_ref[d * R:(d + 1) * R, :].astype(BF)
        r = d ^ dev

        @pl.when(lax.rem(r, 2) == 0)
        def _(more=more, r=r):
            keep_ref[lax.div(r, 2), 0, :, width:] = more

        @pl.when(lax.rem(r, 2) == 1)
        def _(more=more, r=r):
            send_ref[lax.div(r, 2), 0, :, width:] = more


def qkv_grads(where, left, qkv_cut, extra, n_dp):
    W = extra.shape[0]
    C = qkv_cut.shape[2] + 128
    R = W // n_dp
    S = jax.ShapeDtypeStruct
    v = pl.BlockSpec(memory_space=pltpu.VMEM)
    return pl.pallas_call(
        qkv_grad_kernel,
        out_shape=(S((n_dp // 2, 1, R, C), BF),) * 2,
        in_specs=[pl.BlockSpec(memory_space=pltpu.SMEM)] + [v] * 3,
        out_specs=(v, v),
        compiler_params=pltpu.CompilerParams(vmem_limit_bytes=60 << 20),
        cost_estimate=pl.CostEstimate(flops=2 * W * C * left.shape[3], bytes_accessed=4 * W * C, transcendentals=0),
    )(where, left, qkv_cut, extra)


def flip(x, axis, mask, size):
    return lax.ppermute(x, axis, [(i, i ^ mask) for i in range(size)])


def add(a, b):
    return (a.astype(F32) + b.astype(F32)).astype(BF)


def split_kernel(width, where_ref, *refs):
    ins, (a_keep, a_send, b_keep, b_send) = refs[:-4], refs[-4:]
    count = ins[0].shape[-4]
    for q in range(count):
        at = q ^ where_ref[0]
        sums = [(ins[i][at, 0].astype(F32) + ins[i + 1][at, 0].astype(F32)).astype(BF) for i in range(0, len(ins), 2)]
        total = sums[0] if len(sums) == 1 else jnp.concatenate(sums, axis=1)
        out = a_send if q % 2 else a_keep
        out[q // 2, 0] = total[:, :width]
        out = b_send if q >= count // 2 else b_keep
        out[q % (count // 2), 0] = total[:, width:]


def halves(pairs, n_dp, order=None):
    bits = n_dp.bit_length() - 1
    count, group, rows, _ = pairs[0][1].shape
    cols = sum(theirs.shape[3] for _, theirs in pairs)
    a = cols // 256 * 128
    S = jax.ShapeDtypeStruct
    if order is None:
        order = jnp.zeros((1,), jnp.int32)
    specs = []
    for keep, theirs in pairs:
        shape = (count, 1, rows, theirs.shape[3])
        specs += [pl.BlockSpec(shape, lambda g, w: (0, g, 0, 0))] * 2
    widths = (a, a, cols - a, cols - a)
    outs = pl.pallas_call(
        functools.partial(split_kernel, a),
        out_shape=tuple(S((count // 2, group, rows, c), BF) for c in widths),
        grid_spec=pltpu.PrefetchScalarGridSpec(
            num_scalar_prefetch=1, grid=(group,), in_specs=specs,
            out_specs=tuple(pl.BlockSpec((count // 2, 1, rows, c), lambda g, w: (0, g, 0, 0)) for c in widths)),
        compiler_params=pltpu.CompilerParams(vmem_limit_bytes=40 << 20),
        cost_estimate=pl.CostEstimate(flops=0, bytes_accessed=0, transcendentals=0),
    )(order.astype(jnp.int32), *[x for pair in pairs for x in pair])
    left = tuple(range(bits - 1, 0, -1))
    shaped = lambda x: x.reshape((2,) * (bits - 2) + x.shape[1:])
    return [(shaped(outs[0]), shaped(outs[1]), left[:-1], tuple(range(1, bits))),
            (shaped(outs[2]), shaped(outs[3]), left[1:], left)]


def halve(parts, n_dp):
    done = []
    for mine, sent, left, order in parts:
        theirs = flip(sent, "dp", 1 << order[0], n_dp)
        if left:
            total = add(mine, theirs)
            axis = left.index(order[1])
            mine, theirs = (lax.index_in_dim(total, i, axis, keepdims=False) for i in (0, 1))
        done.append((mine, theirs, tuple(b for b in left if b != order[1]) if left else (), order[1:]))
    return done


def finish(parts, n_dp):
    while parts[0][3]:
        parts = halve(parts, n_dp)
    return parts


def tie_parts(parts, *others):
    arrays, others = lax.optimization_barrier(([p[:2] for p in parts], others))
    return [tuple(a) + p[2:] for a, p in zip(arrays, parts)], *others


def unpack_kernel(many, in_ref, *refs):
    parts, (gate_ref, up_ref, down_ref) = refs[:-3], refs[-3:]
    R, D = gate_ref.shape[1], down_ref.shape[1]
    H = gate_ref.shape[2]

    def store(total, at):
        width = total.shape[1]
        gate_ref[0, :, at:at + width] = total[:R]
        up_ref[0, :, at:at + width] = total[R:2 * R]
        for j in range(down_ref.shape[2] // H):
            down_ref[0, :, j * H + at:j * H + at + width] = total[2 * R + j * D:2 * R + (j + 1) * D]

    @pl.when(pl.program_id(0) < many)
    def _():
        store(in_ref[0, 0].astype(F32), 0)

    @pl.when(pl.program_id(0) >= many)
    def _():
        at = 0
        for mine, theirs in (parts[:2], parts[2:]):
            store(mine[0].astype(F32) + theirs[0].astype(F32), at)
            at += mine.shape[2]


def unpack(packed, parts, R, D, W):
    _, many, rows, H = packed.shape
    E = many + parts[0].shape[0]
    S = jax.ShapeDtypeStruct
    out = lambda a, b: pl.BlockSpec((1, a, b), lambda e: (e, 0, 0))
    return pl.pallas_call(
        functools.partial(unpack_kernel, many),
        grid=(E,),
        out_shape=(S((E, R, H), F32), S((E, R, H), F32), S((E, D, W), F32)),
        in_specs=[pl.BlockSpec((1, 1, rows, H), lambda e: (0, jnp.minimum(e, many - 1), 0, 0))]
        + [pl.BlockSpec((1, rows, x.shape[2]), lambda e: (jnp.maximum(e - many, 0), 0, 0)) for x in parts],
        out_specs=(out(R, H), out(R, H), out(D, W)),
        compiler_params=pltpu.CompilerParams(vmem_limit_bytes=40 << 20),
        cost_estimate=pl.CostEstimate(flops=3 * E * R * H, bytes_accessed=18 * E * R * H, transcendentals=0),
    )(packed, *parts)


def spread_kernel(kv, where_ref, *refs):
    parts, (q_ref, k_ref, v_ref, o_ref, extra_ref) = refs[:-5], refs[-5:]
    blocks = len(parts)
    wide, narrow = q_ref.shape[1] // blocks, kv // blocks
    extra = None
    for b, ref in enumerate(parts):
        at = where_ref[0] ^ b
        col = 0
        for out, width in ((o_ref, wide), (q_ref, wide), (k_ref, narrow), (v_ref, narrow)):
            out[:, pl.ds(pl.multiple_of(at * width, width), width)] = ref[:, col:col + width].astype(F32)
            col += width
        more = ref[:, col:].astype(F32)
        extra = more if extra is None else extra + more
    extra_ref[...] = extra


def spread(where, parts, W, kv):
    R, C = parts[0].shape
    S = jax.ShapeDtypeStruct
    v = pl.BlockSpec(memory_space=pltpu.VMEM)
    return pl.pallas_call(
        functools.partial(spread_kernel, kv),
        out_shape=(S((R, W), F32), S((R, kv), F32), S((R, kv), F32), S((R, W), F32), S((R, 128), F32)),
        in_specs=[pl.BlockSpec(memory_space=pltpu.SMEM)] + [v] * len(parts),
        out_specs=(v,) * 5,
        compiler_params=pltpu.CompilerParams(vmem_limit_bytes=40 << 20),
        cost_estimate=pl.CostEstimate(flops=R * C, bytes_accessed=24 * R * C, transcendentals=0),
    )(where, *parts)


def begin_z(x, ne):
    found = {0: x}
    bit = 1
    while bit < ne:
        found[bit] = flip(x, "expert", bit, ne)
        bit *= 2
    return found


def end_z(found, ne):
    for k in range(ne):
        if k not in found:
            found[k] = flip(found[k & (k - 1)], "expert", k & -k, ne)
    return [found[k] for k in range(ne)]


def gather_z(x, ne):
    return end_z(begin_z(x, ne), ne)


def direct_z(x, ne):
    return [x] + [flip(x, "expert", bit, ne) for bit in range(1, ne)]


def gather_dp(w, n_dp, ready):
    half = w.shape[1] // 256 * 128
    found = {(0, 0): w[:, :half], (0, half): w[:, half:]}
    whole = {0: w}
    bits = range(1, n_dp.bit_length() - 1)
    for bit in bits:
        whole[1 << bit] = flip(w, "dp", 1 << bit, n_dp)
    whole, ready = lax.optimization_barrier((whole, ready))
    for bit in bits:
        r = 1 << bit
        found[r, 0], found[r, half] = whole[r][:, :half], whole[r][:, half:]
    for r in range(2, n_dp, 2):
        low, high = r & -r, 1 << (r.bit_length() - 1)
        if low != high:
            found[r, 0] = flip(found[r ^ high, 0], "dp", high, n_dp)
            found[r, half] = flip(found[r ^ low, half], "dp", low, n_dp)
    pieces = {}
    for (r, col), x in found.items():
        if r in whole:
            pieces[r, 0] = whole[r]
        else:
            pieces[r, col] = x
    for (r, col), x in list(pieces.items()):
        pieces[r ^ 1, col] = flip(x, "dp", 1, n_dp)
    places = sorted(pieces)
    return tuple(places), [pieces[p] for p in places], ready


def local(n_dp, ne, tokens, segment_ids, routes, cotangent, query_weight, key_weight, value_matrix, out_weight,
          first_gain, second_gain, router_weight, gate_weight, up_weight, down_weight):
    d = lax.axis_index("dp")
    z = lax.axis_index("expert")
    tie = lax.optimization_barrier
    T, W = tokens.shape
    experts = router_weight.shape[1]
    E, _, H = gate_weight.shape
    R = W // n_dp
    D = H // n_dp
    KV = key_weight.shape[1]
    where = jnp.stack([z, d, jnp.int32(E), jnp.int32(0)]).astype(jnp.int32)

    q_full = lax.all_gather(query_weight, "dp", axis=0, tiled=True)
    side = jnp.concatenate([key_weight, value_matrix, out_weight, router_weight, first_gain[:, None], second_gain[:, None],
                            jnp.zeros((R, 126 - experts), BF)], axis=1)
    segments = segment_ids[0]
    segr, segc = segments[None, :], segments[:, None]
    positions = jnp.arange(T, dtype=jnp.int32) - jnp.sum((segr < segc).astype(jnp.int32), axis=1)
    half = HEAD_SIZE // 2
    freq = ROTARY_BASE ** (-jnp.arange(half, dtype=F32) * 2.0 / HEAD_SIZE)
    angle = positions.astype(F32)[:, None] * freq[None, :]
    cosine = jnp.tile(jnp.cos(angle), (1, 4))
    sine = jnp.sin(angle)
    sine = jnp.concatenate([-sine, sine, -sine, sine], axis=1)
    choices = routes.shape[1]
    payload = jnp.concatenate([cotangent, jnp.pad(routes.astype(BF), ((0, 0), (0, 128 - choices))), tokens], axis=1)
    places, pieces, (cosine, sine, segc, where) = gather_dp(side, n_dp, (cosine, sine, segc, where))
    payloads = gather_z(payload, ne)
    core = lambda x: flip(x, "dp", 1, n_dp)
    exchange = lambda x: lax.all_to_all(x, "expert", split_axis=0, concat_axis=0, tiled=True)
    payloads, pieces, q_full = tie((payloads, pieces, q_full))
    qkv, mixed, resid, normed2, gains, router, kv_full = forward(
        where, tokens, cosine, sine, segr, segc, q_full, pieces, places, KV, experts)
    n2s = gather_z(normed2, ne)
    n2s, mixed = tie((n2s, mixed))
    mixs = direct_z(mixed, ne)
    made = expert_rows(where, n2s, payloads, choices, router, gate_weight, up_weight, down_weight)
    made, mixs = tie((made, mixs))
    rows, gates, n2t, hid, weighed, grow, urow = made
    rows = exchange(rows)
    partial = expert_grads(0, MANY, False, where, payloads, n2t, hid, grow, urow, n_dp)
    packed = lax.psum_scatter(partial, "dp", scatter_dimension=0, tiled=True)
    partial, n2t, weighed = tie((partial, n2t, weighed))
    few, away = expert_grads(MANY, E - MANY, True, where, payloads, n2t, hid, grow, urow, n_dp)
    comb, n1t = combine(where, weighed, down_weight, gains, payloads, n_dp)
    rows, few, away, comb, n1t = tie((rows, few, away, comb, n1t))
    theirs = core(away)
    attended, att_cut, resid_back, extra = middle(rows, gates, router, normed2, resid, gains, cotangent, experts)
    att_cut = exchange(att_cut)
    back, back_cut = backward(where, attended, qkv, cosine, sine, segr, segc, pieces, places, ne)
    att_cut, back, back_cut, few, theirs = tie((att_cut, back, back_cut, few, theirs))
    back_cut = exchange(back_cut)
    few = halve(halves([(few, theirs)], n_dp, (d // 2).reshape(1)), n_dp)
    input_grad, extra = last(back, tokens, gains, resid_back, extra, q_full, kv_full, experts)
    keep4, send4 = out_grads(where, mixs, att_cut, n_dp)
    few, back_cut, extra, keep4, send4, comb = tie_parts(few, back_cut, extra, keep4, send4, comb)
    theirs4 = core(send4)
    few = finish(few, n_dp)
    keep5, send5 = qkv_grads(where, n1t, back_cut, extra, n_dp)
    keep5, send5, theirs4, comb = tie((keep5, send5, theirs4, comb))
    comb = exchange(comb)
    five = finish(halves([(keep4, theirs4), (keep5, core(send5))], n_dp), n_dp)
    part = jnp.concatenate([mine.astype(F32) + theirs.astype(F32) for mine, theirs, *_ in five], axis=-1)[0].astype(BF)
    part, comb = tie((part, comb))
    parts = begin_z(part, ne)
    few, parts = tie_parts(few, parts)
    parts = end_z(parts, ne)
    query_grad, key_grad, value_grad, out_grad, extra = spread(where, parts, W, KV)
    layer_out = (resid + jnp.sum(comb.astype(F32), axis=0)).astype(BF)
    gate_grad, up_grad, down_grad = unpack(packed, [x for p in few for x in p[:2]], R, D, W)
    return (layer_out, input_grad, query_grad, key_grad, value_grad, out_grad, extra[:, experts + 1], extra[:, experts],
            extra[:, :experts], gate_grad, up_grad, down_grad)


def solution(mesh):
    both = P(("dp", "expert"), None)
    dp = P("dp", None)
    own = P("expert", None, None)
    part = P("expert", "dp", None)
    return jax.shard_map(
        functools.partial(local, mesh.shape["dp"], mesh.shape["expert"]),
        mesh=mesh,
        in_specs=(both, both, both, both, dp, dp, dp, dp, P("dp"), P("dp"), dp, own, own, own),
        out_specs=(both, both, dp, dp, dp, dp, P("dp"), P("dp"), dp, part, part, part),
        check_vma=False,
    )
```

```python
import functools
import jax
import jax.numpy as jnp
from jax import lax
from jax.experimental import pallas as pl
from jax.experimental.pallas import tpu as pltpu
from jax.sharding import PartitionSpec as P

HEAD_SIZE = 64
EPSILON = 1e-06
ROTARY_BASE = 10000.0
SCORE_FACTOR = 0.015625
MANY = 4
F32=jnp.float32; BF=jnp.bfloat16
def dot_nn(a,b): return lax.dot_general(a,b,(((1,),(0,)),((),())),preferred_element_type=F32)
def dot_nt(a,b): return lax.dot_general(a,b,(((1,),(1,)),((),())),preferred_element_type=F32)

def column(table, lane):
    at = lax.broadcasted_iota(jnp.int32, table.shape, 1) == lane
    return jnp.sum(jnp.where(at, table, 0.0), axis=1, keepdims=True)

def expert_kernel(blocks, choices, where_ref, *refs):
    n2_refs, refs = refs[:blocks], refs[blocks:]
    pick_refs, refs = refs[:blocks], refs[blocks:]
    (router_ref, gate_ref, up_ref, raw_ref,
     rows_ref, gates_ref, n2t_ref, hid_ref, weighed_ref, grow_ref, urow_ref,
     n2, rows, aux_ref) = refs
    e = pl.program_id(0)
    own = where_ref[0]
    experts_here = pl.num_programs(0)
    T = n2_refs[0].shape[0]; W = n2_refs[0].shape[1]; H = gate_ref.shape[2]
    C = 512

    @pl.when(e == 0)
    def _():
        for b in range(blocks):
            n2[b * T:(b + 1) * T, :] = n2_refs[b][...]
            picks = pick_refs[b][...].astype(F32)
            logits = dot_nn(n2_refs[b][...], router_ref[...])
            lane = lax.broadcasted_iota(jnp.int32, logits.shape, 1)
            named = lane < 0
            for k in range(choices):
                named = named | (lane.astype(F32) == picks[:, k:k + 1])
            logits = jnp.where(named, logits, -1e30)
            top = jnp.max(logits, axis=1, keepdims=True)
            raised = jnp.where(named, jnp.exp(logits - top), 0.0)
            gates_ref[b * T:(b + 1) * T, :] = raised / jnp.sum(raised, axis=1, keepdims=True)
        aux_ref[...] = jnp.zeros_like(aux_ref)
        rows[...] = jnp.zeros_like(rows)

    mine = own * experts_here + e
    g = column(gates_ref[...], mine)
    gate_pre = dot_nn(n2[...], gate_ref[0])
    up_pre = dot_nn(n2[...], up_ref[0])
    raw_back = raw_ref[0]
    sig = 1.0 / (1.0 + jnp.exp(-gate_pre))
    silu = gate_pre * sig
    hidden = (silu * up_pre).astype(BF).astype(F32)
    back = jnp.sum(hidden * raw_back, axis=1, keepdims=True)
    weighed = (g * hidden).astype(BF)
    weighed_ref[0] = weighed
    hid_ref[0] = weighed.T
    part = pl.multiple_of(jnp.minimum(e, W // C - 1) * C, C)
    n2t_ref[pl.ds(part, C), :] = n2[:, pl.ds(part, C)].T
    lane = lax.broadcasted_iota(jnp.int32, aux_ref.shape, 1)
    aux_ref[...] = jnp.where(lane == mine, back, aux_ref[...])
    hid_back = g * raw_back
    grow = (hid_back * up_pre * (sig + silu * (1.0 - sig))).astype(BF)
    urow = (hid_back * silu).astype(BF)
    grow_ref[0] = grow
    urow_ref[0] = urow
    for j in range(W // C):
        cols = slice(j * C, (j + 1) * C)
        rows[:, cols] += dot_nt(grow, gate_ref[0, cols, :]) + dot_nt(urow, up_ref[0, cols, :])

    @pl.when(e == experts_here - 1)
    def _():
        hi = aux_ref[...].astype(BF).astype(F32)
        packed = (hi + pltpu.roll(aux_ref[...] - hi, 64, 1)).astype(BF)
        for b in range(blocks):
            part = slice(b * T, (b + 1) * T)
            rows_ref[own ^ b, :, :W] = rows[part, :].astype(BF)
            rows_ref[own ^ b, :, W:] = packed[part, :]


def expert_rows(where, n2s, payloads, choices, router, gate_w, up_w, raw):
    blocks = len(n2s)
    T, W = n2s[0].shape
    E, _, H = gate_w.shape
    A = blocks * T
    once = lambda s: pl.BlockSpec(s, lambda e, w: (0,) * len(s), pipeline_mode=pl.Buffered(1))
    whole = lambda s: pl.BlockSpec(s, lambda e, w: (0,) * len(s))
    per = lambda s: pl.BlockSpec((1,) + s, lambda e, w: (e,) + (0,) * len(s))
    S = jax.ShapeDtypeStruct
    return pl.pallas_call(
        functools.partial(expert_kernel, blocks, choices),
        out_shape=(S((blocks, T, W + 128), BF), S((A, 128), F32), S((W, A), BF),
                   S((E, H, A), BF), S((E, A, H), BF), S((E, A, H), BF), S((E, A, H), BF)),
        grid_spec=pltpu.PrefetchScalarGridSpec(
            num_scalar_prefetch=1, grid=(E,),
            in_specs=[once((T, W))] * blocks + [pl.BlockSpec((T, 128), lambda e, w: (0, W // 128), pipeline_mode=pl.Buffered(1))] * blocks
            + [once((W, 128)), per((W, H)), per((W, H)), per((A, H))],
            out_specs=[whole((blocks, T, W + 128)), whole((A, 128)), whole((W, A)),
                       per((H, A)), per((A, H)), per((A, H)), per((A, H))],
            scratch_shapes=[pltpu.VMEM((A, W), BF), pltpu.VMEM((A, W), F32), pltpu.VMEM((A, 128), F32)]),
        compiler_params=pltpu.CompilerParams(vmem_limit_bytes=60 << 20),
        cost_estimate=pl.CostEstimate(flops=8 * A * W * H * E, bytes_accessed=6 * E * W * H + 12 * A * W, transcendentals=A * H * E),
    )(where, *n2s, *payloads, router, gate_w, up_w, raw)


def grad_kernel(blocks, apart, where_ref, *refs):
    cot_refs, refs = refs[:blocks], refs[blocks:]
    n2t_ref, hid_ref, grow_ref, urow_ref, *outs = refs
    C = grow_ref.shape[2]
    W = n2t_ref.shape[0]
    H = hid_ref.shape[1]
    n_dp = outs[0].shape[0] * len(outs)
    R, D = W // n_dp, H // n_dp
    core = where_ref[1] % 2

    def store(value, rows):
        if not apart:
            outs[0][:, 0, rows, :] = value
            return
        for own in range(2):
            @pl.when(core == own)
            def _(own=own):
                for d in range(n_dp):
                    outs[(d % 2) ^ own][d // 2, 0, rows, :] = value[d]

    left = n2t_ref[...]
    store(dot_nn(left, grow_ref[0]).astype(BF).reshape(n_dp, R, C), slice(0, R))
    store(dot_nn(left, urow_ref[0]).astype(BF).reshape(n_dp, R, C), slice(R, 2 * R))
    for j in range(W // C):
        cot = jnp.concatenate([ref[:, j * C:(j + 1) * C] for ref in cot_refs], axis=0)
        store(dot_nn(hid_ref[0], cot).astype(BF).reshape(n_dp, D, C), slice(2 * R + j * D, 2 * R + (j + 1) * D))


def expert_grads(first, count, apart, where, cots, n2t, hid, grow, urow, n_dp):
    blocks = len(cots)
    T = cots[0].shape[0]
    W, A = n2t.shape
    _, _, H = grow.shape
    P_ = 2 * (W // n_dp) + (W // H) * (H // n_dp)
    shape = (n_dp // 2 if apart else n_dp, count, P_, H)
    once = lambda s: pl.BlockSpec(s, lambda e, w: (0,) * len(s), pipeline_mode=pl.Buffered(1))
    per = lambda s: pl.BlockSpec((1,) + s, lambda e, w: (e + first,) + (0,) * len(s))
    outs = 2 if apart else 1
    made = pl.pallas_call(
        functools.partial(grad_kernel, blocks, apart),
        out_shape=(jax.ShapeDtypeStruct(shape, BF),) * outs,
        grid_spec=pltpu.PrefetchScalarGridSpec(
            num_scalar_prefetch=1, grid=(count,),
            in_specs=[once((T, W))] * blocks + [once((W, A)), per((H, A)), per((A, H)), per((A, H))],
            out_specs=(pl.BlockSpec((shape[0], 1, P_, H), lambda e, w: (0, e, 0, 0)),) * outs),
        compiler_params=pltpu.CompilerParams(vmem_limit_bytes=60 << 20),
        cost_estimate=pl.CostEstimate(flops=0, bytes_accessed=0, transcendentals=0),
    )(where, *cots, n2t, hid, grow, urow)
    return made if apart else made[0]


def combine_kernel(weighed_ref, down_ref, keep_ref, send_ref, total):
    e = pl.program_id(0)
    half, T, _ = keep_ref.shape
    made = dot_nn(weighed_ref[0], down_ref[0])

    @pl.when(e == 0)
    def _():
        total[...] = made

    @pl.when(e > 0)
    def _():
        total[...] += made

    @pl.when(e == pl.num_programs(0) - 1)
    def _():
        for b in range(2 * half):
            out = send_ref if b % 2 else keep_ref
            out[b // 2] = total[b * T:(b + 1) * T, :].astype(BF)


def combine(weighed, down_w, blocks):
    E, A, H = weighed.shape
    W = down_w.shape[2]
    T = A // blocks
    per = lambda s: pl.BlockSpec((1,) + s, lambda e: (e,) + (0,) * len(s))
    out = pl.BlockSpec((blocks // 2, T, W), lambda e: (0, 0, 0))
    return pl.pallas_call(
        combine_kernel,
        out_shape=(jax.ShapeDtypeStruct((blocks // 2, T, W), BF),) * 2,
        grid=(E,),
        in_specs=[per((A, H)), per((H, W))],
        out_specs=(out, out),
        scratch_shapes=[pltpu.VMEM((A, W), F32)],
        compiler_params=pltpu.CompilerParams(vmem_limit_bytes=60 << 20),
        cost_estimate=pl.CostEstimate(flops=0, bytes_accessed=0, transcendentals=0),
    )(weighed, down_w)


def raw_kernel(blocks, *refs):
    payloads, (down_ref, out_ref, cot) = refs[:blocks], refs[blocks:]
    T = payloads[0].shape[0]

    @pl.when(pl.program_id(0) == 0)
    def _():
        for b in range(blocks):
            cot[b * T:(b + 1) * T, :] = payloads[b][...]

    out_ref[0] = dot_nt(cot[...], down_ref[0])


def raw_back(payloads, down_w):
    blocks = len(payloads)
    T = payloads[0].shape[0]
    E, H, W = down_w.shape
    A = blocks * T
    return pl.pallas_call(
        functools.partial(raw_kernel, blocks),
        grid=(E,),
        out_shape=jax.ShapeDtypeStruct((E, A, H), F32),
        in_specs=[pl.BlockSpec((T, W), lambda e: (0, 0), pipeline_mode=pl.Buffered(1))] * blocks
        + [pl.BlockSpec((1, H, W), lambda e: (e, 0, 0))],
        out_specs=pl.BlockSpec((1, A, H), lambda e: (e, 0, 0)),
        scratch_shapes=[pltpu.VMEM((A, W), BF)],
        compiler_params=pltpu.CompilerParams(vmem_limit_bytes=60 << 20),
        cost_estimate=pl.CostEstimate(flops=0, bytes_accessed=0, transcendentals=0),
    )(*payloads, down_w)


def normed_kernel(where_ref, gains_ref, *refs):
    payloads, out_ref = refs[:-1], refs[-1]
    T = payloads[0].shape[0]
    W = gains_ref.shape[1]
    _, half, R, _ = out_ref.shape
    for b, ref in enumerate(payloads):
        x = ref[:, W + 128:].astype(F32)
        inverse = lax.rsqrt(jnp.mean(x * x, axis=1, keepdims=True) + EPSILON)
        turned = (x * inverse * gains_ref[0:1, :]).astype(BF).T
        for d in range(2 * half):
            r = d ^ where_ref[1]
            out_ref[lax.rem(r, 2), lax.div(r, 2), :, b * T:(b + 1) * T] = turned[d * R:(d + 1) * R, :]


def normed_turned(where, gains, payloads, n_dp):
    T = payloads[0].shape[0]
    W = gains.shape[1]
    v = pl.BlockSpec(memory_space=pltpu.VMEM)
    return pl.pallas_call(
        normed_kernel,
        out_shape=jax.ShapeDtypeStruct((2, n_dp // 2, W // n_dp, len(payloads) * T), BF),
        in_specs=[pl.BlockSpec(memory_space=pltpu.SMEM)] + [v] * (1 + len(payloads)),
        out_specs=v,
        compiler_params=pltpu.CompilerParams(vmem_limit_bytes=40 << 20),
        cost_estimate=pl.CostEstimate(flops=0, bytes_accessed=0, transcendentals=0),
    )(where, gains, *payloads)


def rope_tile(x, cosine, sine):
    lane = lax.broadcasted_iota(jnp.int32, x.shape, 1)
    other = jnp.where(lax.rem(lane, 64) < 32, pltpu.roll(x, 96, 1), pltpu.roll(x, 32, 1))
    return x * cosine + other * sine


def half_mask(shape, half):
    lane = lax.broadcasted_iota(jnp.int32, shape, 1)
    return (lane < 64) if half == 0 else (lane >= 64)


def stacked(tiles, group, per, T):
    out = []
    for i in range(per):
        h = group * per + i
        x = tiles[h // 2]
        if h % 2 != group % 2:
            x = pltpu.roll(x, 64, 1)
        out.append(jnp.where(half_mask(x.shape, group % 2), x, 0.0).astype(BF))
    return jnp.concatenate(out, axis=0)


def unstacked(value, group, per, T, tiles):
    for i in range(per):
        h = group * per + i
        x = value[i * T:(i + 1) * T]
        if h % 2 != group % 2:
            x = pltpu.roll(x, 64, 1)
        x = jnp.where(half_mask(x.shape, h % 2), x, 0.0)
        tiles[h // 2] = x if tiles[h // 2] is None else tiles[h // 2] + x


def allowed(seg_row_ref, seg_col_ref, T, per):
    row = lax.broadcasted_iota(jnp.int32, (T, T), 0)
    col = lax.broadcasted_iota(jnp.int32, (T, T), 1)
    ok = (seg_col_ref[...] == seg_row_ref[...]) & (col <= row)
    bias = jnp.where(ok, 0.0, -1e30)
    return jnp.concatenate([bias] * per, axis=0)


def fetch(places, pieces, dev, dst, sems, at, lo, hi):
    R = pieces[0].shape[0]
    copies = []
    for i, ((r, col), piece) in enumerate(zip(places, pieces)):
        a, b = max(lo, col), min(hi, col + piece.shape[1])
        if a < b:
            row = pl.multiple_of((dev ^ r) * R, R)
            copies.append(pltpu.make_async_copy(
                piece.at[:, a - col:b - col], dst.at[pl.ds(row, R), a - lo:b - lo], sems.at[at + i]))
            copies[-1].start()
    return copies


def forward_kernel(places, kv, experts, dev_ref, tok_ref, cos_ref, sin_ref, segr_ref, segc_ref, q_hbm, *refs):
    pieces, refs = refs[:len(places)], refs[len(places):]
    qkv_ref, mix_ref, resid_ref, n2_ref, gains_ref, router_ref, kv_ref, wq, wo, sems = refs
    T, W = tok_ref.shape
    C = 512
    chunks = W // C
    fetched = fetch(places, pieces, dev_ref[1], wo, sems, chunks, 0, wo.shape[1])
    copies = []
    for j in range(chunks):
        copies.append(pltpu.make_async_copy(q_hbm.at[:, j * C:(j + 1) * C], wq.at[j], sems.at[j]))
        copies[-1].start()
    x = tok_ref[...].astype(F32)
    inverse = lax.rsqrt(jnp.mean(x * x, axis=1, keepdims=True) + EPSILON)
    for copy in fetched:
        copy.wait()
    keep = pltpu.make_async_copy(wo.at[:, :2 * kv], kv_ref, sems.at[chunks + len(places)])
    keep.start()
    small = wo[:, 2 * kv + W:]
    router_ref[...] = small
    turned = small.astype(F32).T
    gain1, gain2 = turned[experts:experts + 1, :], turned[experts + 1:experts + 2, :]
    gains_ref[0:1, :] = gain1
    gains_ref[1:2, :] = gain2
    gains_ref[2:8, :] = jnp.zeros((6, W), F32)
    n1 = (x * inverse * gain1).astype(BF)
    cosine, sine = cos_ref[...], sin_ref[...]
    q_tiles = W // 128
    k_tiles = kv // 128
    side = dot_nn(n1, wo[:, :2 * kv])
    others = [side[:, t * 128:(t + 1) * 128] for t in range(2 * k_tiles)]
    others = [rope_tile(t, cosine, sine).astype(BF) for t in others[:k_tiles]] + [t.astype(BF) for t in others[k_tiles:]]
    tiles = []
    for j in range(chunks):
        copies[j].wait()
        made = dot_nn(n1, wq[j])
        tiles += [rope_tile(made[:, t * 128:(t + 1) * 128], cosine, sine).astype(BF) for t in range(C // 128)]
    tiles += others
    for t, tile in enumerate(tiles):
        qkv_ref[:, t * 128:(t + 1) * 128] = tile
    per = q_tiles // k_tiles
    bias = allowed(segr_ref, segc_ref, T, per)
    q = [t.astype(F32) for t in tiles[:q_tiles]]
    mixed = [None] * q_tiles
    for g in range(2 * k_tiles):
        k_tile, v_tile = tiles[q_tiles + g // 2], tiles[q_tiles + k_tiles + g // 2]
        s = dot_nt(stacked(q, g, per, T), k_tile) * SCORE_FACTOR + bias
        raised = jnp.exp(s - jnp.max(s, axis=1, keepdims=True))
        p = raised / jnp.sum(raised, axis=1, keepdims=True)
        unstacked(dot_nn(p.astype(BF), v_tile), g, per, T, mixed)
    for t in range(q_tiles):
        mix_ref[:, t * 128:(t + 1) * 128] = mixed[t].astype(BF)
    total = jnp.zeros((T, 1), F32)
    for j in range(chunks):
        cols = slice(j * C, (j + 1) * C)
        r = tok_ref[:, cols].astype(F32) + dot_nn(mix_ref[...], wo[:, 2 * kv + j * C:2 * kv + (j + 1) * C])
        resid_ref[:, cols] = r
        total = total + jnp.sum(r * r, axis=1, keepdims=True)
    inverse = lax.rsqrt(total / W + EPSILON)
    n2_ref[...] = (resid_ref[...] * inverse * gain2).astype(BF)
    keep.wait()


def forward(where, tokens, cosine, sine, segr, segc, q_w, pieces, places, kv, experts):
    T, W = tokens.shape
    N = W + 2 * kv
    S = jax.ShapeDtypeStruct
    v = pl.BlockSpec(memory_space=pltpu.VMEM)
    hbm = pl.BlockSpec(memory_space=pl.ANY)
    return pl.pallas_call(
        functools.partial(forward_kernel, places, kv, experts),
        out_shape=(S((T, N), BF), S((T, W), BF), S((T, W), F32), S((T, W), BF), S((8, W), F32), S((W, 128), BF), S((W, 2 * kv), BF)),
        in_specs=[pl.BlockSpec(memory_space=pltpu.SMEM)] + [v] * 5 + [hbm] * (1 + len(places)),
        out_specs=(v,) * 6 + (hbm,),
        scratch_shapes=[pltpu.VMEM((W // 512, W, 512), BF), pltpu.VMEM((W, N + 128), BF),
                        pltpu.SemaphoreType.DMA((W // 512 + len(places) + 1,))],
        compiler_params=pltpu.CompilerParams(vmem_limit_bytes=60 << 20),
        cost_estimate=pl.CostEstimate(flops=0, bytes_accessed=0, transcendentals=0),
    )(where, tokens, cosine, sine, segr, segc, q_w, *pieces)


def split(x):
    hi = x.astype(BF)
    return hi, (x - hi.astype(F32)).astype(BF)


def dot_tn(a, b): return lax.dot_general(a, b, (((0,), (0,)), ((), ())), preferred_element_type=F32)


def ones_at(T, lane):
    return jnp.where(lax.broadcasted_iota(jnp.int32, (T, 128), 1) == lane, 1.0, 0.0).astype(BF)


def middle_kernel(experts, *refs):
    (rows_ref, gates_ref, router_ref, n2_ref, resid_ref, g2_ref, cot_ref, att_ref, cut_ref, back_ref, extra_ref) = refs
    T, W = n2_ref.shape
    total = rows_ref[0].astype(F32)
    for b in range(1, rows_ref.shape[0]):
        total = total + rows_ref[b].astype(F32)
    aux = total[:, W:]
    gate_back = aux + pltpu.roll(aux, 64, 1)
    gates = gates_ref[...]
    hi, lo = split(gates * (gate_back - jnp.sum(gates * gate_back, axis=1, keepdims=True)))
    n2_back = total[:, :W] + dot_nt(hi, router_ref[...]) + dot_nt(lo, router_ref[...])
    resid = resid_ref[...]
    inverse = lax.rsqrt(jnp.mean(resid * resid, axis=1, keepdims=True) + EPSILON)
    scaled = n2_back * g2_ref[1:2, :]
    inner = jnp.mean(scaled * resid, axis=1, keepdims=True)
    back = cot_ref[...].astype(F32) + inverse * scaled - resid * (inverse * inverse * inverse * inner)
    back_ref[...] = back
    att_ref[...] = back.astype(BF)
    width = cut_ref.shape[2]
    for b in range(cut_ref.shape[0]):
        cut_ref[b] = back[:, b * width:(b + 1) * width].astype(BF)
    p_hi, p_lo = split(n2_back * resid * inverse)
    one = ones_at(T, experts)
    extra_ref[...] = dot_tn(n2_ref[...], hi) + dot_tn(n2_ref[...], lo) + dot_tn(p_hi, one) + dot_tn(p_lo, one)


def middle(rows_in, gates, router, n2, resid, gain2, cot, experts):
    T, W = n2.shape
    blocks = rows_in.shape[0]
    S = jax.ShapeDtypeStruct
    v = lambda s: pl.BlockSpec(s, lambda i: (0, 0))
    return pl.pallas_call(
        functools.partial(middle_kernel, experts),
        grid=(1,),
        out_shape=(S((T, W), BF), S((blocks, T, W // blocks), BF), S((T, W), F32), S((W, 128), F32)),
        in_specs=[pl.BlockSpec((blocks, T, W + 128), lambda i: (0, 0, 0)), v((T, 128)), v((W, 128)), v((T, W)), v((T, W)), v((8, W)), v((T, W))],
        out_specs=(v((T, W)), pl.BlockSpec((blocks, T, W // blocks), lambda i: (0, 0, 0)), v((T, W)), v((W, 128))),
        compiler_params=pltpu.CompilerParams(vmem_limit_bytes=40 << 20),
        cost_estimate=pl.CostEstimate(flops=400_000_000_000, bytes_accessed=30 * T * W, transcendentals=T),
    )(rows_in, gates, router, n2, resid, gain2, cot)


def backward_kernel(places, dev_ref, att_ref, qkv_ref, cos_ref, sin_ref, segr_ref, segc_ref, *refs):
    outs, refs = refs[:len(places)], refs[len(places):]
    back_ref, cut_ref, wo, sems = refs
    T, W = att_ref.shape
    fetched = fetch(places, outs, dev_ref[1], wo, sems, 0, qkv_ref.shape[1] - W, qkv_ref.shape[1])
    q_tiles = W // 128
    k_tiles = (qkv_ref.shape[1] - W) // 256
    per = q_tiles // k_tiles
    tile = lambda t: qkv_ref[:, t * 128:(t + 1) * 128]
    q = [tile(t).astype(F32) for t in range(q_tiles)]
    bias = allowed(segr_ref, segc_ref, T, per)
    cosine, sine = cos_ref[...], -sin_ref[...]
    for copy in fetched:
        copy.wait()
    mixed_back = []
    for j in range(W // 512):
        made = dot_nt(att_ref[...], wo[j * 512:(j + 1) * 512, :]).astype(BF).astype(F32)
        mixed_back += [made[:, t * 128:(t + 1) * 128] for t in range(4)]
    q_back = [None] * q_tiles
    k_back = [None] * k_tiles
    v_back = [None] * k_tiles
    for g in range(2 * k_tiles):
        k_tile, v_tile = tile(q_tiles + g // 2), tile(q_tiles + k_tiles + g // 2)
        qs = stacked(q, g, per, T)
        ms = stacked(mixed_back, g, per, T)
        s = dot_nt(qs, k_tile) * SCORE_FACTOR + bias
        raised = jnp.exp(s - jnp.max(s, axis=1, keepdims=True))
        p = raised / jnp.sum(raised, axis=1, keepdims=True)
        dp = dot_nt(ms, v_tile)
        ds = (p * (dp - jnp.sum(p * dp, axis=1, keepdims=True)) * SCORE_FACTOR).astype(BF)
        unstacked(dot_nn(ds, k_tile), g, per, T, q_back)
        kb, vb = dot_tn(ds, qs), dot_tn(p.astype(BF), ms)
        k_back[g // 2] = kb if g % 2 == 0 else k_back[g // 2] + kb
        v_back[g // 2] = vb if g % 2 == 0 else v_back[g // 2] + vb
    made = [rope_tile(t, cosine, sine) for t in q_back + k_back] + v_back
    for t, value in enumerate(made):
        back_ref[:, t * 128:(t + 1) * 128] = value.astype(BF)
        of, place = (q_tiles, t) if t < q_tiles else (k_tiles, (t - q_tiles) % k_tiles)
        each = of // cut_ref.shape[0]
        at = place % each * 128 + (0 if t < q_tiles else (q_tiles + (k_tiles if t >= q_tiles + k_tiles else 0)) // cut_ref.shape[0] * 128)
        cut_ref[place // each, :, at:at + 128] = value.astype(BF)


def backward(where, att, qkv, cosine, sine, segr, segc, outs, places, ne):
    T, W = att.shape
    N = qkv.shape[1]
    S = jax.ShapeDtypeStruct
    v = pl.BlockSpec(memory_space=pltpu.VMEM)
    hbm = pl.BlockSpec(memory_space=pl.ANY)
    return pl.pallas_call(
        functools.partial(backward_kernel, places),
        out_shape=(S((T, N), BF), S((ne, T, N // ne), BF)),
        in_specs=[pl.BlockSpec(memory_space=pltpu.SMEM)] + [v] * 6 + [hbm] * len(places),
        out_specs=(v, v),
        scratch_shapes=[pltpu.VMEM((W, W), BF), pltpu.SemaphoreType.DMA((len(places),))],
        compiler_params=pltpu.CompilerParams(vmem_limit_bytes=60 << 20),
        cost_estimate=pl.CostEstimate(flops=0, bytes_accessed=0, transcendentals=0),
    )(where, att, qkv, cosine, sine, segr, segc, *outs)


def last_kernel(experts, back_ref, tok_ref, g1_ref, resid_back_ref, extra_ref, q_ref, kv_ref, grad_ref, more_ref, nb):
    j = pl.program_id(0)
    T, W = tok_ref.shape
    C = q_ref.shape[0]
    nb[j] = dot_nt(back_ref[:, :W], q_ref[...]) + dot_nt(back_ref[:, W:], kv_ref[...])

    @pl.when(j == pl.num_programs(0) - 1)
    def _():
        x = tok_ref[...].astype(F32)
        inverse = lax.rsqrt(jnp.mean(x * x, axis=1, keepdims=True) + EPSILON)
        n1_back = jnp.concatenate([nb[i] for i in range(W // C)], axis=1)
        scaled = n1_back * g1_ref[0:1, :]
        inner = jnp.mean(scaled * x, axis=1, keepdims=True)
        grad_ref[...] = resid_back_ref[...] + inverse * scaled - x * (inverse * inverse * inverse * inner)
        p_hi, p_lo = split(n1_back * x * inverse)
        one = ones_at(T, experts + 1)
        more_ref[...] = extra_ref[...] + dot_tn(p_hi, one) + dot_tn(p_lo, one)


def last(back, tokens, gains, resid_back, extra, q_w, kv_w, experts):
    T, W = tokens.shape
    N = back.shape[1]
    C = 512
    S = jax.ShapeDtypeStruct
    v = lambda s: pl.BlockSpec(s, lambda j: (0, 0))
    return pl.pallas_call(
        functools.partial(last_kernel, experts),
        grid=(W // C,),
        out_shape=(S((T, W), F32), S((W, 128), F32)),
        in_specs=[v((T, N)), v((T, W)), v((8, W)), v((T, W)), v((W, 128)), pl.BlockSpec((C, W), lambda j: (j, 0)),
                  pl.BlockSpec((C, N - W), lambda j: (j, 0))],
        out_specs=(v((T, W)), v((W, 128))),
        scratch_shapes=[pltpu.VMEM((W // C, T, C), F32)],
        compiler_params=pltpu.CompilerParams(vmem_limit_bytes=40 << 20),
        cost_estimate=pl.CostEstimate(flops=0, bytes_accessed=0, transcendentals=0),
    )(back, tokens, gains, resid_back, extra, q_w, kv_w)


def out_grad_kernel(blocks, where_ref, *refs):
    mix_refs, (att_ref, keep_ref, send_ref, left) = refs[:blocks], refs[blocks:]
    own, dev = where_ref[0], where_ref[1]
    T = mix_refs[0].shape[0]
    half, _, R, C = keep_ref.shape
    for b in range(blocks):
        turned = mix_refs[b][...].T
        for d in range(2 * half):
            r = d ^ dev
            left[lax.rem(r, 2), lax.div(r, 2), :, b * T:(b + 1) * T] = turned[d * R:(d + 1) * R, :]
    right = jnp.concatenate([att_ref[own ^ b] for b in range(blocks)], axis=0)
    for s, out in ((1, send_ref), (0, keep_ref)):
        out[:, 0] = dot_nn(left[s].reshape(half * R, blocks * T), right).astype(BF).reshape(half, R, C)


def out_grads(where, mixs, att_cut, n_dp):
    blocks = len(mixs)
    T, W = mixs[0].shape
    C = att_cut.shape[2]
    R = W // n_dp
    S = jax.ShapeDtypeStruct
    v = pl.BlockSpec(memory_space=pltpu.VMEM)
    return pl.pallas_call(
        functools.partial(out_grad_kernel, blocks),
        out_shape=(S((n_dp // 2, 1, R, C), BF),) * 2,
        in_specs=[pl.BlockSpec(memory_space=pltpu.SMEM)] + [v] * (blocks + 1),
        out_specs=(v, v),
        scratch_shapes=[pltpu.VMEM((2, n_dp // 2, R, blocks * T), BF)],
        compiler_params=pltpu.CompilerParams(vmem_limit_bytes=60 << 20),
        cost_estimate=pl.CostEstimate(flops=0, bytes_accessed=0, transcendentals=0),
    )(where, *mixs, att_cut)


def qkv_grad_kernel(where_ref, left_ref, qkv_ref, extra_ref, keep_ref, send_ref):
    own, dev = where_ref[0], where_ref[1]
    blocks, _, width = qkv_ref.shape
    half, _, R, C = keep_ref.shape
    right = jnp.concatenate([qkv_ref[own ^ b] for b in range(blocks)], axis=0)
    for s, out in ((1, send_ref), (0, keep_ref)):
        left = left_ref[s].reshape(half * R, left_ref.shape[3])
        out[:, 0, :, :width] = dot_nn(left, right).astype(BF).reshape(half, R, width)
    for d in range(2 * half):
        more = extra_ref[d * R:(d + 1) * R, :].astype(BF)
        r = d ^ dev

        @pl.when(lax.rem(r, 2) == 0)
        def _(more=more, r=r):
            keep_ref[lax.div(r, 2), 0, :, width:] = more

        @pl.when(lax.rem(r, 2) == 1)
        def _(more=more, r=r):
            send_ref[lax.div(r, 2), 0, :, width:] = more


def qkv_grads(where, left, qkv_cut, extra, n_dp):
    W = extra.shape[0]
    C = qkv_cut.shape[2] + 128
    R = W // n_dp
    S = jax.ShapeDtypeStruct
    v = pl.BlockSpec(memory_space=pltpu.VMEM)
    return pl.pallas_call(
        qkv_grad_kernel,
        out_shape=(S((n_dp // 2, 1, R, C), BF),) * 2,
        in_specs=[pl.BlockSpec(memory_space=pltpu.SMEM)] + [v] * 3,
        out_specs=(v, v),
        compiler_params=pltpu.CompilerParams(vmem_limit_bytes=60 << 20),
        cost_estimate=pl.CostEstimate(flops=2 * W * C * left.shape[3], bytes_accessed=4 * W * C, transcendentals=0),
    )(where, left, qkv_cut, extra)


def flip(x, axis, mask, size):
    return lax.ppermute(x, axis, [(i, i ^ mask) for i in range(size)])


def add(a, b):
    return (a.astype(F32) + b.astype(F32)).astype(BF)


def split_kernel(width, where_ref, *refs):
    ins, (a_keep, a_send, b_keep, b_send) = refs[:-4], refs[-4:]
    count = ins[0].shape[-4]
    for q in range(count):
        at = q ^ where_ref[0]
        sums = [(ins[i][at, 0].astype(F32) + ins[i + 1][at, 0].astype(F32)).astype(BF) for i in range(0, len(ins), 2)]
        total = sums[0] if len(sums) == 1 else jnp.concatenate(sums, axis=1)
        out = a_send if q % 2 else a_keep
        out[q // 2, 0] = total[:, :width]
        out = b_send if q >= count // 2 else b_keep
        out[q % (count // 2), 0] = total[:, width:]


def halves(pairs, n_dp, order=None):
    bits = n_dp.bit_length() - 1
    count, group, rows, _ = pairs[0][1].shape
    cols = sum(theirs.shape[3] for _, theirs in pairs)
    a = cols // 256 * 128
    S = jax.ShapeDtypeStruct
    if order is None:
        order = jnp.zeros((1,), jnp.int32)
    specs = []
    for keep, theirs in pairs:
        shape = (count, 1, rows, theirs.shape[3])
        specs += [pl.BlockSpec(shape, lambda g, w: (0, g, 0, 0))] * 2
    widths = (a, a, cols - a, cols - a)
    outs = pl.pallas_call(
        functools.partial(split_kernel, a),
        out_shape=tuple(S((count // 2, group, rows, c), BF) for c in widths),
        grid_spec=pltpu.PrefetchScalarGridSpec(
            num_scalar_prefetch=1, grid=(group,), in_specs=specs,
            out_specs=tuple(pl.BlockSpec((count // 2, 1, rows, c), lambda g, w: (0, g, 0, 0)) for c in widths)),
        compiler_params=pltpu.CompilerParams(vmem_limit_bytes=40 << 20),
        cost_estimate=pl.CostEstimate(flops=0, bytes_accessed=0, transcendentals=0),
    )(order.astype(jnp.int32), *[x for pair in pairs for x in pair])
    left = tuple(range(bits - 1, 0, -1))
    shaped = lambda x: x.reshape((2,) * (bits - 2) + x.shape[1:])
    return [(shaped(outs[0]), shaped(outs[1]), left[:-1], tuple(range(1, bits))),
            (shaped(outs[2]), shaped(outs[3]), left[1:], left)]


def halve(parts, n_dp):
    done = []
    for mine, sent, left, order in parts:
        theirs = flip(sent, "dp", 1 << order[0], n_dp)
        if left:
            total = add(mine, theirs)
            axis = left.index(order[1])
            mine, theirs = (lax.index_in_dim(total, i, axis, keepdims=False) for i in (0, 1))
        done.append((mine, theirs, tuple(b for b in left if b != order[1]) if left else (), order[1:]))
    return done


def finish(parts, n_dp):
    while parts[0][3]:
        parts = halve(parts, n_dp)
    return parts


def tie_parts(parts, *others):
    arrays, others = lax.optimization_barrier(([p[:2] for p in parts], others))
    return [tuple(a) + p[2:] for a, p in zip(arrays, parts)], *others


def unpack_kernel(many, in_ref, *refs):
    parts, (gate_ref, up_ref, down_ref) = refs[:-3], refs[-3:]
    R, D = gate_ref.shape[1], down_ref.shape[1]
    H = gate_ref.shape[2]

    def store(total, at):
        width = total.shape[1]
        gate_ref[0, :, at:at + width] = total[:R]
        up_ref[0, :, at:at + width] = total[R:2 * R]
        for j in range(down_ref.shape[2] // H):
            down_ref[0, :, j * H + at:j * H + at + width] = total[2 * R + j * D:2 * R + (j + 1) * D]

    @pl.when(pl.program_id(0) < many)
    def _():
        store(in_ref[0, 0].astype(F32), 0)

    @pl.when(pl.program_id(0) >= many)
    def _():
        at = 0
        for mine, theirs in (parts[:2], parts[2:]):
            store(mine[0].astype(F32) + theirs[0].astype(F32), at)
            at += mine.shape[2]


def unpack(packed, parts, R, D, W):
    _, many, rows, H = packed.shape
    E = many + parts[0].shape[0]
    S = jax.ShapeDtypeStruct
    out = lambda a, b: pl.BlockSpec((1, a, b), lambda e: (e, 0, 0))
    return pl.pallas_call(
        functools.partial(unpack_kernel, many),
        grid=(E,),
        out_shape=(S((E, R, H), F32), S((E, R, H), F32), S((E, D, W), F32)),
        in_specs=[pl.BlockSpec((1, 1, rows, H), lambda e: (0, jnp.minimum(e, many - 1), 0, 0))]
        + [pl.BlockSpec((1, rows, x.shape[2]), lambda e: (jnp.maximum(e - many, 0), 0, 0)) for x in parts],
        out_specs=(out(R, H), out(R, H), out(D, W)),
        compiler_params=pltpu.CompilerParams(vmem_limit_bytes=40 << 20),
        cost_estimate=pl.CostEstimate(flops=3 * E * R * H, bytes_accessed=18 * E * R * H, transcendentals=0),
    )(packed, *parts)


def spread_kernel(kv, where_ref, *refs):
    parts, (q_ref, k_ref, v_ref, o_ref, extra_ref) = refs[:-5], refs[-5:]
    blocks = len(parts)
    wide, narrow = q_ref.shape[1] // blocks, kv // blocks
    extra = None
    for b, ref in enumerate(parts):
        at = where_ref[0] ^ b
        col = 0
        for out, width in ((o_ref, wide), (q_ref, wide), (k_ref, narrow), (v_ref, narrow)):
            out[:, pl.ds(pl.multiple_of(at * width, width), width)] = ref[:, col:col + width].astype(F32)
            col += width
        more = ref[:, col:].astype(F32)
        extra = more if extra is None else extra + more
    extra_ref[...] = extra


def spread(where, parts, W, kv):
    R, C = parts[0].shape
    S = jax.ShapeDtypeStruct
    v = pl.BlockSpec(memory_space=pltpu.VMEM)
    return pl.pallas_call(
        functools.partial(spread_kernel, kv),
        out_shape=(S((R, W), F32), S((R, kv), F32), S((R, kv), F32), S((R, W), F32), S((R, 128), F32)),
        in_specs=[pl.BlockSpec(memory_space=pltpu.SMEM)] + [v] * len(parts),
        out_specs=(v,) * 5,
        compiler_params=pltpu.CompilerParams(vmem_limit_bytes=40 << 20),
        cost_estimate=pl.CostEstimate(flops=R * C, bytes_accessed=24 * R * C, transcendentals=0),
    )(where, *parts)


def begin_z(x, ne):
    found = {0: x}
    bit = 1
    while bit < ne:
        found[bit] = flip(x, "expert", bit, ne)
        bit *= 2
    return found


def end_z(found, ne):
    for k in range(ne):
        if k not in found:
            found[k] = flip(found[k & (k - 1)], "expert", k & -k, ne)
    return [found[k] for k in range(ne)]


def gather_z(x, ne):
    return end_z(begin_z(x, ne), ne)


def gather_dp(w, n_dp, ready):
    half = w.shape[1] // 256 * 128
    found = {(0, 0): w[:, :half], (0, half): w[:, half:]}
    whole = {0: w}
    bits = range(1, n_dp.bit_length() - 1)
    for bit in bits:
        whole[1 << bit] = flip(w, "dp", 1 << bit, n_dp)
    whole, ready = lax.optimization_barrier((whole, ready))
    for bit in bits:
        r = 1 << bit
        found[r, 0], found[r, half] = whole[r][:, :half], whole[r][:, half:]
    for r in range(2, n_dp, 2):
        low, high = r & -r, 1 << (r.bit_length() - 1)
        if low != high:
            found[r, 0] = flip(found[r ^ high, 0], "dp", high, n_dp)
            found[r, half] = flip(found[r ^ low, half], "dp", low, n_dp)
    pieces = {}
    for (r, col), x in found.items():
        if r in whole:
            pieces[r, 0] = whole[r]
        else:
            pieces[r, col] = x
    for (r, col), x in list(pieces.items()):
        pieces[r ^ 1, col] = flip(x, "dp", 1, n_dp)
    places = sorted(pieces)
    return tuple(places), [pieces[p] for p in places], ready


def local(n_dp, ne, tokens, segment_ids, routes, cotangent, query_weight, key_weight, value_matrix, out_weight,
          first_gain, second_gain, router_weight, gate_weight, up_weight, down_weight):
    d = lax.axis_index("dp")
    z = lax.axis_index("expert")
    tie = lax.optimization_barrier
    T, W = tokens.shape
    experts = router_weight.shape[1]
    E, _, H = gate_weight.shape
    R = W // n_dp
    D = H // n_dp
    KV = key_weight.shape[1]
    where = jnp.stack([z, d, jnp.int32(E), jnp.int32(0)]).astype(jnp.int32)

    q_full = lax.all_gather(query_weight, "dp", axis=0, tiled=True)
    side = jnp.concatenate([key_weight, value_matrix, out_weight, router_weight, first_gain[:, None], second_gain[:, None],
                            jnp.zeros((R, 126 - experts), BF)], axis=1)
    segments = segment_ids[0]
    segr, segc = segments[None, :], segments[:, None]
    positions = jnp.arange(T, dtype=jnp.int32) - jnp.sum((segr < segc).astype(jnp.int32), axis=1)
    half = HEAD_SIZE // 2
    freq = ROTARY_BASE ** (-jnp.arange(half, dtype=F32) * 2.0 / HEAD_SIZE)
    angle = positions.astype(F32)[:, None] * freq[None, :]
    cosine = jnp.tile(jnp.cos(angle), (1, 4))
    sine = jnp.sin(angle)
    sine = jnp.concatenate([-sine, sine, -sine, sine], axis=1)
    choices = routes.shape[1]
    payload = jnp.concatenate([cotangent, jnp.pad(routes.astype(BF), ((0, 0), (0, 128 - choices))), tokens], axis=1)
    places, pieces, (cosine, sine, segc, where) = gather_dp(side, n_dp, (cosine, sine, segc, where))
    payloads = gather_z(payload, ne)
    core = lambda x: flip(x, "dp", 1, n_dp)
    exchange = lambda x: lax.all_to_all(x, "expert", split_axis=0, concat_axis=0, tiled=True)
    payloads, pieces, q_full = tie((payloads, pieces, q_full))
    qkv, mixed, resid, normed2, gains, router, kv_full = forward(
        where, tokens, cosine, sine, segr, segc, q_full, pieces, places, KV, experts)
    raw = raw_back(payloads, down_weight)
    n1t = normed_turned(where, gains, payloads, n_dp)
    n2s, raw, n1t = tie((begin_z(normed2, ne), raw, n1t))
    n2s, mixed = tie((end_z(n2s, ne), mixed))
    mixs = begin_z(mixed, ne)
    made = expert_rows(where, n2s, payloads, choices, router, gate_weight, up_weight, raw)
    made, mixs = tie((made, mixs))
    rows, gates, n2t, hid, weighed, grow, urow = made
    rows = exchange(rows)
    partial = expert_grads(0, MANY, False, where, payloads, n2t, hid, grow, urow, n_dp)
    packed = lax.psum_scatter(partial, "dp", scatter_dimension=0, tiled=True)
    partial, n2t, weighed = tie((partial, n2t, weighed))
    few, away = expert_grads(MANY, E - MANY, True, where, payloads, n2t, hid, grow, urow, n_dp)
    comb, comb_away = combine(weighed, down_weight, ne)
    rows, few, away, comb, comb_away, mixs = tie((rows, few, away, comb, comb_away, mixs))
    mixs = end_z(mixs, ne)
    comb_in = flip(comb_away, "expert", 1, ne)
    theirs = core(away)
    attended, att_cut, resid_back, extra = middle(rows, gates, router, normed2, resid, gains, cotangent, experts)
    att_cut = exchange(att_cut)
    back, back_cut = backward(where, attended, qkv, cosine, sine, segr, segc, pieces, places, ne)
    att_cut, back, back_cut, few, theirs, comb_in = tie((att_cut, back, back_cut, few, theirs, comb_in))
    back_cut = exchange(back_cut)
    few = halves([(few, theirs)], n_dp, (d // 2).reshape(1))
    input_grad, extra = last(back, tokens, gains, resid_back, extra, q_full, kv_full, experts)
    keep4, send4 = out_grads(where, mixs, att_cut, n_dp)
    comb = comb.astype(F32) + comb_in.astype(F32)
    comb, comb_far = comb[0], comb[1:].astype(BF)
    few, back_cut, extra, keep4, send4, comb_far = tie_parts(few, back_cut, extra, keep4, send4, comb_far)
    comb_far = [flip(comb_far[i], "expert", 2 * (i + 1), ne) for i in range(ne // 2 - 1)]
    theirs4 = core(send4)
    keep5, send5 = qkv_grads(where, n1t, back_cut, extra, n_dp)
    keep5, send5, theirs4 = tie((keep5, send5, theirs4))
    five = halve(halves([(keep4, theirs4), (keep5, core(send5))], n_dp), n_dp)
    five, comb_far = tie_parts(five, comb_far)
    five = finish(five, n_dp)
    part = jnp.concatenate([mine.astype(F32) + theirs.astype(F32) for mine, theirs, *_ in five], axis=-1)[0].astype(BF)
    few, part = tie_parts(few, part)
    parts = begin_z(part, ne)
    few, parts = tie_parts(halve(few, n_dp), parts)
    parts = end_z(parts, ne)
    few = finish(few, n_dp)
    made = unpack(packed, [x for p in few for x in p[:2]], R, D, W)
    parts, (gate_grad, up_grad, down_grad) = tie((parts, made))
    query_grad, key_grad, value_grad, out_grad, extra = spread(where, parts, W, KV)
    layer_out = (resid + comb + sum(x.astype(F32) for x in comb_far)).astype(BF)
    return (layer_out, input_grad, query_grad, key_grad, value_grad, out_grad, extra[:, experts + 1], extra[:, experts],
            extra[:, :experts], gate_grad, up_grad, down_grad)


def solution(mesh):
    both = P(("dp", "expert"), None)
    dp = P("dp", None)
    own = P("expert", None, None)
    part = P("expert", "dp", None)
    return jax.shard_map(
        functools.partial(local, mesh.shape["dp"], mesh.shape["expert"]),
        mesh=mesh,
        in_specs=(both, both, both, both, dp, dp, dp, dp, P("dp"), P("dp"), dp, own, own, own),
        out_specs=(both, both, dp, dp, dp, dp, P("dp"), P("dp"), dp, part, part, part),
        check_vma=False,
    )
```

```python
import functools
import jax
import jax.numpy as jnp
from jax import lax
from jax.experimental import pallas as pl
from jax.experimental.pallas import tpu as pltpu
from jax.sharding import PartitionSpec as P

HEAD_SIZE = 64
EPSILON = 1e-06
ROTARY_BASE = 10000.0
SCORE_FACTOR = 0.015625
MANY = 4
F32=jnp.float32; BF=jnp.bfloat16
def dot_nn(a,b): return lax.dot_general(a,b,(((1,),(0,)),((),())),preferred_element_type=F32)
def dot_nt(a,b): return lax.dot_general(a,b,(((1,),(1,)),((),())),preferred_element_type=F32)

def column(table, lane):
    at = lax.broadcasted_iota(jnp.int32, table.shape, 1) == lane
    return jnp.sum(jnp.where(at, table, 0.0), axis=1, keepdims=True)

def expert_kernel(blocks, choices, where_ref, *refs):
    n2_refs, refs = refs[:blocks], refs[blocks:]
    pick_refs, refs = refs[:blocks], refs[blocks:]
    (router_ref, gate_ref, up_ref, raw_ref,
     rows_ref, gates_ref, n2t_ref, hid_ref, weighed_ref, grow_ref, urow_ref,
     n2, rows, aux_ref) = refs
    e = pl.program_id(0)
    own = where_ref[0]
    experts_here = pl.num_programs(0)
    T = n2_refs[0].shape[0]; W = n2_refs[0].shape[1]; H = gate_ref.shape[2]
    C = 512

    @pl.when(e == 0)
    def _():
        for b in range(blocks):
            n2[b * T:(b + 1) * T, :] = n2_refs[b][...]
            picks = pick_refs[b][...].astype(F32)
            logits = dot_nn(n2_refs[b][...], router_ref[...])
            lane = lax.broadcasted_iota(jnp.int32, logits.shape, 1)
            named = lane < 0
            for k in range(choices):
                named = named | (lane.astype(F32) == picks[:, k:k + 1])
            logits = jnp.where(named, logits, -1e30)
            top = jnp.max(logits, axis=1, keepdims=True)
            raised = jnp.where(named, jnp.exp(logits - top), 0.0)
            gates_ref[b * T:(b + 1) * T, :] = raised / jnp.sum(raised, axis=1, keepdims=True)
        aux_ref[...] = jnp.zeros_like(aux_ref)
        rows[...] = jnp.zeros_like(rows)

    mine = own * experts_here + e
    g = column(gates_ref[...], mine)
    sides = [slice(h * (H // 2), (h + 1) * (H // 2)) for h in range(2)]
    pres = [(dot_nn(n2[...], gate_ref[0, :, s]), dot_nn(n2[...], up_ref[0, :, s])) for s in sides]
    back = jnp.zeros((blocks * T, 1), F32)
    for s, (gate_pre, up_pre) in zip(sides, pres):
        raw = raw_ref[0, :, s]
        sig = 0.5 * jnp.tanh(0.5 * gate_pre) + 0.5
        silu = gate_pre * sig
        hidden = (silu * up_pre).astype(BF).astype(F32)
        back = back + jnp.sum(hidden * raw, axis=1, keepdims=True)
        weighed = (g * hidden).astype(BF)
        weighed_ref[0, :, s] = weighed
        hid_ref[0, s, :] = weighed.T
        hid_back = g * raw
        grow = (hid_back * up_pre * (sig + silu * (1.0 - sig))).astype(BF)
        urow = (hid_back * silu).astype(BF)
        grow_ref[0, :, s] = grow
        urow_ref[0, :, s] = urow
    lane = lax.broadcasted_iota(jnp.int32, aux_ref.shape, 1)
    aux_ref[...] = jnp.where(lane == mine, back, aux_ref[...])
    part = pl.multiple_of(jnp.minimum(e, W // C - 1) * C, C)
    n2t_ref[pl.ds(part, C), :] = n2[:, pl.ds(part, C)].T
    for j in range(W // C):
        cols = slice(j * C, (j + 1) * C)
        rows[:, cols] += dot_nt(grow_ref[0], gate_ref[0, cols, :]) + dot_nt(urow_ref[0], up_ref[0, cols, :])

    @pl.when(e == experts_here - 1)
    def _():
        hi = aux_ref[...].astype(BF).astype(F32)
        packed = (hi + pltpu.roll(aux_ref[...] - hi, 64, 1)).astype(BF)
        for b in range(blocks):
            part = slice(b * T, (b + 1) * T)
            rows_ref[own ^ b, :, :W] = rows[part, :].astype(BF)
            rows_ref[own ^ b, :, W:] = packed[part, :]


def expert_rows(where, n2s, payloads, choices, router, gate_w, up_w, raw):
    blocks = len(n2s)
    T, W = n2s[0].shape
    E, _, H = gate_w.shape
    A = blocks * T
    once = lambda s: pl.BlockSpec(s, lambda e, w: (0,) * len(s), pipeline_mode=pl.Buffered(1))
    whole = lambda s: pl.BlockSpec(s, lambda e, w: (0,) * len(s))
    per = lambda s: pl.BlockSpec((1,) + s, lambda e, w: (e,) + (0,) * len(s))
    S = jax.ShapeDtypeStruct
    return pl.pallas_call(
        functools.partial(expert_kernel, blocks, choices),
        out_shape=(S((blocks, T, W + 128), BF), S((A, 128), F32), S((W, A), BF),
                   S((E, H, A), BF), S((E, A, H), BF), S((E, A, H), BF), S((E, A, H), BF)),
        grid_spec=pltpu.PrefetchScalarGridSpec(
            num_scalar_prefetch=1, grid=(E,),
            in_specs=[once((T, W))] * blocks + [pl.BlockSpec((T, 128), lambda e, w: (0, W // 128), pipeline_mode=pl.Buffered(1))] * blocks
            + [once((W, 128)), per((W, H)), per((W, H)), per((A, H))],
            out_specs=[whole((blocks, T, W + 128)), whole((A, 128)), whole((W, A)),
                       per((H, A)), per((A, H)), per((A, H)), per((A, H))],
            scratch_shapes=[pltpu.VMEM((A, W), BF), pltpu.VMEM((A, W), F32), pltpu.VMEM((A, 128), F32)]),
        compiler_params=pltpu.CompilerParams(vmem_limit_bytes=60 << 20),
        cost_estimate=pl.CostEstimate(flops=8 * A * W * H * E, bytes_accessed=6 * E * W * H + 12 * A * W, transcendentals=A * H * E),
    )(where, *n2s, *payloads, router, gate_w, up_w, raw)


def grad_kernel(blocks, apart, where_ref, *refs):
    cot_refs, refs = refs[:blocks], refs[blocks:]
    n2t_ref, hid_ref, grow_ref, urow_ref, *outs = refs
    C = grow_ref.shape[2]
    W = n2t_ref.shape[0]
    H = hid_ref.shape[1]
    n_dp = outs[0].shape[0] * len(outs)
    R, D = W // n_dp, H // n_dp
    core = where_ref[1] % 2

    def store(value, rows):
        if not apart:
            outs[0][:, 0, rows, :] = value
            return
        for own in range(2):
            @pl.when(core == own)
            def _(own=own):
                for d in range(n_dp):
                    outs[(d % 2) ^ own][d // 2, 0, rows, :] = value[d]

    left = n2t_ref[...]
    store(dot_nn(left, grow_ref[0]).astype(BF).reshape(n_dp, R, C), slice(0, R))
    store(dot_nn(left, urow_ref[0]).astype(BF).reshape(n_dp, R, C), slice(R, 2 * R))
    for j in range(W // C):
        cot = jnp.concatenate([ref[:, j * C:(j + 1) * C] for ref in cot_refs], axis=0)
        store(dot_nn(hid_ref[0], cot).astype(BF).reshape(n_dp, D, C), slice(2 * R + j * D, 2 * R + (j + 1) * D))


def expert_grads(first, count, apart, where, cots, n2t, hid, grow, urow, n_dp):
    blocks = len(cots)
    T = cots[0].shape[0]
    W, A = n2t.shape
    _, _, H = grow.shape
    P_ = 2 * (W // n_dp) + (W // H) * (H // n_dp)
    shape = (n_dp // 2 if apart else n_dp, count, P_, H)
    once = lambda s: pl.BlockSpec(s, lambda e, w: (0,) * len(s), pipeline_mode=pl.Buffered(1))
    per = lambda s: pl.BlockSpec((1,) + s, lambda e, w: (e + first,) + (0,) * len(s))
    outs = 2 if apart else 1
    made = pl.pallas_call(
        functools.partial(grad_kernel, blocks, apart),
        out_shape=(jax.ShapeDtypeStruct(shape, BF),) * outs,
        grid_spec=pltpu.PrefetchScalarGridSpec(
            num_scalar_prefetch=1, grid=(count,),
            in_specs=[once((T, W))] * blocks + [once((W, A)), per((H, A)), per((A, H)), per((A, H))],
            out_specs=(pl.BlockSpec((shape[0], 1, P_, H), lambda e, w: (0, e, 0, 0)),) * outs),
        compiler_params=pltpu.CompilerParams(vmem_limit_bytes=60 << 20),
        cost_estimate=pl.CostEstimate(flops=0, bytes_accessed=0, transcendentals=0),
    )(where, *cots, n2t, hid, grow, urow)
    return made if apart else made[0]


def combine_kernel(weighed_ref, down_ref, keep_ref, send_ref, total):
    e = pl.program_id(0)
    half, T, _ = keep_ref.shape
    made = dot_nn(weighed_ref[0], down_ref[0])

    @pl.when(e == 0)
    def _():
        total[...] = made

    @pl.when(e > 0)
    def _():
        total[...] += made

    @pl.when(e == pl.num_programs(0) - 1)
    def _():
        for b in range(2 * half):
            out = send_ref if b % 2 else keep_ref
            out[b // 2] = total[b * T:(b + 1) * T, :].astype(BF)


def combine(weighed, down_w, blocks):
    E, A, H = weighed.shape
    W = down_w.shape[2]
    T = A // blocks
    per = lambda s: pl.BlockSpec((1,) + s, lambda e: (e,) + (0,) * len(s))
    out = pl.BlockSpec((blocks // 2, T, W), lambda e: (0, 0, 0))
    return pl.pallas_call(
        combine_kernel,
        out_shape=(jax.ShapeDtypeStruct((blocks // 2, T, W), BF),) * 2,
        grid=(E,),
        in_specs=[per((A, H)), per((H, W))],
        out_specs=(out, out),
        scratch_shapes=[pltpu.VMEM((A, W), F32)],
        compiler_params=pltpu.CompilerParams(vmem_limit_bytes=60 << 20),
        cost_estimate=pl.CostEstimate(flops=0, bytes_accessed=0, transcendentals=0),
    )(weighed, down_w)


def raw_kernel(blocks, *refs):
    payloads, (down_ref, out_ref, cot) = refs[:blocks], refs[blocks:]
    T = payloads[0].shape[0]

    @pl.when(pl.program_id(0) == 0)
    def _():
        for b in range(blocks):
            cot[b * T:(b + 1) * T, :] = payloads[b][...]

    out_ref[0] = dot_nt(cot[...], down_ref[0])


def raw_back(payloads, down_w):
    blocks = len(payloads)
    T = payloads[0].shape[0]
    E, H, W = down_w.shape
    A = blocks * T
    return pl.pallas_call(
        functools.partial(raw_kernel, blocks),
        grid=(E,),
        out_shape=jax.ShapeDtypeStruct((E, A, H), F32),
        in_specs=[pl.BlockSpec((T, W), lambda e: (0, 0), pipeline_mode=pl.Buffered(1))] * blocks
        + [pl.BlockSpec((1, H, W), lambda e: (e, 0, 0))],
        out_specs=pl.BlockSpec((1, A, H), lambda e: (e, 0, 0)),
        scratch_shapes=[pltpu.VMEM((A, W), BF)],
        compiler_params=pltpu.CompilerParams(vmem_limit_bytes=60 << 20),
        cost_estimate=pl.CostEstimate(flops=0, bytes_accessed=0, transcendentals=0),
    )(*payloads, down_w)


def normed_kernel(where_ref, gains_ref, *refs):
    payloads, out_ref = refs[:-1], refs[-1]
    T = payloads[0].shape[0]
    W = gains_ref.shape[1]
    _, half, R, _ = out_ref.shape
    for b, ref in enumerate(payloads):
        x = ref[:, W + 128:].astype(F32)
        inverse = lax.rsqrt(jnp.mean(x * x, axis=1, keepdims=True) + EPSILON)
        turned = (x * inverse * gains_ref[0:1, :]).astype(BF).T
        for d in range(2 * half):
            r = d ^ where_ref[1]
            out_ref[lax.rem(r, 2), lax.div(r, 2), :, b * T:(b + 1) * T] = turned[d * R:(d + 1) * R, :]


def normed_turned(where, gains, payloads, n_dp):
    T = payloads[0].shape[0]
    W = gains.shape[1]
    v = pl.BlockSpec(memory_space=pltpu.VMEM)
    return pl.pallas_call(
        normed_kernel,
        out_shape=jax.ShapeDtypeStruct((2, n_dp // 2, W // n_dp, len(payloads) * T), BF),
        in_specs=[pl.BlockSpec(memory_space=pltpu.SMEM)] + [v] * (1 + len(payloads)),
        out_specs=v,
        compiler_params=pltpu.CompilerParams(vmem_limit_bytes=40 << 20),
        cost_estimate=pl.CostEstimate(flops=0, bytes_accessed=0, transcendentals=0),
    )(where, gains, *payloads)


def rope_tile(x, cosine, sine):
    lane = lax.broadcasted_iota(jnp.int32, x.shape, 1)
    other = jnp.where(lax.rem(lane, 64) < 32, pltpu.roll(x, 96, 1), pltpu.roll(x, 32, 1))
    return x * cosine + other * sine


def half_mask(shape, half):
    lane = lax.broadcasted_iota(jnp.int32, shape, 1)
    return (lane < 64) if half == 0 else (lane >= 64)


def stacked(tiles, group, per, T):
    out = []
    for i in range(per):
        h = group * per + i
        x = tiles[h // 2]
        if h % 2 != group % 2:
            x = pltpu.roll(x, 64, 1)
        out.append(jnp.where(half_mask(x.shape, group % 2), x, 0.0).astype(BF))
    return jnp.concatenate(out, axis=0)


def unstacked(value, group, per, T, tiles):
    for i in range(per):
        h = group * per + i
        x = value[i * T:(i + 1) * T]
        if h % 2 != group % 2:
            x = pltpu.roll(x, 64, 1)
        x = jnp.where(half_mask(x.shape, h % 2), x, 0.0)
        tiles[h // 2] = x if tiles[h // 2] is None else tiles[h // 2] + x


def allowed(seg_row_ref, seg_col_ref, T, per):
    row = lax.broadcasted_iota(jnp.int32, (T, T), 0)
    col = lax.broadcasted_iota(jnp.int32, (T, T), 1)
    ok = (seg_col_ref[...] == seg_row_ref[...]) & (col <= row)
    bias = jnp.where(ok, 0.0, -1e30)
    return jnp.concatenate([bias] * per, axis=0)


def fetch(places, pieces, dev, dst, sems, at, lo, hi):
    R = pieces[0].shape[0]
    copies = []
    for i, ((r, col), piece) in enumerate(zip(places, pieces)):
        a, b = max(lo, col), min(hi, col + piece.shape[1])
        if a < b:
            row = pl.multiple_of((dev ^ r) * R, R)
            copies.append(pltpu.make_async_copy(
                piece.at[:, a - col:b - col], dst.at[pl.ds(row, R), a - lo:b - lo], sems.at[at + i]))
            copies[-1].start()
    return copies


def forward_kernel(places, kv, experts, dev_ref, tok_ref, cos_ref, sin_ref, segr_ref, segc_ref, q_hbm, *refs):
    pieces, refs = refs[:len(places)], refs[len(places):]
    qkv_ref, mix_ref, resid_ref, n2_ref, gains_ref, router_ref, kv_ref, wq, wo, sems = refs
    T, W = tok_ref.shape
    C = 512
    chunks = W // C
    fetched = fetch(places, pieces, dev_ref[1], wo, sems, chunks, 0, wo.shape[1])
    copies = []
    for j in range(chunks):
        copies.append(pltpu.make_async_copy(q_hbm.at[:, j * C:(j + 1) * C], wq.at[j], sems.at[j]))
        copies[-1].start()
    x = tok_ref[...].astype(F32)
    inverse = lax.rsqrt(jnp.mean(x * x, axis=1, keepdims=True) + EPSILON)
    for copy in fetched:
        copy.wait()
    keep = pltpu.make_async_copy(wo.at[:, :2 * kv], kv_ref, sems.at[chunks + len(places)])
    keep.start()
    small = wo[:, 2 * kv + W:]
    router_ref[...] = small
    turned = small.astype(F32).T
    gain1, gain2 = turned[experts:experts + 1, :], turned[experts + 1:experts + 2, :]
    gains_ref[0:1, :] = gain1
    gains_ref[1:2, :] = gain2
    gains_ref[2:8, :] = jnp.zeros((6, W), F32)
    n1 = (x * inverse * gain1).astype(BF)
    cosine, sine = cos_ref[...], sin_ref[...]
    q_tiles = W // 128
    k_tiles = kv // 128
    side = dot_nn(n1, wo[:, :2 * kv])
    others = [side[:, t * 128:(t + 1) * 128] for t in range(2 * k_tiles)]
    others = [rope_tile(t, cosine, sine).astype(BF) for t in others[:k_tiles]] + [t.astype(BF) for t in others[k_tiles:]]
    tiles = []
    for j in range(chunks):
        copies[j].wait()
        made = dot_nn(n1, wq[j])
        tiles += [rope_tile(made[:, t * 128:(t + 1) * 128], cosine, sine).astype(BF) for t in range(C // 128)]
    tiles += others
    for t, tile in enumerate(tiles):
        qkv_ref[:, t * 128:(t + 1) * 128] = tile
    per = q_tiles // k_tiles
    bias = allowed(segr_ref, segc_ref, T, per)
    q = [t.astype(F32) for t in tiles[:q_tiles]]
    mixed = [None] * q_tiles
    for g in range(2 * k_tiles):
        k_tile, v_tile = tiles[q_tiles + g // 2], tiles[q_tiles + k_tiles + g // 2]
        s = dot_nt(stacked(q, g, per, T), k_tile) * SCORE_FACTOR + bias
        raised = jnp.exp(s - jnp.max(s, axis=1, keepdims=True))
        p = raised / jnp.sum(raised, axis=1, keepdims=True)
        unstacked(dot_nn(p.astype(BF), v_tile), g, per, T, mixed)
    for t in range(q_tiles):
        mix_ref[:, t * 128:(t + 1) * 128] = mixed[t].astype(BF)
    total = jnp.zeros((T, 1), F32)
    for j in range(chunks):
        cols = slice(j * C, (j + 1) * C)
        r = tok_ref[:, cols].astype(F32) + dot_nn(mix_ref[...], wo[:, 2 * kv + j * C:2 * kv + (j + 1) * C])
        resid_ref[:, cols] = r
        total = total + jnp.sum(r * r, axis=1, keepdims=True)
    inverse = lax.rsqrt(total / W + EPSILON)
    n2_ref[...] = (resid_ref[...] * inverse * gain2).astype(BF)
    keep.wait()


def forward(where, tokens, cosine, sine, segr, segc, q_w, pieces, places, kv, experts):
    T, W = tokens.shape
    N = W + 2 * kv
    S = jax.ShapeDtypeStruct
    v = pl.BlockSpec(memory_space=pltpu.VMEM)
    hbm = pl.BlockSpec(memory_space=pl.ANY)
    return pl.pallas_call(
        functools.partial(forward_kernel, places, kv, experts),
        out_shape=(S((T, N), BF), S((T, W), BF), S((T, W), F32), S((T, W), BF), S((8, W), F32), S((W, 128), BF), S((W, 2 * kv), BF)),
        in_specs=[pl.BlockSpec(memory_space=pltpu.SMEM)] + [v] * 5 + [hbm] * (1 + len(places)),
        out_specs=(v,) * 6 + (hbm,),
        scratch_shapes=[pltpu.VMEM((W // 512, W, 512), BF), pltpu.VMEM((W, N + 128), BF),
                        pltpu.SemaphoreType.DMA((W // 512 + len(places) + 1,))],
        compiler_params=pltpu.CompilerParams(vmem_limit_bytes=60 << 20),
        cost_estimate=pl.CostEstimate(flops=0, bytes_accessed=0, transcendentals=0),
    )(where, tokens, cosine, sine, segr, segc, q_w, *pieces)


def split(x):
    hi = x.astype(BF)
    return hi, (x - hi.astype(F32)).astype(BF)


def dot_tn(a, b): return lax.dot_general(a, b, (((0,), (0,)), ((), ())), preferred_element_type=F32)


def ones_at(T, lane):
    return jnp.where(lax.broadcasted_iota(jnp.int32, (T, 128), 1) == lane, 1.0, 0.0).astype(BF)


def middle_kernel(experts, *refs):
    (rows_ref, gates_ref, router_ref, n2_ref, resid_ref, g2_ref, cot_ref, att_ref, cut_ref, back_ref, extra_ref) = refs
    T, W = n2_ref.shape
    total = rows_ref[0].astype(F32)
    for b in range(1, rows_ref.shape[0]):
        total = total + rows_ref[b].astype(F32)
    aux = total[:, W:]
    gate_back = aux + pltpu.roll(aux, 64, 1)
    gates = gates_ref[...]
    hi, lo = split(gates * (gate_back - jnp.sum(gates * gate_back, axis=1, keepdims=True)))
    n2_back = total[:, :W] + dot_nt(hi, router_ref[...]) + dot_nt(lo, router_ref[...])
    resid = resid_ref[...]
    inverse = lax.rsqrt(jnp.mean(resid * resid, axis=1, keepdims=True) + EPSILON)
    scaled = n2_back * g2_ref[1:2, :]
    inner = jnp.mean(scaled * resid, axis=1, keepdims=True)
    back = cot_ref[...].astype(F32) + inverse * scaled - resid * (inverse * inverse * inverse * inner)
    back_ref[...] = back
    att_ref[...] = back.astype(BF)
    width = cut_ref.shape[2]
    for b in range(cut_ref.shape[0]):
        cut_ref[b] = back[:, b * width:(b + 1) * width].astype(BF)
    p_hi, p_lo = split(n2_back * resid * inverse)
    one = ones_at(T, experts)
    extra_ref[...] = dot_tn(n2_ref[...], hi) + dot_tn(n2_ref[...], lo) + dot_tn(p_hi, one) + dot_tn(p_lo, one)


def middle(rows_in, gates, router, n2, resid, gain2, cot, experts):
    T, W = n2.shape
    blocks = rows_in.shape[0]
    S = jax.ShapeDtypeStruct
    v = lambda s: pl.BlockSpec(s, lambda i: (0, 0))
    return pl.pallas_call(
        functools.partial(middle_kernel, experts),
        grid=(1,),
        out_shape=(S((T, W), BF), S((blocks, T, W // blocks), BF), S((T, W), F32), S((W, 128), F32)),
        in_specs=[pl.BlockSpec((blocks, T, W + 128), lambda i: (0, 0, 0)), v((T, 128)), v((W, 128)), v((T, W)), v((T, W)), v((8, W)), v((T, W))],
        out_specs=(v((T, W)), pl.BlockSpec((blocks, T, W // blocks), lambda i: (0, 0, 0)), v((T, W)), v((W, 128))),
        compiler_params=pltpu.CompilerParams(vmem_limit_bytes=40 << 20),
        cost_estimate=pl.CostEstimate(flops=400_000_000_000, bytes_accessed=30 * T * W, transcendentals=T),
    )(rows_in, gates, router, n2, resid, gain2, cot)


def backward_kernel(places, dev_ref, att_ref, qkv_ref, cos_ref, sin_ref, segr_ref, segc_ref, *refs):
    outs, refs = refs[:len(places)], refs[len(places):]
    back_ref, cut_ref, wo, sems = refs
    T, W = att_ref.shape
    fetched = fetch(places, outs, dev_ref[1], wo, sems, 0, qkv_ref.shape[1] - W, qkv_ref.shape[1])
    q_tiles = W // 128
    k_tiles = (qkv_ref.shape[1] - W) // 256
    per = q_tiles // k_tiles
    tile = lambda t: qkv_ref[:, t * 128:(t + 1) * 128]
    q = [tile(t).astype(F32) for t in range(q_tiles)]
    bias = allowed(segr_ref, segc_ref, T, per)
    cosine, sine = cos_ref[...], -sin_ref[...]
    for copy in fetched:
        copy.wait()
    mixed_back = []
    for j in range(W // 512):
        made = dot_nt(att_ref[...], wo[j * 512:(j + 1) * 512, :]).astype(BF).astype(F32)
        mixed_back += [made[:, t * 128:(t + 1) * 128] for t in range(4)]
    q_back = [None] * q_tiles
    k_back = [None] * k_tiles
    v_back = [None] * k_tiles
    for g in range(2 * k_tiles):
        k_tile, v_tile = tile(q_tiles + g // 2), tile(q_tiles + k_tiles + g // 2)
        qs = stacked(q, g, per, T)
        ms = stacked(mixed_back, g, per, T)
        s = dot_nt(qs, k_tile) * SCORE_FACTOR + bias
        raised = jnp.exp(s - jnp.max(s, axis=1, keepdims=True))
        p = raised / jnp.sum(raised, axis=1, keepdims=True)
        dp = dot_nt(ms, v_tile)
        ds = (p * (dp - jnp.sum(p * dp, axis=1, keepdims=True)) * SCORE_FACTOR).astype(BF)
        unstacked(dot_nn(ds, k_tile), g, per, T, q_back)
        kb, vb = dot_tn(ds, qs), dot_tn(p.astype(BF), ms)
        k_back[g // 2] = kb if g % 2 == 0 else k_back[g // 2] + kb
        v_back[g // 2] = vb if g % 2 == 0 else v_back[g // 2] + vb
    made = [rope_tile(t, cosine, sine) for t in q_back + k_back] + v_back
    for t, value in enumerate(made):
        back_ref[:, t * 128:(t + 1) * 128] = value.astype(BF)
        of, place = (q_tiles, t) if t < q_tiles else (k_tiles, (t - q_tiles) % k_tiles)
        each = of // cut_ref.shape[0]
        at = place % each * 128 + (0 if t < q_tiles else (q_tiles + (k_tiles if t >= q_tiles + k_tiles else 0)) // cut_ref.shape[0] * 128)
        cut_ref[place // each, :, at:at + 128] = value.astype(BF)


def backward(where, att, qkv, cosine, sine, segr, segc, outs, places, ne):
    T, W = att.shape
    N = qkv.shape[1]
    S = jax.ShapeDtypeStruct
    v = pl.BlockSpec(memory_space=pltpu.VMEM)
    hbm = pl.BlockSpec(memory_space=pl.ANY)
    return pl.pallas_call(
        functools.partial(backward_kernel, places),
        out_shape=(S((T, N), BF), S((ne, T, N // ne), BF)),
        in_specs=[pl.BlockSpec(memory_space=pltpu.SMEM)] + [v] * 6 + [hbm] * len(places),
        out_specs=(v, v),
        scratch_shapes=[pltpu.VMEM((W, W), BF), pltpu.SemaphoreType.DMA((len(places),))],
        compiler_params=pltpu.CompilerParams(vmem_limit_bytes=60 << 20),
        cost_estimate=pl.CostEstimate(flops=0, bytes_accessed=0, transcendentals=0),
    )(where, att, qkv, cosine, sine, segr, segc, *outs)


def last_kernel(experts, back_ref, tok_ref, g1_ref, resid_back_ref, extra_ref, q_ref, kv_ref, grad_ref, more_ref, nb):
    j = pl.program_id(0)
    T, W = tok_ref.shape
    C = q_ref.shape[0]
    nb[j] = dot_nt(back_ref[:, :W], q_ref[...]) + dot_nt(back_ref[:, W:], kv_ref[...])

    @pl.when(j == pl.num_programs(0) - 1)
    def _():
        x = tok_ref[...].astype(F32)
        inverse = lax.rsqrt(jnp.mean(x * x, axis=1, keepdims=True) + EPSILON)
        n1_back = jnp.concatenate([nb[i] for i in range(W // C)], axis=1)
        scaled = n1_back * g1_ref[0:1, :]
        inner = jnp.mean(scaled * x, axis=1, keepdims=True)
        grad_ref[...] = resid_back_ref[...] + inverse * scaled - x * (inverse * inverse * inverse * inner)
        p_hi, p_lo = split(n1_back * x * inverse)
        one = ones_at(T, experts + 1)
        more_ref[...] = extra_ref[...] + dot_tn(p_hi, one) + dot_tn(p_lo, one)


def last(back, tokens, gains, resid_back, extra, q_w, kv_w, experts):
    T, W = tokens.shape
    N = back.shape[1]
    C = 512
    S = jax.ShapeDtypeStruct
    v = lambda s: pl.BlockSpec(s, lambda j: (0, 0))
    return pl.pallas_call(
        functools.partial(last_kernel, experts),
        grid=(W // C,),
        out_shape=(S((T, W), F32), S((W, 128), F32)),
        in_specs=[v((T, N)), v((T, W)), v((8, W)), v((T, W)), v((W, 128)), pl.BlockSpec((C, W), lambda j: (j, 0)),
                  pl.BlockSpec((C, N - W), lambda j: (j, 0))],
        out_specs=(v((T, W)), v((W, 128))),
        scratch_shapes=[pltpu.VMEM((W // C, T, C), F32)],
        compiler_params=pltpu.CompilerParams(vmem_limit_bytes=40 << 20),
        cost_estimate=pl.CostEstimate(flops=0, bytes_accessed=0, transcendentals=0),
    )(back, tokens, gains, resid_back, extra, q_w, kv_w)


def out_grad_kernel(blocks, where_ref, *refs):
    mix_refs, (att_ref, keep_ref, send_ref, left) = refs[:blocks], refs[blocks:]
    own, dev = where_ref[0], where_ref[1]
    T = mix_refs[0].shape[0]
    half, _, R, C = keep_ref.shape
    for b in range(blocks):
        turned = mix_refs[b][...].T
        for d in range(2 * half):
            r = d ^ dev
            left[lax.rem(r, 2), lax.div(r, 2), :, b * T:(b + 1) * T] = turned[d * R:(d + 1) * R, :]
    right = jnp.concatenate([att_ref[own ^ b] for b in range(blocks)], axis=0)
    for s, out in ((1, send_ref), (0, keep_ref)):
        out[:, 0] = dot_nn(left[s].reshape(half * R, blocks * T), right).astype(BF).reshape(half, R, C)


def out_grads(where, mixs, att_cut, n_dp):
    blocks = len(mixs)
    T, W = mixs[0].shape
    C = att_cut.shape[2]
    R = W // n_dp
    S = jax.ShapeDtypeStruct
    v = pl.BlockSpec(memory_space=pltpu.VMEM)
    return pl.pallas_call(
        functools.partial(out_grad_kernel, blocks),
        out_shape=(S((n_dp // 2, 1, R, C), BF),) * 2,
        in_specs=[pl.BlockSpec(memory_space=pltpu.SMEM)] + [v] * (blocks + 1),
        out_specs=(v, v),
        scratch_shapes=[pltpu.VMEM((2, n_dp // 2, R, blocks * T), BF)],
        compiler_params=pltpu.CompilerParams(vmem_limit_bytes=60 << 20),
        cost_estimate=pl.CostEstimate(flops=0, bytes_accessed=0, transcendentals=0),
    )(where, *mixs, att_cut)


def qkv_grad_kernel(where_ref, left_ref, qkv_ref, extra_ref, keep_ref, send_ref):
    own, dev = where_ref[0], where_ref[1]
    blocks, _, width = qkv_ref.shape
    half, _, R, C = keep_ref.shape
    right = jnp.concatenate([qkv_ref[own ^ b] for b in range(blocks)], axis=0)
    for s, out in ((1, send_ref), (0, keep_ref)):
        left = left_ref[s].reshape(half * R, left_ref.shape[3])
        out[:, 0, :, :width] = dot_nn(left, right).astype(BF).reshape(half, R, width)
    for d in range(2 * half):
        more = extra_ref[d * R:(d + 1) * R, :].astype(BF)
        r = d ^ dev

        @pl.when(lax.rem(r, 2) == 0)
        def _(more=more, r=r):
            keep_ref[lax.div(r, 2), 0, :, width:] = more

        @pl.when(lax.rem(r, 2) == 1)
        def _(more=more, r=r):
            send_ref[lax.div(r, 2), 0, :, width:] = more


def qkv_grads(where, left, qkv_cut, extra, n_dp):
    W = extra.shape[0]
    C = qkv_cut.shape[2] + 128
    R = W // n_dp
    S = jax.ShapeDtypeStruct
    v = pl.BlockSpec(memory_space=pltpu.VMEM)
    return pl.pallas_call(
        qkv_grad_kernel,
        out_shape=(S((n_dp // 2, 1, R, C), BF),) * 2,
        in_specs=[pl.BlockSpec(memory_space=pltpu.SMEM)] + [v] * 3,
        out_specs=(v, v),
        compiler_params=pltpu.CompilerParams(vmem_limit_bytes=60 << 20),
        cost_estimate=pl.CostEstimate(flops=2 * W * C * left.shape[3], bytes_accessed=4 * W * C, transcendentals=0),
    )(where, left, qkv_cut, extra)


def flip(x, axis, mask, size):
    return lax.ppermute(x, axis, [(i, i ^ mask) for i in range(size)])


def add(a, b):
    return (a.astype(F32) + b.astype(F32)).astype(BF)


def split_kernel(width, where_ref, *refs):
    ins, (a_keep, a_send, b_keep, b_send) = refs[:-4], refs[-4:]
    count = ins[0].shape[-4]
    for q in range(count):
        at = q ^ where_ref[0]
        sums = [(ins[i][at, 0].astype(F32) + ins[i + 1][at, 0].astype(F32)).astype(BF) for i in range(0, len(ins), 2)]
        total = sums[0] if len(sums) == 1 else jnp.concatenate(sums, axis=1)
        out = a_send if q % 2 else a_keep
        out[q // 2, 0] = total[:, :width]
        out = b_send if q >= count // 2 else b_keep
        out[q % (count // 2), 0] = total[:, width:]


def halves(pairs, n_dp, order=None):
    bits = n_dp.bit_length() - 1
    count, group, rows, _ = pairs[0][1].shape
    cols = sum(theirs.shape[3] for _, theirs in pairs)
    a = cols // 256 * 128
    S = jax.ShapeDtypeStruct
    if order is None:
        order = jnp.zeros((1,), jnp.int32)
    specs = []
    for keep, theirs in pairs:
        shape = (count, 1, rows, theirs.shape[3])
        specs += [pl.BlockSpec(shape, lambda g, w: (0, g, 0, 0))] * 2
    widths = (a, a, cols - a, cols - a)
    outs = pl.pallas_call(
        functools.partial(split_kernel, a),
        out_shape=tuple(S((count // 2, group, rows, c), BF) for c in widths),
        grid_spec=pltpu.PrefetchScalarGridSpec(
            num_scalar_prefetch=1, grid=(group,), in_specs=specs,
            out_specs=tuple(pl.BlockSpec((count // 2, 1, rows, c), lambda g, w: (0, g, 0, 0)) for c in widths)),
        compiler_params=pltpu.CompilerParams(vmem_limit_bytes=40 << 20),
        cost_estimate=pl.CostEstimate(flops=0, bytes_accessed=0, transcendentals=0),
    )(order.astype(jnp.int32), *[x for pair in pairs for x in pair])
    left = tuple(range(bits - 1, 0, -1))
    shaped = lambda x: x.reshape((2,) * (bits - 2) + x.shape[1:])
    return [(shaped(outs[0]), shaped(outs[1]), left[:-1], tuple(range(1, bits))),
            (shaped(outs[2]), shaped(outs[3]), left[1:], left)]


def halve(parts, n_dp):
    done = []
    for mine, sent, left, order in parts:
        theirs = flip(sent, "dp", 1 << order[0], n_dp)
        if left:
            total = add(mine, theirs)
            axis = left.index(order[1])
            mine, theirs = (lax.index_in_dim(total, i, axis, keepdims=False) for i in (0, 1))
        done.append((mine, theirs, tuple(b for b in left if b != order[1]) if left else (), order[1:]))
    return done


def finish(parts, n_dp):
    while parts[0][3]:
        parts = halve(parts, n_dp)
    return parts


def tie_parts(parts, *others):
    arrays, others = lax.optimization_barrier(([p[:2] for p in parts], others))
    return [tuple(a) + p[2:] for a, p in zip(arrays, parts)], *others


def unpack_kernel(parts, *refs):
    gate_ref, up_ref, down_ref = refs[-3:]
    R, D = gate_ref.shape[1], down_ref.shape[1]
    H = gate_ref.shape[2]
    at = 0
    for i in range(0, len(parts), 2):
        total = refs[parts[i]][0].astype(F32)
        if parts[i + 1] is not None:
            total = total + refs[parts[i + 1]][0].astype(F32)
        width = total.shape[1]
        gate_ref[0, :, at:at + width] = total[:R]
        up_ref[0, :, at:at + width] = total[R:2 * R]
        for j in range(down_ref.shape[2] // H):
            down_ref[0, :, j * H + at:j * H + at + width] = total[2 * R + j * D:2 * R + (j + 1) * D]
        at += width


def unpack(first, ins, parts, before, E, R, D, W):
    count, rows, _ = ins[0].shape
    H = before[0].shape[2] if before else ins[0].shape[2]
    S = jax.ShapeDtypeStruct
    out = lambda a, b: pl.BlockSpec((1, a, b), lambda e: (e + first, 0, 0))
    return pl.pallas_call(
        functools.partial(unpack_kernel, parts),
        grid=(count,),
        out_shape=(S((E, R, H), F32), S((E, R, H), F32), S((E, D, W), F32)),
        in_specs=[pl.BlockSpec((1, rows, x.shape[2]), lambda e: (e, 0, 0)) for x in ins]
        + [pl.BlockSpec(memory_space=pl.ANY)] * len(before),
        out_specs=(out(R, H), out(R, H), out(D, W)),
        input_output_aliases={len(ins) + i: i for i in range(len(before))},
        compiler_params=pltpu.CompilerParams(vmem_limit_bytes=40 << 20),
        cost_estimate=pl.CostEstimate(flops=3 * count * R * H, bytes_accessed=18 * count * R * H, transcendentals=0),
    )(*ins, *before)


def spread_kernel(kv, where_ref, *refs):
    parts, (q_ref, k_ref, v_ref, o_ref, extra_ref) = refs[:-5], refs[-5:]
    blocks = len(parts)
    wide, narrow = q_ref.shape[1] // blocks, kv // blocks
    extra = None
    for b, ref in enumerate(parts):
        at = where_ref[0] ^ b
        col = 0
        for out, width in ((o_ref, wide), (q_ref, wide), (k_ref, narrow), (v_ref, narrow)):
            out[:, pl.ds(pl.multiple_of(at * width, width), width)] = ref[:, col:col + width].astype(F32)
            col += width
        more = ref[:, col:].astype(F32)
        extra = more if extra is None else extra + more
    extra_ref[...] = extra


def spread(where, parts, W, kv):
    R, C = parts[0].shape
    S = jax.ShapeDtypeStruct
    v = pl.BlockSpec(memory_space=pltpu.VMEM)
    return pl.pallas_call(
        functools.partial(spread_kernel, kv),
        out_shape=(S((R, W), F32), S((R, kv), F32), S((R, kv), F32), S((R, W), F32), S((R, 128), F32)),
        in_specs=[pl.BlockSpec(memory_space=pltpu.SMEM)] + [v] * len(parts),
        out_specs=(v,) * 5,
        compiler_params=pltpu.CompilerParams(vmem_limit_bytes=40 << 20),
        cost_estimate=pl.CostEstimate(flops=R * C, bytes_accessed=24 * R * C, transcendentals=0),
    )(where, *parts)


def begin_z(x, ne):
    found = {0: x}
    bit = 1
    while bit < ne:
        found[bit] = flip(x, "expert", bit, ne)
        bit *= 2
    return found


def end_z(found, ne):
    for k in range(ne):
        if k not in found:
            found[k] = flip(found[k & (k - 1)], "expert", k & -k, ne)
    return [found[k] for k in range(ne)]


def gather_z(x, ne):
    return end_z(begin_z(x, ne), ne)


def gather_dp(w, n_dp, ready):
    half = w.shape[1] // 256 * 128
    found = {(0, 0): w[:, :half], (0, half): w[:, half:]}
    whole = {0: w}
    bits = range(1, n_dp.bit_length() - 1)
    for bit in bits:
        whole[1 << bit] = flip(w, "dp", 1 << bit, n_dp)
    whole, ready = lax.optimization_barrier((whole, ready))
    for bit in bits:
        r = 1 << bit
        found[r, 0], found[r, half] = whole[r][:, :half], whole[r][:, half:]
    for r in range(2, n_dp, 2):
        low, high = r & -r, 1 << (r.bit_length() - 1)
        if low != high:
            found[r, 0] = flip(found[r ^ high, 0], "dp", high, n_dp)
            found[r, half] = flip(found[r ^ low, half], "dp", low, n_dp)
    pieces = {}
    for (r, col), x in found.items():
        if r in whole:
            pieces[r, 0] = whole[r]
        else:
            pieces[r, col] = x
    for (r, col), x in list(pieces.items()):
        pieces[r ^ 1, col] = flip(x, "dp", 1, n_dp)
    places = sorted(pieces)
    return tuple(places), [pieces[p] for p in places], ready


def local(n_dp, ne, tokens, segment_ids, routes, cotangent, query_weight, key_weight, value_matrix, out_weight,
          first_gain, second_gain, router_weight, gate_weight, up_weight, down_weight):
    d = lax.axis_index("dp")
    z = lax.axis_index("expert")
    tie = lax.optimization_barrier
    T, W = tokens.shape
    experts = router_weight.shape[1]
    E, _, H = gate_weight.shape
    R = W // n_dp
    D = H // n_dp
    KV = key_weight.shape[1]
    where = jnp.stack([z, d, jnp.int32(E), jnp.int32(0)]).astype(jnp.int32)

    q_full = lax.all_gather(query_weight, "dp", axis=0, tiled=True)
    side = jnp.concatenate([key_weight, value_matrix, out_weight, router_weight, first_gain[:, None], second_gain[:, None],
                            jnp.zeros((R, 126 - experts), BF)], axis=1)
    segments = segment_ids[0]
    segr, segc = segments[None, :], segments[:, None]
    positions = jnp.arange(T, dtype=jnp.int32) - jnp.sum((segr < segc).astype(jnp.int32), axis=1)
    half = HEAD_SIZE // 2
    freq = ROTARY_BASE ** (-jnp.arange(half, dtype=F32) * 2.0 / HEAD_SIZE)
    angle = positions.astype(F32)[:, None] * freq[None, :]
    cosine = jnp.tile(jnp.cos(angle), (1, 4))
    sine = jnp.sin(angle)
    sine = jnp.concatenate([-sine, sine, -sine, sine], axis=1)
    choices = routes.shape[1]
    payload = jnp.concatenate([cotangent, jnp.pad(routes.astype(BF), ((0, 0), (0, 128 - choices))), tokens], axis=1)
    places, pieces, (cosine, sine, segc, where) = gather_dp(side, n_dp, (cosine, sine, segc, where))
    payloads = gather_z(payload, ne)
    core = lambda x: flip(x, "dp", 1, n_dp)
    exchange = lambda x: lax.all_to_all(x, "expert", split_axis=0, concat_axis=0, tiled=True)
    payloads, pieces, q_full = tie((payloads, pieces, q_full))
    qkv, mixed, resid, normed2, gains, router, kv_full = forward(
        where, tokens, cosine, sine, segr, segc, q_full, pieces, places, KV, experts)
    raw = raw_back(payloads, down_weight)
    n1t = normed_turned(where, gains, payloads, n_dp)
    n2s, raw, n1t = tie((begin_z(normed2, ne), raw, n1t))
    n2s, mixed = tie((end_z(n2s, ne), mixed))
    mixs = begin_z(mixed, ne)
    made = expert_rows(where, n2s, payloads, choices, router, gate_weight, up_weight, raw)
    made, mixs = tie((made, mixs))
    rows, gates, n2t, hid, weighed, grow, urow = made
    rows = exchange(rows)
    partial = expert_grads(0, MANY, False, where, payloads, n2t, hid, grow, urow, n_dp)
    packed = lax.psum_scatter(partial, "dp", scatter_dimension=0, tiled=True)
    partial, n2t, weighed = tie((partial, n2t, weighed))
    few, away = expert_grads(MANY, E - MANY, True, where, payloads, n2t, hid, grow, urow, n_dp)
    comb, comb_away = combine(weighed, down_weight, ne)
    rows, few, away, comb, comb_away, mixs = tie((rows, few, away, comb, comb_away, mixs))
    mixs = end_z(mixs, ne)
    comb_in = flip(comb_away, "expert", 1, ne)
    theirs = core(away)
    attended, att_cut, resid_back, extra = middle(rows, gates, router, normed2, resid, gains, cotangent, experts)
    att_cut = exchange(att_cut)
    back, back_cut = backward(where, attended, qkv, cosine, sine, segr, segc, pieces, places, ne)
    att_cut, back, back_cut, few, theirs, comb_in = tie((att_cut, back, back_cut, few, theirs, comb_in))
    back_cut = exchange(back_cut)
    few = halves([(few, theirs)], n_dp, (d // 2).reshape(1))
    input_grad, extra = last(back, tokens, gains, resid_back, extra, q_full, kv_full, experts)
    keep4, send4 = out_grads(where, mixs, att_cut, n_dp)
    comb = comb.astype(F32) + comb_in.astype(F32)
    comb, comb_far = comb[0], comb[1:].astype(BF)
    few, back_cut, extra, keep4, send4, comb_far = tie_parts(few, back_cut, extra, keep4, send4, comb_far)
    comb_far = [flip(comb_far[i], "expert", 2 * (i + 1), ne) for i in range(ne // 2 - 1)]
    theirs4 = core(send4)
    keep5, send5 = qkv_grads(where, n1t, back_cut, extra, n_dp)
    keep5, send5, theirs4 = tie((keep5, send5, theirs4))
    five = halve(halves([(keep4, theirs4), (keep5, core(send5))], n_dp), n_dp)
    five, comb_far = tie_parts(five, comb_far)
    five = finish(five, n_dp)
    part = jnp.concatenate([mine.astype(F32) + theirs.astype(F32) for mine, theirs, *_ in five], axis=-1)[0].astype(BF)
    few, part = tie_parts(few, part)
    parts = gather_z(part, ne)
    few = finish(few, n_dp)
    made = unpack(0, [packed[0]], (0, None), (), E, R, D, W)
    parts, made = tie((parts, made))
    query_grad, key_grad, value_grad, out_grad, extra = spread(where, parts, W, KV)
    gate_grad, up_grad, down_grad = unpack(MANY, [x for p in few for x in p[:2]], (0, 1, 2, 3), made, E, R, D, W)
    layer_out = (resid + comb + sum(x.astype(F32) for x in comb_far)).astype(BF)
    return (layer_out, input_grad, query_grad, key_grad, value_grad, out_grad, extra[:, experts + 1], extra[:, experts],
            extra[:, :experts], gate_grad, up_grad, down_grad)


def solution(mesh):
    both = P(("dp", "expert"), None)
    dp = P("dp", None)
    own = P("expert", None, None)
    part = P("expert", "dp", None)
    return jax.shard_map(
        functools.partial(local, mesh.shape["dp"], mesh.shape["expert"]),
        mesh=mesh,
        in_specs=(both, both, both, both, dp, dp, dp, dp, P("dp"), P("dp"), dp, own, own, own),
        out_specs=(both, both, dp, dp, dp, dp, P("dp"), P("dp"), dp, part, part, part),
        check_vma=False,
    )
```

```python
import functools
import jax
import jax.numpy as jnp
from jax import lax
from jax.experimental import pallas as pl
from jax.experimental.pallas import tpu as pltpu
from jax.sharding import PartitionSpec as P

HEAD_SIZE = 64
EPSILON = 1e-06
ROTARY_BASE = 10000.0
SCORE_FACTOR = 0.015625
MANY = 4
F32=jnp.float32; BF=jnp.bfloat16
def dot_nn(a,b): return lax.dot_general(a,b,(((1,),(0,)),((),())),preferred_element_type=F32)
def dot_nt(a,b): return lax.dot_general(a,b,(((1,),(1,)),((),())),preferred_element_type=F32)

def column(table, lane):
    at = lax.broadcasted_iota(jnp.int32, table.shape, 1) == lane
    return jnp.sum(jnp.where(at, table, 0.0), axis=1, keepdims=True)

def expert_kernel(blocks, choices, where_ref, *refs):
    n2_refs, refs = refs[:blocks], refs[blocks:]
    pick_refs, refs = refs[:blocks], refs[blocks:]
    (router_ref, gate_ref, up_ref, raw_ref,
     rows_ref, gates_ref, n2t_ref, hid_ref, weighed_ref, grow_ref, urow_ref,
     n2, rows, aux_ref) = refs
    e = pl.program_id(0)
    own = where_ref[0]
    experts_here = pl.num_programs(0)
    T = n2_refs[0].shape[0]; W = n2_refs[0].shape[1]; H = gate_ref.shape[2]
    C = 512

    @pl.when(e == 0)
    def _():
        for b in range(blocks):
            n2[b * T:(b + 1) * T, :] = n2_refs[b][...]
            picks = pick_refs[b][...].astype(F32)
            logits = dot_nn(n2_refs[b][...], router_ref[...])
            lane = lax.broadcasted_iota(jnp.int32, logits.shape, 1)
            named = lane < 0
            for k in range(choices):
                named = named | (lane.astype(F32) == picks[:, k:k + 1])
            logits = jnp.where(named, logits, -1e30)
            top = jnp.max(logits, axis=1, keepdims=True)
            raised = jnp.where(named, jnp.exp(logits - top), 0.0)
            gates_ref[b * T:(b + 1) * T, :] = raised / jnp.sum(raised, axis=1, keepdims=True)
        aux_ref[...] = jnp.zeros_like(aux_ref)
        rows[...] = jnp.zeros_like(rows)

    mine = own * experts_here + e
    g = column(gates_ref[...], mine)
    sides = [slice(h * (H // 2), (h + 1) * (H // 2)) for h in range(2)]
    pres = [(dot_nn(n2[...], gate_ref[0, :, s]), dot_nn(n2[...], up_ref[0, :, s])) for s in sides]
    back = jnp.zeros((blocks * T, 1), F32)
    for s, (gate_pre, up_pre) in zip(sides, pres):
        raw = raw_ref[0, :, s]
        sig = 0.5 * jnp.tanh(0.5 * gate_pre) + 0.5
        silu = gate_pre * sig
        hidden = (silu * up_pre).astype(BF).astype(F32)
        back = back + jnp.sum(hidden * raw, axis=1, keepdims=True)
        weighed = (g * hidden).astype(BF)
        weighed_ref[0, :, s] = weighed
        hid_ref[0, s, :] = weighed.T
        hid_back = g * raw
        grow = (hid_back * up_pre * (sig + silu * (1.0 - sig))).astype(BF)
        urow = (hid_back * silu).astype(BF)
        grow_ref[0, :, s] = grow
        urow_ref[0, :, s] = urow
    lane = lax.broadcasted_iota(jnp.int32, aux_ref.shape, 1)
    aux_ref[...] = jnp.where(lane == mine, back, aux_ref[...])
    part = pl.multiple_of(jnp.minimum(e, W // C - 1) * C, C)
    n2t_ref[pl.ds(part, C), :] = n2[:, pl.ds(part, C)].T
    for j in range(W // C):
        cols = slice(j * C, (j + 1) * C)
        rows[:, cols] += dot_nt(grow_ref[0], gate_ref[0, cols, :]) + dot_nt(urow_ref[0], up_ref[0, cols, :])

    @pl.when(e == experts_here - 1)
    def _():
        hi = aux_ref[...].astype(BF).astype(F32)
        packed = (hi + pltpu.roll(aux_ref[...] - hi, 64, 1)).astype(BF)
        for b in range(blocks):
            part = slice(b * T, (b + 1) * T)
            rows_ref[own ^ b, :, :W] = rows[part, :].astype(BF)
            rows_ref[own ^ b, :, W:] = packed[part, :]


def expert_rows(where, n2s, payloads, choices, router, gate_w, up_w, raw):
    blocks = len(n2s)
    T, W = n2s[0].shape
    E, _, H = gate_w.shape
    A = blocks * T
    once = lambda s: pl.BlockSpec(s, lambda e, w: (0,) * len(s), pipeline_mode=pl.Buffered(1))
    whole = lambda s: pl.BlockSpec(s, lambda e, w: (0,) * len(s))
    per = lambda s: pl.BlockSpec((1,) + s, lambda e, w: (e,) + (0,) * len(s))
    S = jax.ShapeDtypeStruct
    return pl.pallas_call(
        functools.partial(expert_kernel, blocks, choices),
        out_shape=(S((blocks, T, W + 128), BF), S((A, 128), F32), S((W, A), BF),
                   S((E, H, A), BF), S((E, A, H), BF), S((E, A, H), BF), S((E, A, H), BF)),
        grid_spec=pltpu.PrefetchScalarGridSpec(
            num_scalar_prefetch=1, grid=(E,),
            in_specs=[once((T, W))] * blocks + [pl.BlockSpec((T, 128), lambda e, w: (0, W // 128), pipeline_mode=pl.Buffered(1))] * blocks
            + [once((W, 128)), per((W, H)), per((W, H)), per((A, H))],
            out_specs=[whole((blocks, T, W + 128)), whole((A, 128)), whole((W, A)),
                       per((H, A)), per((A, H)), per((A, H)), per((A, H))],
            scratch_shapes=[pltpu.VMEM((A, W), BF), pltpu.VMEM((A, W), F32), pltpu.VMEM((A, 128), F32)]),
        compiler_params=pltpu.CompilerParams(vmem_limit_bytes=60 << 20),
        cost_estimate=pl.CostEstimate(flops=8 * A * W * H * E, bytes_accessed=6 * E * W * H + 12 * A * W, transcendentals=A * H * E),
    )(where, *n2s, *payloads, router, gate_w, up_w, raw)


def grad_kernel(blocks, apart, where_ref, *refs):
    cot_refs, refs = refs[:blocks], refs[blocks:]
    n2t_ref, hid_ref, grow_ref, urow_ref, *outs = refs
    C = grow_ref.shape[2]
    W = n2t_ref.shape[0]
    H = hid_ref.shape[1]
    n_dp = outs[0].shape[0] * len(outs)
    R, D = W // n_dp, H // n_dp
    core = where_ref[1] % 2

    def store(value, rows):
        if not apart:
            outs[0][:, 0, rows, :] = value
            return
        for own in range(2):
            @pl.when(core == own)
            def _(own=own):
                for d in range(n_dp):
                    outs[(d % 2) ^ own][d // 2, 0, rows, :] = value[d]

    left = n2t_ref[...]
    store(dot_nn(left, grow_ref[0]).astype(BF).reshape(n_dp, R, C), slice(0, R))
    store(dot_nn(left, urow_ref[0]).astype(BF).reshape(n_dp, R, C), slice(R, 2 * R))
    for j in range(W // C):
        cot = jnp.concatenate([ref[:, j * C:(j + 1) * C] for ref in cot_refs], axis=0)
        store(dot_nn(hid_ref[0], cot).astype(BF).reshape(n_dp, D, C), slice(2 * R + j * D, 2 * R + (j + 1) * D))


def expert_grads(first, count, apart, where, cots, n2t, hid, grow, urow, n_dp):
    blocks = len(cots)
    T = cots[0].shape[0]
    W, A = n2t.shape
    _, _, H = grow.shape
    P_ = 2 * (W // n_dp) + (W // H) * (H // n_dp)
    shape = (n_dp // 2 if apart else n_dp, count, P_, H)
    once = lambda s: pl.BlockSpec(s, lambda e, w: (0,) * len(s), pipeline_mode=pl.Buffered(1))
    per = lambda s: pl.BlockSpec((1,) + s, lambda e, w: (e + first,) + (0,) * len(s))
    outs = 2 if apart else 1
    made = pl.pallas_call(
        functools.partial(grad_kernel, blocks, apart),
        out_shape=(jax.ShapeDtypeStruct(shape, BF),) * outs,
        grid_spec=pltpu.PrefetchScalarGridSpec(
            num_scalar_prefetch=1, grid=(count,),
            in_specs=[once((T, W))] * blocks + [once((W, A)), per((H, A)), per((A, H)), per((A, H))],
            out_specs=(pl.BlockSpec((shape[0], 1, P_, H), lambda e, w: (0, e, 0, 0)),) * outs),
        compiler_params=pltpu.CompilerParams(vmem_limit_bytes=60 << 20),
        cost_estimate=pl.CostEstimate(flops=0, bytes_accessed=0, transcendentals=0),
    )(where, *cots, n2t, hid, grow, urow)
    return made if apart else made[0]


def combine_kernel(weighed_ref, down_ref, keep_ref, send_ref, total):
    e = pl.program_id(0)
    half, T, _ = keep_ref.shape
    made = dot_nn(weighed_ref[0], down_ref[0])

    @pl.when(e == 0)
    def _():
        total[...] = made

    @pl.when(e > 0)
    def _():
        total[...] += made

    @pl.when(e == pl.num_programs(0) - 1)
    def _():
        for b in range(2 * half):
            out = send_ref if b % 2 else keep_ref
            out[b // 2] = total[b * T:(b + 1) * T, :].astype(BF)


def combine(weighed, down_w, blocks):
    E, A, H = weighed.shape
    W = down_w.shape[2]
    T = A // blocks
    per = lambda s: pl.BlockSpec((1,) + s, lambda e: (e,) + (0,) * len(s))
    out = pl.BlockSpec((blocks // 2, T, W), lambda e: (0, 0, 0))
    return pl.pallas_call(
        combine_kernel,
        out_shape=(jax.ShapeDtypeStruct((blocks // 2, T, W), BF),) * 2,
        grid=(E,),
        in_specs=[per((A, H)), per((H, W))],
        out_specs=(out, out),
        scratch_shapes=[pltpu.VMEM((A, W), F32)],
        compiler_params=pltpu.CompilerParams(vmem_limit_bytes=60 << 20),
        cost_estimate=pl.CostEstimate(flops=0, bytes_accessed=0, transcendentals=0),
    )(weighed, down_w)


def raw_kernel(blocks, *refs):
    payloads, (down_ref, out_ref, cot) = refs[:blocks], refs[blocks:]
    T = payloads[0].shape[0]

    @pl.when(pl.program_id(0) == 0)
    def _():
        for b in range(blocks):
            cot[b * T:(b + 1) * T, :] = payloads[b][...]

    out_ref[0] = dot_nt(cot[...], down_ref[0])


def raw_back(payloads, down_w):
    blocks = len(payloads)
    T = payloads[0].shape[0]
    E, H, W = down_w.shape
    A = blocks * T
    return pl.pallas_call(
        functools.partial(raw_kernel, blocks),
        grid=(E,),
        out_shape=jax.ShapeDtypeStruct((E, A, H), F32),
        in_specs=[pl.BlockSpec((T, W), lambda e: (0, 0), pipeline_mode=pl.Buffered(1))] * blocks
        + [pl.BlockSpec((1, H, W), lambda e: (e, 0, 0))],
        out_specs=pl.BlockSpec((1, A, H), lambda e: (e, 0, 0)),
        scratch_shapes=[pltpu.VMEM((A, W), BF)],
        compiler_params=pltpu.CompilerParams(vmem_limit_bytes=60 << 20),
        cost_estimate=pl.CostEstimate(flops=0, bytes_accessed=0, transcendentals=0),
    )(*payloads, down_w)


def normed_kernel(where_ref, gains_ref, *refs):
    payloads, out_ref = refs[:-1], refs[-1]
    T = payloads[0].shape[0]
    W = gains_ref.shape[1]
    _, half, R, _ = out_ref.shape
    for b, ref in enumerate(payloads):
        x = ref[:, W + 128:].astype(F32)
        inverse = lax.rsqrt(jnp.mean(x * x, axis=1, keepdims=True) + EPSILON)
        turned = (x * inverse * gains_ref[0:1, :]).astype(BF).T
        for d in range(2 * half):
            r = d ^ where_ref[1]
            out_ref[lax.rem(r, 2), lax.div(r, 2), :, b * T:(b + 1) * T] = turned[d * R:(d + 1) * R, :]


def normed_turned(where, gains, payloads, n_dp):
    T = payloads[0].shape[0]
    W = gains.shape[1]
    v = pl.BlockSpec(memory_space=pltpu.VMEM)
    return pl.pallas_call(
        normed_kernel,
        out_shape=jax.ShapeDtypeStruct((2, n_dp // 2, W // n_dp, len(payloads) * T), BF),
        in_specs=[pl.BlockSpec(memory_space=pltpu.SMEM)] + [v] * (1 + len(payloads)),
        out_specs=v,
        compiler_params=pltpu.CompilerParams(vmem_limit_bytes=40 << 20),
        cost_estimate=pl.CostEstimate(flops=0, bytes_accessed=0, transcendentals=0),
    )(where, gains, *payloads)


def rope_tile(x, cosine, sine):
    lane = lax.broadcasted_iota(jnp.int32, x.shape, 1)
    other = jnp.where(lax.rem(lane, 64) < 32, pltpu.roll(x, 96, 1), pltpu.roll(x, 32, 1))
    return x * cosine + other * sine


def half_mask(shape, half):
    lane = lax.broadcasted_iota(jnp.int32, shape, 1)
    return (lane < 64) if half == 0 else (lane >= 64)


def stacked(tiles, group, per, T):
    out = []
    for i in range(per):
        h = group * per + i
        x = tiles[h // 2]
        if h % 2 != group % 2:
            x = pltpu.roll(x, 64, 1)
        out.append(jnp.where(half_mask(x.shape, group % 2), x, 0.0).astype(BF))
    return jnp.concatenate(out, axis=0)


def unstacked(value, group, per, T, tiles):
    for i in range(per):
        h = group * per + i
        x = value[i * T:(i + 1) * T]
        if h % 2 != group % 2:
            x = pltpu.roll(x, 64, 1)
        x = jnp.where(half_mask(x.shape, h % 2), x, 0.0)
        tiles[h // 2] = x if tiles[h // 2] is None else tiles[h // 2] + x


def allowed(seg_row_ref, seg_col_ref, T, per):
    row = lax.broadcasted_iota(jnp.int32, (T, T), 0)
    col = lax.broadcasted_iota(jnp.int32, (T, T), 1)
    ok = (seg_col_ref[...] == seg_row_ref[...]) & (col <= row)
    bias = jnp.where(ok, 0.0, -1e30)
    return jnp.concatenate([bias] * per, axis=0)


def fetch(places, pieces, dev, dst, sems, at, lo, hi):
    R = pieces[0].shape[0]
    copies = []
    for i, ((r, col), piece) in enumerate(zip(places, pieces)):
        a, b = max(lo, col), min(hi, col + piece.shape[1])
        if a < b:
            row = pl.multiple_of((dev ^ r) * R, R)
            copies.append(pltpu.make_async_copy(
                piece.at[:, a - col:b - col], dst.at[pl.ds(row, R), a - lo:b - lo], sems.at[at + i]))
            copies[-1].start()
    return copies


def forward_kernel(places, kv, experts, dev_ref, tok_ref, cos_ref, sin_ref, segr_ref, segc_ref, q_hbm, *refs):
    pieces, refs = refs[:len(places)], refs[len(places):]
    qkv_ref, mix_ref, resid_ref, n2_ref, gains_ref, router_ref, kv_ref, wq, wkv, wsm, wo, sems = refs
    T, W = tok_ref.shape
    C = 512
    chunks = W // C
    some = len(places)
    fetched = fetch(places, pieces, dev_ref[1], wkv, sems, chunks, 0, 2 * kv)
    fetched += fetch(places, pieces, dev_ref[1], wsm, sems, chunks + some, 2 * kv + W, 2 * kv + W + 128)
    copies = []
    for j in range(chunks):
        copies.append(pltpu.make_async_copy(q_hbm.at[:, j * C:(j + 1) * C], wq.at[j], sems.at[j]))
        copies[-1].start()
    late = fetch(places, pieces, dev_ref[1], wo, sems, chunks + 2 * some, 2 * kv, 2 * kv + W)
    x = tok_ref[...].astype(F32)
    inverse = lax.rsqrt(jnp.mean(x * x, axis=1, keepdims=True) + EPSILON)
    for copy in fetched:
        copy.wait()
    keep = pltpu.make_async_copy(wkv, kv_ref, sems.at[chunks + 3 * some])
    keep.start()
    small = wsm[...]
    router_ref[...] = small
    turned = small.astype(F32).T
    gain1, gain2 = turned[experts:experts + 1, :], turned[experts + 1:experts + 2, :]
    gains_ref[0:1, :] = gain1
    gains_ref[1:2, :] = gain2
    gains_ref[2:8, :] = jnp.zeros((6, W), F32)
    n1 = (x * inverse * gain1).astype(BF)
    cosine, sine = cos_ref[...], sin_ref[...]
    q_tiles = W // 128
    k_tiles = kv // 128
    side = dot_nn(n1, wkv[...])
    others = [side[:, t * 128:(t + 1) * 128] for t in range(2 * k_tiles)]
    others = [rope_tile(t, cosine, sine).astype(BF) for t in others[:k_tiles]] + [t.astype(BF) for t in others[k_tiles:]]
    tiles = []
    for j in range(chunks):
        copies[j].wait()
        made = dot_nn(n1, wq[j])
        tiles += [rope_tile(made[:, t * 128:(t + 1) * 128], cosine, sine).astype(BF) for t in range(C // 128)]
    tiles += others
    for t, tile in enumerate(tiles):
        qkv_ref[:, t * 128:(t + 1) * 128] = tile
    per = q_tiles // k_tiles
    bias = allowed(segr_ref, segc_ref, T, per)
    q = [t.astype(F32) for t in tiles[:q_tiles]]
    mixed = [None] * q_tiles
    for g in range(2 * k_tiles):
        k_tile, v_tile = tiles[q_tiles + g // 2], tiles[q_tiles + k_tiles + g // 2]
        s = dot_nt(stacked(q, g, per, T), k_tile) * SCORE_FACTOR + bias
        raised = jnp.exp(s - jnp.max(s, axis=1, keepdims=True))
        p = raised / jnp.sum(raised, axis=1, keepdims=True)
        unstacked(dot_nn(p.astype(BF), v_tile), g, per, T, mixed)
    for t in range(q_tiles):
        mix_ref[:, t * 128:(t + 1) * 128] = mixed[t].astype(BF)
    for copy in late:
        copy.wait()
    total = jnp.zeros((T, 1), F32)
    for j in range(chunks):
        cols = slice(j * C, (j + 1) * C)
        r = tok_ref[:, cols].astype(F32) + dot_nn(mix_ref[...], wo[:, cols])
        resid_ref[:, cols] = r
        total = total + jnp.sum(r * r, axis=1, keepdims=True)
    inverse = lax.rsqrt(total / W + EPSILON)
    n2_ref[...] = (resid_ref[...] * inverse * gain2).astype(BF)
    keep.wait()


def forward(where, tokens, cosine, sine, segr, segc, q_w, pieces, places, kv, experts):
    T, W = tokens.shape
    N = W + 2 * kv
    S = jax.ShapeDtypeStruct
    v = pl.BlockSpec(memory_space=pltpu.VMEM)
    hbm = pl.BlockSpec(memory_space=pl.ANY)
    return pl.pallas_call(
        functools.partial(forward_kernel, places, kv, experts),
        out_shape=(S((T, N), BF), S((T, W), BF), S((T, W), F32), S((T, W), BF), S((8, W), F32), S((W, 128), BF), S((W, 2 * kv), BF)),
        in_specs=[pl.BlockSpec(memory_space=pltpu.SMEM)] + [v] * 5 + [hbm] * (1 + len(places)),
        out_specs=(v,) * 6 + (hbm,),
        scratch_shapes=[pltpu.VMEM((W // 512, W, 512), BF), pltpu.VMEM((W, 2 * kv), BF), pltpu.VMEM((W, 128), BF), pltpu.VMEM((W, W), BF),
                        pltpu.SemaphoreType.DMA((W // 512 + 3 * len(places) + 1,))],
        compiler_params=pltpu.CompilerParams(vmem_limit_bytes=60 << 20),
        cost_estimate=pl.CostEstimate(flops=0, bytes_accessed=0, transcendentals=0),
    )(where, tokens, cosine, sine, segr, segc, q_w, *pieces)


def split(x):
    hi = x.astype(BF)
    return hi, (x - hi.astype(F32)).astype(BF)


def dot_tn(a, b): return lax.dot_general(a, b, (((0,), (0,)), ((), ())), preferred_element_type=F32)


def ones_at(T, lane):
    return jnp.where(lax.broadcasted_iota(jnp.int32, (T, 128), 1) == lane, 1.0, 0.0).astype(BF)


def middle_kernel(experts, *refs):
    (rows_ref, gates_ref, router_ref, n2_ref, resid_ref, g2_ref, cot_ref, att_ref, cut_ref, back_ref, extra_ref) = refs
    T, W = n2_ref.shape
    total = rows_ref[0].astype(F32)
    for b in range(1, rows_ref.shape[0]):
        total = total + rows_ref[b].astype(F32)
    aux = total[:, W:]
    gate_back = aux + pltpu.roll(aux, 64, 1)
    gates = gates_ref[...]
    hi, lo = split(gates * (gate_back - jnp.sum(gates * gate_back, axis=1, keepdims=True)))
    n2_back = total[:, :W] + dot_nt(hi, router_ref[...]) + dot_nt(lo, router_ref[...])
    resid = resid_ref[...]
    inverse = lax.rsqrt(jnp.mean(resid * resid, axis=1, keepdims=True) + EPSILON)
    scaled = n2_back * g2_ref[1:2, :]
    inner = jnp.mean(scaled * resid, axis=1, keepdims=True)
    back = cot_ref[...].astype(F32) + inverse * scaled - resid * (inverse * inverse * inverse * inner)
    back_ref[...] = back
    att_ref[...] = back.astype(BF)
    width = cut_ref.shape[2]
    for b in range(cut_ref.shape[0]):
        cut_ref[b] = back[:, b * width:(b + 1) * width].astype(BF)
    p_hi, p_lo = split(n2_back * resid * inverse)
    one = ones_at(T, experts)
    extra_ref[...] = dot_tn(n2_ref[...], hi) + dot_tn(n2_ref[...], lo) + dot_tn(p_hi, one) + dot_tn(p_lo, one)


def middle(rows_in, gates, router, n2, resid, gain2, cot, experts):
    T, W = n2.shape
    blocks = rows_in.shape[0]
    S = jax.ShapeDtypeStruct
    v = lambda s: pl.BlockSpec(s, lambda i: (0, 0))
    return pl.pallas_call(
        functools.partial(middle_kernel, experts),
        grid=(1,),
        out_shape=(S((T, W), BF), S((blocks, T, W // blocks), BF), S((T, W), F32), S((W, 128), F32)),
        in_specs=[pl.BlockSpec((blocks, T, W + 128), lambda i: (0, 0, 0)), v((T, 128)), v((W, 128)), v((T, W)), v((T, W)), v((8, W)), v((T, W))],
        out_specs=(v((T, W)), pl.BlockSpec((blocks, T, W // blocks), lambda i: (0, 0, 0)), v((T, W)), v((W, 128))),
        compiler_params=pltpu.CompilerParams(vmem_limit_bytes=40 << 20),
        cost_estimate=pl.CostEstimate(flops=400_000_000_000, bytes_accessed=30 * T * W, transcendentals=T),
    )(rows_in, gates, router, n2, resid, gain2, cot)


def backward_kernel(places, dev_ref, att_ref, qkv_ref, cos_ref, sin_ref, segr_ref, segc_ref, *refs):
    outs, refs = refs[:len(places)], refs[len(places):]
    back_ref, cut_ref, wo, sems = refs
    T, W = att_ref.shape
    fetched = fetch(places, outs, dev_ref[1], wo, sems, 0, qkv_ref.shape[1] - W, qkv_ref.shape[1])
    q_tiles = W // 128
    k_tiles = (qkv_ref.shape[1] - W) // 256
    per = q_tiles // k_tiles
    tile = lambda t: qkv_ref[:, t * 128:(t + 1) * 128]
    q = [tile(t).astype(F32) for t in range(q_tiles)]
    bias = allowed(segr_ref, segc_ref, T, per)
    cosine, sine = cos_ref[...], -sin_ref[...]
    for copy in fetched:
        copy.wait()
    mixed_back = []
    for j in range(W // 512):
        made = dot_nt(att_ref[...], wo[j * 512:(j + 1) * 512, :]).astype(BF).astype(F32)
        mixed_back += [made[:, t * 128:(t + 1) * 128] for t in range(4)]
    q_back = [None] * q_tiles
    k_back = [None] * k_tiles
    v_back = [None] * k_tiles
    for g in range(2 * k_tiles):
        k_tile, v_tile = tile(q_tiles + g // 2), tile(q_tiles + k_tiles + g // 2)
        qs = stacked(q, g, per, T)
        ms = stacked(mixed_back, g, per, T)
        s = dot_nt(qs, k_tile) * SCORE_FACTOR + bias
        raised = jnp.exp(s - jnp.max(s, axis=1, keepdims=True))
        p = raised / jnp.sum(raised, axis=1, keepdims=True)
        dp = dot_nt(ms, v_tile)
        ds = (p * (dp - jnp.sum(p * dp, axis=1, keepdims=True)) * SCORE_FACTOR).astype(BF)
        unstacked(dot_nn(ds, k_tile), g, per, T, q_back)
        kb, vb = dot_tn(ds, qs), dot_tn(p.astype(BF), ms)
        k_back[g // 2] = kb if g % 2 == 0 else k_back[g // 2] + kb
        v_back[g // 2] = vb if g % 2 == 0 else v_back[g // 2] + vb
    made = [rope_tile(t, cosine, sine) for t in q_back + k_back] + v_back
    for t, value in enumerate(made):
        back_ref[:, t * 128:(t + 1) * 128] = value.astype(BF)
        of, place = (q_tiles, t) if t < q_tiles else (k_tiles, (t - q_tiles) % k_tiles)
        each = of // cut_ref.shape[0]
        at = place % each * 128 + (0 if t < q_tiles else (q_tiles + (k_tiles if t >= q_tiles + k_tiles else 0)) // cut_ref.shape[0] * 128)
        cut_ref[place // each, :, at:at + 128] = value.astype(BF)


def backward(where, att, qkv, cosine, sine, segr, segc, outs, places, ne):
    T, W = att.shape
    N = qkv.shape[1]
    S = jax.ShapeDtypeStruct
    v = pl.BlockSpec(memory_space=pltpu.VMEM)
    hbm = pl.BlockSpec(memory_space=pl.ANY)
    return pl.pallas_call(
        functools.partial(backward_kernel, places),
        out_shape=(S((T, N), BF), S((ne, T, N // ne), BF)),
        in_specs=[pl.BlockSpec(memory_space=pltpu.SMEM)] + [v] * 6 + [hbm] * len(places),
        out_specs=(v, v),
        scratch_shapes=[pltpu.VMEM((W, W), BF), pltpu.SemaphoreType.DMA((len(places),))],
        compiler_params=pltpu.CompilerParams(vmem_limit_bytes=60 << 20),
        cost_estimate=pl.CostEstimate(flops=0, bytes_accessed=0, transcendentals=0),
    )(where, att, qkv, cosine, sine, segr, segc, *outs)


def last_kernel(experts, back_ref, tok_ref, g1_ref, resid_back_ref, extra_ref, q_ref, kv_ref, grad_ref, more_ref, nb):
    j = pl.program_id(0)
    T, W = tok_ref.shape
    C = q_ref.shape[0]
    nb[j] = dot_nt(back_ref[:, :W], q_ref[...]) + dot_nt(back_ref[:, W:], kv_ref[...])

    @pl.when(j == pl.num_programs(0) - 1)
    def _():
        x = tok_ref[...].astype(F32)
        inverse = lax.rsqrt(jnp.mean(x * x, axis=1, keepdims=True) + EPSILON)
        n1_back = jnp.concatenate([nb[i] for i in range(W // C)], axis=1)
        scaled = n1_back * g1_ref[0:1, :]
        inner = jnp.mean(scaled * x, axis=1, keepdims=True)
        grad_ref[...] = resid_back_ref[...] + inverse * scaled - x * (inverse * inverse * inverse * inner)
        p_hi, p_lo = split(n1_back * x * inverse)
        one = ones_at(T, experts + 1)
        more_ref[...] = extra_ref[...] + dot_tn(p_hi, one) + dot_tn(p_lo, one)


def last(back, tokens, gains, resid_back, extra, q_w, kv_w, experts):
    T, W = tokens.shape
    N = back.shape[1]
    C = 512
    S = jax.ShapeDtypeStruct
    v = lambda s: pl.BlockSpec(s, lambda j: (0, 0))
    return pl.pallas_call(
        functools.partial(last_kernel, experts),
        grid=(W // C,),
        out_shape=(S((T, W), F32), S((W, 128), F32)),
        in_specs=[v((T, N)), v((T, W)), v((8, W)), v((T, W)), v((W, 128)), pl.BlockSpec((C, W), lambda j: (j, 0)),
                  pl.BlockSpec((C, N - W), lambda j: (j, 0))],
        out_specs=(v((T, W)), v((W, 128))),
        scratch_shapes=[pltpu.VMEM((W // C, T, C), F32)],
        compiler_params=pltpu.CompilerParams(vmem_limit_bytes=40 << 20),
        cost_estimate=pl.CostEstimate(flops=0, bytes_accessed=0, transcendentals=0),
    )(back, tokens, gains, resid_back, extra, q_w, kv_w)


def out_grad_kernel(blocks, where_ref, *refs):
    mix_refs, (att_ref, keep_ref, send_ref, left) = refs[:blocks], refs[blocks:]
    own, dev = where_ref[0], where_ref[1]
    T = mix_refs[0].shape[0]
    half, _, R, C = keep_ref.shape
    for b in range(blocks):
        turned = mix_refs[b][...].T
        for d in range(2 * half):
            r = d ^ dev
            left[lax.rem(r, 2), lax.div(r, 2), :, b * T:(b + 1) * T] = turned[d * R:(d + 1) * R, :]
    right = jnp.concatenate([att_ref[own ^ b] for b in range(blocks)], axis=0)
    for s, out in ((1, send_ref), (0, keep_ref)):
        out[:, 0] = dot_nn(left[s].reshape(half * R, blocks * T), right).astype(BF).reshape(half, R, C)


def out_grads(where, mixs, att_cut, n_dp):
    blocks = len(mixs)
    T, W = mixs[0].shape
    C = att_cut.shape[2]
    R = W // n_dp
    S = jax.ShapeDtypeStruct
    v = pl.BlockSpec(memory_space=pltpu.VMEM)
    return pl.pallas_call(
        functools.partial(out_grad_kernel, blocks),
        out_shape=(S((n_dp // 2, 1, R, C), BF),) * 2,
        in_specs=[pl.BlockSpec(memory_space=pltpu.SMEM)] + [v] * (blocks + 1),
        out_specs=(v, v),
        scratch_shapes=[pltpu.VMEM((2, n_dp // 2, R, blocks * T), BF)],
        compiler_params=pltpu.CompilerParams(vmem_limit_bytes=60 << 20),
        cost_estimate=pl.CostEstimate(flops=0, bytes_accessed=0, transcendentals=0),
    )(where, *mixs, att_cut)


def qkv_grad_kernel(where_ref, left_ref, qkv_ref, extra_ref, keep_ref, send_ref):
    own, dev = where_ref[0], where_ref[1]
    blocks, _, width = qkv_ref.shape
    half, _, R, C = keep_ref.shape
    right = jnp.concatenate([qkv_ref[own ^ b] for b in range(blocks)], axis=0)
    for s, out in ((1, send_ref), (0, keep_ref)):
        left = left_ref[s].reshape(half * R, left_ref.shape[3])
        out[:, 0, :, :width] = dot_nn(left, right).astype(BF).reshape(half, R, width)
    for d in range(2 * half):
        more = extra_ref[d * R:(d + 1) * R, :].astype(BF)
        r = d ^ dev

        @pl.when(lax.rem(r, 2) == 0)
        def _(more=more, r=r):
            keep_ref[lax.div(r, 2), 0, :, width:] = more

        @pl.when(lax.rem(r, 2) == 1)
        def _(more=more, r=r):
            send_ref[lax.div(r, 2), 0, :, width:] = more


def qkv_grads(where, left, qkv_cut, extra, n_dp):
    W = extra.shape[0]
    C = qkv_cut.shape[2] + 128
    R = W // n_dp
    S = jax.ShapeDtypeStruct
    v = pl.BlockSpec(memory_space=pltpu.VMEM)
    return pl.pallas_call(
        qkv_grad_kernel,
        out_shape=(S((n_dp // 2, 1, R, C), BF),) * 2,
        in_specs=[pl.BlockSpec(memory_space=pltpu.SMEM)] + [v] * 3,
        out_specs=(v, v),
        compiler_params=pltpu.CompilerParams(vmem_limit_bytes=60 << 20),
        cost_estimate=pl.CostEstimate(flops=2 * W * C * left.shape[3], bytes_accessed=4 * W * C, transcendentals=0),
    )(where, left, qkv_cut, extra)


def flip(x, axis, mask, size):
    return lax.ppermute(x, axis, [(i, i ^ mask) for i in range(size)])


def add(a, b):
    return (a.astype(F32) + b.astype(F32)).astype(BF)


def split_kernel(width, where_ref, *refs):
    ins, (a_keep, a_send, b_keep, b_send) = refs[:-4], refs[-4:]
    count = ins[0].shape[-4]
    for q in range(count):
        at = q ^ where_ref[0]
        sums = [(ins[i][at, 0].astype(F32) + ins[i + 1][at, 0].astype(F32)).astype(BF) for i in range(0, len(ins), 2)]
        total = sums[0] if len(sums) == 1 else jnp.concatenate(sums, axis=1)
        out = a_send if q % 2 else a_keep
        out[q // 2, 0] = total[:, :width]
        out = b_send if q >= count // 2 else b_keep
        out[q % (count // 2), 0] = total[:, width:]


def halves(pairs, n_dp, order=None):
    bits = n_dp.bit_length() - 1
    count, group, rows, _ = pairs[0][1].shape
    cols = sum(theirs.shape[3] for _, theirs in pairs)
    a = cols // 256 * 128
    S = jax.ShapeDtypeStruct
    if order is None:
        order = jnp.zeros((1,), jnp.int32)
    specs = []
    for keep, theirs in pairs:
        shape = (count, 1, rows, theirs.shape[3])
        specs += [pl.BlockSpec(shape, lambda g, w: (0, g, 0, 0))] * 2
    widths = (a, a, cols - a, cols - a)
    outs = pl.pallas_call(
        functools.partial(split_kernel, a),
        out_shape=tuple(S((count // 2, group, rows, c), BF) for c in widths),
        grid_spec=pltpu.PrefetchScalarGridSpec(
            num_scalar_prefetch=1, grid=(group,), in_specs=specs,
            out_specs=tuple(pl.BlockSpec((count // 2, 1, rows, c), lambda g, w: (0, g, 0, 0)) for c in widths)),
        compiler_params=pltpu.CompilerParams(vmem_limit_bytes=40 << 20),
        cost_estimate=pl.CostEstimate(flops=0, bytes_accessed=0, transcendentals=0),
    )(order.astype(jnp.int32), *[x for pair in pairs for x in pair])
    left = tuple(range(bits - 1, 0, -1))
    shaped = lambda x: x.reshape((2,) * (bits - 2) + x.shape[1:])
    return [(shaped(outs[0]), shaped(outs[1]), left[:-1], tuple(range(1, bits))),
            (shaped(outs[2]), shaped(outs[3]), left[1:], left)]


def halve(parts, n_dp):
    done = []
    for mine, sent, left, order in parts:
        theirs = flip(sent, "dp", 1 << order[0], n_dp)
        if left:
            total = add(mine, theirs)
            axis = left.index(order[1])
            mine, theirs = (lax.index_in_dim(total, i, axis, keepdims=False) for i in (0, 1))
        done.append((mine, theirs, tuple(b for b in left if b != order[1]) if left else (), order[1:]))
    return done


def finish(parts, n_dp):
    while parts[0][3]:
        parts = halve(parts, n_dp)
    return parts


def tie_parts(parts, *others):
    arrays, others = lax.optimization_barrier(([p[:2] for p in parts], others))
    return [tuple(a) + p[2:] for a, p in zip(arrays, parts)], *others


def unpack_kernel(parts, *refs):
    gate_ref, up_ref, down_ref = refs[-3:]
    R, D = gate_ref.shape[1], down_ref.shape[1]
    H = gate_ref.shape[2]
    at = 0
    for i in range(0, len(parts), 2):
        total = refs[parts[i]][0].astype(F32)
        if parts[i + 1] is not None:
            total = total + refs[parts[i + 1]][0].astype(F32)
        width = total.shape[1]
        gate_ref[0, :, at:at + width] = total[:R]
        up_ref[0, :, at:at + width] = total[R:2 * R]
        for j in range(down_ref.shape[2] // H):
            down_ref[0, :, j * H + at:j * H + at + width] = total[2 * R + j * D:2 * R + (j + 1) * D]
        at += width


def unpack(first, ins, parts, before, E, R, D, W):
    count, rows, _ = ins[0].shape
    H = before[0].shape[2] if before else ins[0].shape[2]
    S = jax.ShapeDtypeStruct
    out = lambda a, b: pl.BlockSpec((1, a, b), lambda e: (e + first, 0, 0))
    return pl.pallas_call(
        functools.partial(unpack_kernel, parts),
        grid=(count,),
        out_shape=(S((E, R, H), F32), S((E, R, H), F32), S((E, D, W), F32)),
        in_specs=[pl.BlockSpec((1, rows, x.shape[2]), lambda e: (e, 0, 0)) for x in ins]
        + [pl.BlockSpec(memory_space=pl.ANY)] * len(before),
        out_specs=(out(R, H), out(R, H), out(D, W)),
        input_output_aliases={len(ins) + i: i for i in range(len(before))},
        compiler_params=pltpu.CompilerParams(vmem_limit_bytes=40 << 20),
        cost_estimate=pl.CostEstimate(flops=3 * count * R * H, bytes_accessed=18 * count * R * H, transcendentals=0),
    )(*ins, *before)


def spread_kernel(kv, where_ref, *refs):
    parts, (q_ref, k_ref, v_ref, o_ref, extra_ref) = refs[:-5], refs[-5:]
    blocks = len(parts)
    wide, narrow = q_ref.shape[1] // blocks, kv // blocks
    extra = None
    for b, ref in enumerate(parts):
        at = where_ref[0] ^ b
        col = 0
        for out, width in ((o_ref, wide), (q_ref, wide), (k_ref, narrow), (v_ref, narrow)):
            out[:, pl.ds(pl.multiple_of(at * width, width), width)] = ref[:, col:col + width].astype(F32)
            col += width
        more = ref[:, col:].astype(F32)
        extra = more if extra is None else extra + more
    extra_ref[...] = extra


def spread(where, parts, W, kv):
    R, C = parts[0].shape
    S = jax.ShapeDtypeStruct
    v = pl.BlockSpec(memory_space=pltpu.VMEM)
    return pl.pallas_call(
        functools.partial(spread_kernel, kv),
        out_shape=(S((R, W), F32), S((R, kv), F32), S((R, kv), F32), S((R, W), F32), S((R, 128), F32)),
        in_specs=[pl.BlockSpec(memory_space=pltpu.SMEM)] + [v] * len(parts),
        out_specs=(v,) * 5,
        compiler_params=pltpu.CompilerParams(vmem_limit_bytes=40 << 20),
        cost_estimate=pl.CostEstimate(flops=R * C, bytes_accessed=24 * R * C, transcendentals=0),
    )(where, *parts)


def begin_z(x, ne):
    found = {0: x}
    bit = 1
    while bit < ne:
        found[bit] = flip(x, "expert", bit, ne)
        bit *= 2
    return found


def end_z(found, ne):
    for k in range(ne):
        if k not in found:
            found[k] = flip(found[k & (k - 1)], "expert", k & -k, ne)
    return [found[k] for k in range(ne)]


def gather_z(x, ne):
    return end_z(begin_z(x, ne), ne)


def gather_dp(w, n_dp, ready):
    half = w.shape[1] // 256 * 128
    found = {(0, 0): w[:, :half], (0, half): w[:, half:]}
    whole = {0: w}
    bits = range(1, n_dp.bit_length() - 1)
    for bit in bits:
        whole[1 << bit] = flip(w, "dp", 1 << bit, n_dp)
    whole, ready = lax.optimization_barrier((whole, ready))
    for bit in bits:
        r = 1 << bit
        found[r, 0], found[r, half] = whole[r][:, :half], whole[r][:, half:]
    for r in range(2, n_dp, 2):
        low, high = r & -r, 1 << (r.bit_length() - 1)
        if low != high:
            found[r, 0] = flip(found[r ^ high, 0], "dp", high, n_dp)
            found[r, half] = flip(found[r ^ low, half], "dp", low, n_dp)
    pieces = {}
    for (r, col), x in found.items():
        if r in whole:
            pieces[r, 0] = whole[r]
        else:
            pieces[r, col] = x
    for (r, col), x in list(pieces.items()):
        pieces[r ^ 1, col] = flip(x, "dp", 1, n_dp)
    places = sorted(pieces)
    return tuple(places), [pieces[p] for p in places], ready


def local(n_dp, ne, tokens, segment_ids, routes, cotangent, query_weight, key_weight, value_matrix, out_weight,
          first_gain, second_gain, router_weight, gate_weight, up_weight, down_weight):
    d = lax.axis_index("dp")
    z = lax.axis_index("expert")
    tie = lax.optimization_barrier
    T, W = tokens.shape
    experts = router_weight.shape[1]
    E, _, H = gate_weight.shape
    R = W // n_dp
    D = H // n_dp
    KV = key_weight.shape[1]
    where = jnp.stack([z, d, jnp.int32(E), jnp.int32(0)]).astype(jnp.int32)

    q_full = lax.all_gather(query_weight, "dp", axis=0, tiled=True)
    side = jnp.concatenate([key_weight, value_matrix, out_weight, router_weight, first_gain[:, None], second_gain[:, None],
                            jnp.zeros((R, 126 - experts), BF)], axis=1)
    segments = segment_ids[0]
    segr, segc = segments[None, :], segments[:, None]
    positions = jnp.arange(T, dtype=jnp.int32) - jnp.sum((segr < segc).astype(jnp.int32), axis=1)
    half = HEAD_SIZE // 2
    freq = ROTARY_BASE ** (-jnp.arange(half, dtype=F32) * 2.0 / HEAD_SIZE)
    angle = positions.astype(F32)[:, None] * freq[None, :]
    cosine = jnp.tile(jnp.cos(angle), (1, 4))
    sine = jnp.sin(angle)
    sine = jnp.concatenate([-sine, sine, -sine, sine], axis=1)
    choices = routes.shape[1]
    payload = jnp.concatenate([cotangent, jnp.pad(routes.astype(BF), ((0, 0), (0, 128 - choices))), tokens], axis=1)
    places, pieces, (cosine, sine, segc, where) = gather_dp(side, n_dp, (cosine, sine, segc, where))
    payloads = gather_z(payload, ne)
    core = lambda x: flip(x, "dp", 1, n_dp)
    exchange = lambda x: lax.all_to_all(x, "expert", split_axis=0, concat_axis=0, tiled=True)
    payloads, pieces, q_full = tie((payloads, pieces, q_full))
    qkv, mixed, resid, normed2, gains, router, kv_full = forward(
        where, tokens, cosine, sine, segr, segc, q_full, pieces, places, KV, experts)
    raw = raw_back(payloads, down_weight)
    n1t = normed_turned(where, gains, payloads, n_dp)
    n2s, raw, n1t = tie((begin_z(normed2, ne), raw, n1t))
    n2s, mixed = tie((end_z(n2s, ne), mixed))
    mixs = begin_z(mixed, ne)
    made = expert_rows(where, n2s, payloads, choices, router, gate_weight, up_weight, raw)
    made, mixs = tie((made, mixs))
    rows, gates, n2t, hid, weighed, grow, urow = made
    rows = exchange(rows)
    partial = expert_grads(0, MANY, False, where, payloads, n2t, hid, grow, urow, n_dp)
    packed = lax.psum_scatter(partial, "dp", scatter_dimension=0, tiled=True)
    partial, n2t, weighed = tie((partial, n2t, weighed))
    few, away = expert_grads(MANY, E - MANY, True, where, payloads, n2t, hid, grow, urow, n_dp)
    comb, comb_away = combine(weighed, down_weight, ne)
    rows, few, away, comb, comb_away, mixs = tie((rows, few, away, comb, comb_away, mixs))
    mixs = end_z(mixs, ne)
    comb_in = flip(comb_away, "expert", 1, ne)
    theirs = core(away)
    attended, att_cut, resid_back, extra = middle(rows, gates, router, normed2, resid, gains, cotangent, experts)
    att_cut = exchange(att_cut)
    back, back_cut = backward(where, attended, qkv, cosine, sine, segr, segc, pieces, places, ne)
    att_cut, back, back_cut, few, theirs, comb_in = tie((att_cut, back, back_cut, few, theirs, comb_in))
    back_cut = exchange(back_cut)
    few = halves([(few, theirs)], n_dp, (d // 2).reshape(1))
    input_grad, extra = last(back, tokens, gains, resid_back, extra, q_full, kv_full, experts)
    keep4, send4 = out_grads(where, mixs, att_cut, n_dp)
    comb = comb.astype(F32) + comb_in.astype(F32)
    comb, comb_far = comb[0], comb[1:].astype(BF)
    few, back_cut, extra, keep4, send4, comb_far = tie_parts(few, back_cut, extra, keep4, send4, comb_far)
    comb_far = [flip(comb_far[i], "expert", 2 * (i + 1), ne) for i in range(ne // 2 - 1)]
    theirs4 = core(send4)
    keep5, send5 = qkv_grads(where, n1t, back_cut, extra, n_dp)
    keep5, send5, theirs4 = tie((keep5, send5, theirs4))
    five = halve(halves([(keep4, theirs4), (keep5, core(send5))], n_dp), n_dp)
    five, comb_far = tie_parts(five, comb_far)
    five = finish(five, n_dp)
    part = jnp.concatenate([mine.astype(F32) + theirs.astype(F32) for mine, theirs, *_ in five], axis=-1)[0].astype(BF)
    few, part = tie_parts(few, part)
    parts = gather_z(part, ne)
    few = finish(few, n_dp)
    made = unpack(0, [packed[0]], (0, None), (), E, R, D, W)
    parts, made = tie((parts, made))
    query_grad, key_grad, value_grad, out_grad, extra = spread(where, parts, W, KV)
    gate_grad, up_grad, down_grad = unpack(MANY, [x for p in few for x in p[:2]], (0, 1, 2, 3), made, E, R, D, W)
    layer_out = (resid + comb + sum(x.astype(F32) for x in comb_far)).astype(BF)
    return (layer_out, input_grad, query_grad, key_grad, value_grad, out_grad, extra[:, experts + 1], extra[:, experts],
            extra[:, :experts], gate_grad, up_grad, down_grad)


def solution(mesh):
    both = P(("dp", "expert"), None)
    dp = P("dp", None)
    own = P("expert", None, None)
    part = P("expert", "dp", None)
    return jax.shard_map(
        functools.partial(local, mesh.shape["dp"], mesh.shape["expert"]),
        mesh=mesh,
        in_specs=(both, both, both, both, dp, dp, dp, dp, P("dp"), P("dp"), dp, own, own, own),
        out_specs=(both, both, dp, dp, dp, dp, P("dp"), P("dp"), dp, part, part, part),
        check_vma=False,
    )
```
